32 devices in a mesh: dp: 16 (over z, y, x), rep: 2 (over core).
Axes of the slice: x: 2, y: 2, z: 4, core: 2. Of those that a mesh axis runs over, the one named last changes fastest.
Arguments:
- tokens: bfloat16 [32, 384, 1024], P(('dp', 'rep')), may hold values from -6 to 6
- doc_lengths: int32 [32, 4], P(('dp', 'rep')), may hold values from 1 to 192, 384 in all within a row
- cotangent: bfloat16 [32, 384, 1024], P(('dp', 'rep')), may hold values from -6 to 6
- norm_gain: bfloat16 [1024], P('dp'), may hold values from 0.25 to 1.75
- input_weight: bfloat16 [1024, 4096], P('dp'), may hold values from -0.1875 to 0.1875
- filter_weight: bfloat16 [2048, 4], P('dp'), may hold values from -3 to 3
- filter_bias: bfloat16 [2048], P('dp'), may hold values from -0.5 to 0.5
- select_weight: bfloat16 [2048, 96], P('dp'), may hold values from -0.125 to 0.125
- delta_weight: bfloat16 [2048, 64], P('dp'), may hold values from -0.75 to 0.75
- delta_bias: bfloat16 [2048], P('dp'), may hold values from -4.59375 to -1.5
- decay_log: bfloat16 [2048, 16], P('dp'), may hold values from 0 to 2.765625
- skip_gain: bfloat16 [2048], P('dp'), may hold values from 0 to 2
- output_weight: bfloat16 [1024, 2048], P('dp'), may hold values from -0.25 to 0.25
Outputs:
- mixed_out: bfloat16 [32, 384, 1024], P(('dp', 'rep'))
- tokens_grad: float32 [32, 384, 1024], P(('dp', 'rep'))
- norm_gain_grad: float32 [1024], P('dp')
- input_weight_grad: float32 [1024, 4096], P('dp')
- filter_weight_grad: float32 [2048, 4], P('dp')
- filter_bias_grad: float32 [2048], P('dp')
- select_weight_grad: float32 [2048, 96], P('dp')
- delta_weight_grad: float32 [2048, 64], P('dp')
- delta_bias_grad: float32 [2048], P('dp')
- decay_log_grad: float32 [2048, 16], P('dp')
- skip_gain_grad: float32 [2048], P('dp')
- output_weight_grad: float32 [1024, 2048], P('dp')
The draws below stay inside these ranges and needn't reach their ends.
Inputs may be any that keep to these rules, and one draw needn't show every extreme that they name: `doc_lengths`: in each row the 4 lengths sum to 384, and the longest is exactly 192.
All inputs are finite; a program needn't handle non-finite values.
Results may differ from the reference program's by a relative error of at most 0.012.
Values may be sent and summed in bfloat16 or wider, within the bound.
A program may use at most 320 MiB of HBM per device.

```python
import math
import jax
import jax.numpy as jnp
import numpy as np
from jax import lax

D = 1024
INNER = 2048
STATE = 16
RANK = 64
KERNEL = 4
SEQ = 384
BLOCK = 128
DOCS = 4
DOC_MOST = 192
ROWS = 32


def raised(array, own_key, source, target, shards_of, factor):
    def block_of(position):
        return (jnp.arange(array.shape[position]) // (array.shape[position] // shards_of)).reshape((-1,) + (1,) * (array.ndim - 1 - position))

    near = jax.random.permutation(own_key, shards_of)[block_of(target)]
    far = (block_of(target) + shards_of // 2) % shards_of
    return jnp.where((block_of(source) == near) | (block_of(source) == far), factor * array, array)


def block_scale(key, dims, shards, least, largest):
    factor_of, own = 1.0, jax.random.fold_in(key, 6)
    for dim, blocks in shards:
        draws = jnp.exp(jax.random.uniform(jax.random.fold_in(own, dim), (blocks,), jnp.float32, least / len(shards), largest / len(shards)))
        factor_of = factor_of * jnp.repeat(draws, dims[dim] // blocks).reshape([-1 if axis == dim else 1 for axis in range(len(dims))])
    return factor_of


def split_up(number_of, total, bound, slope):
    weights = [(1 << 20) // math.isqrt(rank ** slope) + 1 for rank in range(2, number_of + 1)]
    surplus, holding = total - bound - (number_of - 1), [1] * (number_of - 1)
    while surplus > 0:
        free = [i for i in range(number_of - 1) if holding[i] < bound]
        mass, budget = sum([weights[i] for i in free]), surplus
        for i in free:
            addition = min(bound - holding[i], max(1, budget * weights[i] // mass), surplus)
            holding[i] = holding[i] + addition
            surplus = surplus - addition
    return np.array([bound] + holding)


def uneven_parts(stream_key, amount, total, most, skew):
    if amount == 2:
        one = jax.random.randint(stream_key, (), max(1, total - most), min(most, total - 1) + 1)
        return jnp.stack([one, total - one])
    tallies = jnp.asarray(split_up(amount, total, most, skew), jnp.int32)
    pairs = (amount - 1) // 2
    giver, receiver = tallies[1:1 + 2 * pairs:2], tallies[2:2 + 2 * pairs:2]
    room = jnp.minimum(giver - 1, most - receiver)
    moved = jax.random.randint(jax.random.fold_in(stream_key, 1), (pairs,), 0, 1 << 20) % (room + 1)
    tallies = tallies.at[1:1 + 2 * pairs:2].set(giver - moved).at[2:2 + 2 * pairs:2].set(receiver + moved)
    return tallies[jax.random.permutation(jax.random.fold_in(stream_key, 2), amount)]


def scatter_about(own_key, extent, deviation, bound, shards=(), kind=jnp.bfloat16):
    array = jax.random.normal(own_key, extent, jnp.float32) * deviation
    if len(shards) > 0:
        array = block_scale(own_key, extent, shards, -0.22, 0.18) * array
    return jnp.clip(array, min=-bound, max=bound).astype(kind)


def noise_with(own_key, extent, spread, most, cuts, heavy, kind=jnp.bfloat16):
    drawn = spread * jax.random.normal(own_key, extent, jnp.float32)
    if cuts:
        drawn = drawn * block_scale(own_key, extent, cuts, -0.22, 0.18)
    return jnp.clip(raised(drawn, jax.random.fold_in(own_key, 3), *heavy), -most, most).astype(kind)


def setup_inputs(seed: int = 0) -> dict:
    splits = jax.random.split(jax.random.key(seed), 14)
    return {
        "tokens": noise_with(splits[0], (ROWS, SEQ, D), 1.0, 6.0, ((0, 32),), (0, 2, 32, 2.75)),
        "doc_lengths": jax.vmap(lambda own: uneven_parts(own, DOCS, SEQ, DOC_MOST, 2))(jax.random.split(splits[1], ROWS)).reshape((ROWS, DOCS)).astype(jnp.int32),
        "cotangent": noise_with(splits[2], (ROWS, SEQ, D), 1.0, 6.0, ((0, 32),), (0, 2, 32, 2.75)),
        "norm_gain": jnp.clip(1.0 + 0.15 * jax.random.normal(splits[3], (D,), jnp.float32), 0.25, 1.75).astype(jnp.bfloat16),
        "input_weight": scatter_about(splits[4], (D, 2 * INNER), D ** -0.5, 0.1875, ((0, 16),)),
        "filter_weight": scatter_about(splits[5], (INNER, KERNEL), KERNEL ** -0.5, 3.0, ((0, 16),)),
        "filter_bias": jnp.clip(jax.random.uniform(splits[6], (INNER,), jnp.float32, -0.5, 0.5) * block_scale(splits[6], (INNER,), ((0, 16),), -0.4, 0.0), -0.5, 0.5).astype(jnp.bfloat16),
        "select_weight": scatter_about(splits[7], (INNER, RANK + 2 * STATE), INNER ** -0.5, 0.125, ((0, 16),)),
        "delta_weight": scatter_about(splits[8], (INNER, RANK), RANK ** -0.5, 0.75, ((0, 16),)),
        "delta_bias": jnp.clip(-4.59375 + 3.09375 * jax.random.uniform(splits[9], (INNER,), jnp.float32) ** block_scale(splits[9], (INNER,), ((0, 16),), -0.2, 0.2), -4.59375, -1.5).astype(jnp.bfloat16),
        "decay_log": jnp.clip(2.765625 * jax.random.uniform(splits[10], (INNER, STATE), jnp.float32) ** block_scale(splits[10], (INNER, STATE), ((0, 16),), -0.2, 0.2), 0.0, 2.765625).astype(jnp.bfloat16),
        "skip_gain": jnp.clip(2.0 * jax.random.uniform(splits[11], (INNER,), jnp.float32) ** block_scale(splits[11], (INNER,), ((0, 16),), -0.2, 0.2), 0.0, 2.0).astype(jnp.bfloat16),
        "output_weight": scatter_about(splits[12], (D, INNER), (INNER // 4) ** -0.5, 0.25, ((0, 16),)),
    }


EPS = 1e-05
exact_mode = lax.Precision.HIGHEST

@jax.custom_vjp
def low(v):
    return lax.optimization_barrier(v.astype(jnp.bfloat16)).astype(jnp.float32)

@jax.custom_vjp
def low_back(v):
    return v

def low_keep(v):
    return (low(v), None)

def low_pass(kept, grad):
    return (grad,)

def back_keep(v):
    return (v, None)

def back_low(kept, grad):
    return (low(grad),)
low.defvjp(low_keep, low_pass)
low_back.defvjp(back_keep, back_low)

def doc_offsets(lengths):
    starts = jnp.cumsum(lengths, axis=-1) - lengths
    places = jnp.arange(SEQ, dtype=jnp.int32)
    passed = places[None, :, None] >= starts[:, None, :]
    begins = lax.optimization_barrier(jnp.max(jnp.where(passed, starts[:, None, :], 0), axis=-1))
    return places[None, :] - begins

def lagged(values, steps_back):
    if steps_back == 0:
        return values
    return jnp.pad(values, ((0, 0), (steps_back, 0), (0, 0)))[:, :values.shape[1]]

def selective(step_size, activated, write_coef, read_coef, keeping, decay_rates):
    groups = step_size.shape[0]
    blocks = SEQ // BLOCK

    def blocked(values):
        moved = jnp.swapaxes(values, 0, 1)
        return moved.reshape((blocks, BLOCK) + moved.shape[1:])

    def one_block(running, pieces):

        def one_place(current, inputs_now):
            sizes_now, drive_now, write_now, read_now, keep_now = inputs_now
            factor = jnp.exp(sizes_now[:, None, :] * decay_rates[None]) * keep_now[:, None, None]
            current = factor * current + write_now[:, :, None] * drive_now[:, None, :]
            return (current, lax.optimization_barrier(jnp.sum(current * read_now[:, :, None], axis=1)))
        return lax.scan(one_place, running, pieces)
    initial = jnp.zeros((groups, STATE, INNER), step_size.dtype)
    driven = step_size * activated
    stacked = (blocked(step_size), blocked(driven), blocked(write_coef), blocked(read_coef), blocked(keeping))
    final_state, results = lax.scan(jax.checkpoint(one_block), initial, stacked)
    results = results.reshape((SEQ, groups, INNER))
    return jnp.swapaxes(results, 0, 1)

def block_layer(rows_in, lengths, params):
    norm_gain, input_weight, filter_weight, filter_bias, select_weight, delta_weight, delta_bias, decay_log, skip_gain, output_weight = params
    inv_rms = lax.rsqrt(lax.optimization_barrier(jnp.mean(rows_in * rows_in, axis=-1, keepdims=True)) + EPS)
    normed = low(rows_in * inv_rms * norm_gain)
    projected = low_back(jnp.einsum('gsd,df->gsf', normed, input_weight, precision=exact_mode))
    inner_in = projected[..., :INNER]
    gate_in = projected[..., INNER:]
    offsets = doc_offsets(lengths)
    conv_out = filter_bias
    for steps_back in range(KERNEL):
        shifted = jnp.where((offsets >= steps_back)[..., None], lagged(inner_in, steps_back), 0.0)
        conv_out = conv_out + filter_weight[:, KERNEL - 1 - steps_back] * shifted
    activated = jax.nn.silu(conv_out)
    x_out = low_back(jnp.einsum('gse,ef->gsf', low(activated), select_weight, precision=exact_mode))
    delta_low = low(x_out[..., :RANK])
    write_coef = x_out[..., RANK:RANK + STATE]
    read_coef = x_out[..., RANK + STATE:]
    dt_pre = low_back(jnp.einsum('gsr,er->gse', delta_low, delta_weight, precision=exact_mode)) + delta_bias
    step_size = jax.nn.softplus(dt_pre)
    decay_rates = -jnp.exp(decay_log).T
    keeping = (offsets > 0).astype(rows_in.dtype)
    scanned = selective(step_size, activated, write_coef, read_coef, keeping, decay_rates) + skip_gain * activated
    gated = low(scanned * jax.nn.silu(gate_in))
    return rows_in + jnp.einsum('gse,de->gsd', gated, output_weight, precision=exact_mode)

def reference(tokens, doc_lengths, cotangent, norm_gain, input_weight, filter_weight, filter_bias, select_weight, delta_weight, delta_bias, decay_log, skip_gain, output_weight):
    group_rows = math.gcd(ROWS, max(1, 4096 // SEQ))
    group_count = ROWS // group_rows
    floats = tokens.astype(jnp.float32).reshape(group_count, group_rows, SEQ, D)
    lengths = doc_lengths.reshape(group_count, group_rows, DOCS)
    params = tuple((weight.astype(jnp.float32) for weight in (norm_gain, input_weight, filter_weight, filter_bias, select_weight, delta_weight, delta_bias, decay_log, skip_gain, output_weight)))

    def whole_layer(rows_all, weights):

        def one_group(unused, pieces):
            return (unused, block_layer(pieces[0], pieces[1], weights))
        return lax.scan(jax.checkpoint(one_group), jnp.zeros((), jnp.float32), (rows_all, lengths))[1]
    mixed_out, pullback = jax.vjp(whole_layer, floats, params)
    tokens_grad, weight_grads = pullback(cotangent.astype(jnp.float32).reshape(group_count, group_rows, SEQ, D))
    return (mixed_out.reshape(ROWS, SEQ, D).astype(jnp.bfloat16), tokens_grad.reshape(ROWS, SEQ, D), weight_grads[0], weight_grads[1], weight_grads[2], weight_grads[3], weight_grads[4], weight_grads[5], weight_grads[6], weight_grads[7], weight_grads[8], weight_grads[9])
```

```python
import functools
import math

import jax
import jax.numpy as jnp
from jax import lax
from jax.experimental import pallas as pl
from jax.experimental.pallas import tpu as pltpu
from jax.sharding import PartitionSpec as P

EPS = 1e-05
CH = 16
N = 16
F32 = jnp.float32
BF = jnp.bfloat16
NT = (((1,), (1,)), ((), ()))
TN = (((0,), (0,)), ((), ()))
BIG = 1e30

def fwd_kernel(dt_ref, dx_ref, bt_ref, cblk_ref, a2_ref, y_ref, h_ref, st_ref, *, tb, lg):
    E = dt_ref.shape[1]
    @pl.when(pl.program_id(0) == 0)
    def _():
        st_ref[...] = jnp.zeros_like(st_ref)

    def chunk(c, _):
        t0 = pl.multiple_of(c * CH, CH)
        bt = bt_ref[c]
        for g in range(E // lg):
            ls = slice(g * lg, (g + 1) * lg)
            a2 = a2_ref[:, ls]
            h = st_ref[:, ls]
            for k in range(CH):
                dt = jnp.broadcast_to(dt_ref[pl.ds(t0 + k, 1), ls], (N, lg))
                dx = jnp.broadcast_to(dx_ref[pl.ds(t0 + k, 1), ls], (N, lg))
                b = jnp.broadcast_to(bt[:, k:k + 1], (N, lg))
                h = jnp.exp2(dt * a2) * h + b * dx
                h_ref[pl.ds(pl.multiple_of((t0 + k) * N, N), N), ls] = h.astype(BF)
            st_ref[:, ls] = h
        y_ref[pl.ds(t0, CH), :] = jnp.dot(cblk_ref[pl.ds(t0, CH), :], h_ref[pl.ds(pl.multiple_of(t0 * N, CH * N), CH * N), :],
                                          preferred_element_type=F32)
        return 0
    lax.fori_loop(0, tb // CH, chunk, 0)

def scan_forward(dtm, dx, btc, cblk, a2, tb=128, lg=512):
    T, E = dtm.shape
    nb = T // tb
    return pl.pallas_call(
        functools.partial(fwd_kernel, tb=tb, lg=lg),
        grid=(nb,),
        in_specs=[pl.BlockSpec((tb, E), lambda i: (i, 0)), pl.BlockSpec((tb, E), lambda i: (i, 0)),
                  pl.BlockSpec((tb // CH, N, CH), lambda i: (i, 0, 0)), pl.BlockSpec((tb, CH * N), lambda i: (i, 0)),
                  pl.BlockSpec((N, E), lambda i: (0, 0))],
        out_specs=[pl.BlockSpec((tb, E), lambda i: (i, 0)), pl.BlockSpec((tb * N, E), lambda i: (i, 0))],
        out_shape=[jax.ShapeDtypeStruct((T, E), F32), jax.ShapeDtypeStruct((T * N, E), BF)],
        scratch_shapes=[pltpu.VMEM((N, E), F32)],
        compiler_params=pltpu.CompilerParams(vmem_limit_bytes=40 << 20),
        name="scan_fwd",
    )(dtm, dx, btc, cblk, a2)

def bwd_kernel(dt_ref, g_ref, dxl_ref, ct_ref, bblk_ref, a2_ref, h_ref, hp_ref,
               dg_ref, st_ref, wg_ref, rg_ref, ra_ref, carry_ref, sg_s, da_s, *, tb, lg):
    E = dt_ref.shape[1]
    @pl.when(pl.program_id(0) == 0)
    def _():
        carry_ref[...] = jnp.zeros_like(carry_ref)
        ra_ref[...] = jnp.zeros_like(ra_ref)
    rows = lax.broadcasted_iota(jnp.int32, (CH, CH * N), 0)
    cols = lax.broadcasted_iota(jnp.int32, (CH, CH * N), 1)
    mask = (cols // N) == rows
    ones = mask.astype(BF)
    nc = tb // CH
    nt = (((1,), (1,)), ((), ()))

    def do_chunk(c, first):
        t0 = pl.multiple_of(c * CH, CH)
        ct = ct_ref[c]
        for g in range(E // lg):
            ls = slice(g * lg, (g + 1) * lg)
            a2 = a2_ref[:, ls]
            carry = carry_ref[:, ls]
            racc = ra_ref[:, ls]
            for k in range(CH - 1, -1, -1):
                dt = jnp.broadcast_to(dt_ref[pl.ds(t0 + k, 1), ls], (N, lg))
                gg = jnp.broadcast_to(g_ref[pl.ds(t0 + k, 1), ls], (N, lg))
                cc = jnp.broadcast_to(ct[:, k:k + 1], (N, lg))
                if k == 0 and first:
                    hp = hp_ref[:, ls]
                else:
                    hp = h_ref[pl.ds(pl.multiple_of((t0 + k - 1) * N, N), N), ls]
                sg = cc * gg + carry
                carry = jnp.exp2(dt * a2) * sg
                dterm = carry * hp.astype(F32)
                racc = racc + dterm * dt
                sg_s[k * N:(k + 1) * N, ls] = sg.astype(BF)
                da_s[k * N:(k + 1) * N, ls] = (dterm * a2).astype(BF)
            carry_ref[:, ls] = carry
            ra_ref[:, ls] = racc
        sgc = sg_s[...]
        dg_ref[pl.ds(t0, CH), :] = jnp.dot(bblk_ref[pl.ds(t0, CH), :], sgc, preferred_element_type=F32)
        st_ref[pl.ds(t0, CH), :] = jnp.dot(ones, da_s[...], preferred_element_type=F32) * math.log(2.0)
        wo = lax.dot_general(dxl_ref[pl.ds(t0, CH), :], sgc, nt, preferred_element_type=F32)
        wg_ref[0, pl.ds(c, 1), :] = jnp.sum(jnp.where(mask, wo, 0.0), axis=0, keepdims=True)
        hc = h_ref[pl.ds(pl.multiple_of(t0 * N, CH * N), CH * N), :]
        ro = lax.dot_general(g_ref[pl.ds(t0, CH), :].astype(BF), hc, nt, preferred_element_type=F32)
        rg_ref[0, pl.ds(c, 1), :] = jnp.sum(jnp.where(mask, ro, 0.0), axis=0, keepdims=True)

    def chunk(i, _):
        do_chunk(nc - 1 - i, False)
        return 0
    lax.fori_loop(0, nc - 1, chunk, 0)
    do_chunk(0, True)

def scan_backward(dtm, g, dxl, ctc, bblk, a2, h, tb=128, lg=512):
    T, E = dtm.shape
    nb = T // tb
    r = lambda i: (nb - 1 - i, 0)
    nc = tb // CH
    return pl.pallas_call(
        functools.partial(bwd_kernel, tb=tb, lg=lg),
        grid=(nb,),
        in_specs=[pl.BlockSpec((tb, E), r), pl.BlockSpec((tb, E), r), pl.BlockSpec((tb, E), r),
                  pl.BlockSpec((nc, N, CH), lambda i: (nb - 1 - i, 0, 0)), pl.BlockSpec((tb, CH * N), r),
                  pl.BlockSpec((N, E), lambda i: (0, 0)),
                  pl.BlockSpec((tb * N, E), r),
                  pl.BlockSpec((N, E), lambda i: (jnp.maximum((nb - 1 - i) * tb - 1, 0), 0))],
        out_specs=[pl.BlockSpec((tb, E), r), pl.BlockSpec((tb, E), r),
                   pl.BlockSpec((1, nc, CH * N), lambda i: (nb - 1 - i, 0, 0)), pl.BlockSpec((1, nc, CH * N), lambda i: (nb - 1 - i, 0, 0)),
                   pl.BlockSpec((N, E), lambda i: (0, 0))],
        out_shape=[jax.ShapeDtypeStruct((T, E), F32), jax.ShapeDtypeStruct((T, E), F32),
                   jax.ShapeDtypeStruct((nb, nc, CH * N), F32), jax.ShapeDtypeStruct((nb, nc, CH * N), F32),
                   jax.ShapeDtypeStruct((N, E), F32)],
        scratch_shapes=[pltpu.VMEM((N, E), F32), pltpu.VMEM((CH * N, E), BF), pltpu.VMEM((CH * N, E), BF)],
        compiler_params=pltpu.CompilerParams(vmem_limit_bytes=40 << 20),
        name="scan_bwd",
    )(dtm, g, dxl, ctc, bblk, a2, h, h)

def block_diagonal(m):
    T = m.shape[0]
    eye = jnp.tile(jnp.eye(CH, dtype=F32), (T // CH, 1))
    return (eye[:, :, None] * m[:, None, :]).reshape(T, CH * N).astype(BF)

def chunked(m):
    return jnp.swapaxes(m.reshape(m.shape[0] // CH, CH, N), 1, 2)


def doc_offsets(lengths, length):
    starts = jnp.cumsum(lengths, axis=-1) - lengths
    places = jnp.arange(length, dtype=jnp.int32)
    passed = places[None, :, None] >= starts[:, None, :]
    begins = jnp.max(jnp.where(passed, starts[:, None, :], 0), axis=-1)
    return places[None, :] - begins


def dot(a, b, dims=(((1,), (0,)), ((), ()))):
    return lax.dot_general(a, b, dims, preferred_element_type=F32)


def lag(v, j):
    return v if j == 0 else jnp.pad(v, ((j, 0), (0, 0)))[: v.shape[0]]


def lead(v, j):
    return v if j == 0 else jnp.pad(v, ((0, j), (0, 0)))[j:]


def local(
    tokens,
    doc_lengths,
    cotangent,
    norm_gain,
    input_weight,
    filter_weight,
    filter_bias,
    select_weight,
    delta_weight,
    delta_bias,
    decay_log,
    skip_gain,
    output_weight,
    *,
    dp,
):
    core = lax.axis_index("rep")
    rows, length, width = tokens.shape
    inner = input_weight.shape[1] // 2
    half = inner // 2
    rank = delta_weight.shape[1]
    state = decay_log.shape[1]
    taps = filter_weight.shape[1]
    own_e = filter_weight.shape[0]
    own_d = norm_gain.shape[0]
    total = 2 * rows * length

    def columns(weight, start):
        return lax.dynamic_slice(weight, (0, start + core * half), (weight.shape[0], half))

    def gather(x):
        return lax.all_gather(x, "dp", axis=0, tiled=True)

    w_inner = gather(columns(input_weight, 0))
    w_gate = gather(columns(input_weight, inner))
    w_out = gather(columns(output_weight, 0))
    smalls = jnp.concatenate(
        [
            select_weight,
            delta_weight,
            decay_log,
            filter_weight,
            filter_bias[:, None],
            delta_bias[:, None],
            skip_gain[:, None],
            jnp.pad(norm_gain, (0, own_e - own_d))[:, None],
        ],
        axis=1,
    )
    smalls = jnp.pad(smalls, ((0, 0), (0, 256 - smalls.shape[1])))
    smalls = gather(smalls)
    c0 = rank + 2 * state
    c1 = c0 + rank
    c2 = c1 + state
    c3 = c2 + taps
    gain = smalls.reshape(dp, own_e, 256)[:, :own_d, c3 + 3].reshape(width).astype(F32)
    mine = lax.dynamic_slice(smalls, (core * half, 0), (half, 256))
    select = mine[:, :c0]
    delta = mine[:, c0:c1]
    rates = -jnp.exp(mine[:, c1:c2].astype(F32)).T
    taps_w = mine[:, c2:c3].astype(F32)
    f_bias = mine[:, c3].astype(F32)
    d_bias = mine[:, c3 + 1].astype(F32)
    skip = mine[:, c3 + 2].astype(F32)

    def both(x):
        return lax.all_gather(x, "rep", axis=0, tiled=True)

    toks = both(tokens.reshape(rows * length, width))
    cot = both(cotangent.reshape(rows * length, width))
    offsets = doc_offsets(both(doc_lengths), length).reshape(total, 1)
    keeping = offsets > 0

    floats = toks.astype(F32)
    inv_rms = lax.rsqrt(jnp.mean(floats * floats, axis=-1, keepdims=True) + EPS)
    scaled = floats * inv_rms
    normed = (scaled * gain).astype(BF)
    inner_in = dot(normed, w_inner)
    gate_in = dot(normed, w_gate)

    conv_out = f_bias
    for j in range(taps):
        conv_out = conv_out + taps_w[:, taps - 1 - j] * jnp.where(offsets >= j, lag(inner_in, j), 0.0)
    sig_c = jax.nn.sigmoid(conv_out)
    act = conv_out * sig_c
    act_low = act.astype(BF)
    x_out = lax.psum(dot(act_low, select), "rep")
    delta_low = x_out[:, :rank].astype(BF)
    write = x_out[:, rank : rank + state]
    read = x_out[:, rank + state :]
    dt_pre = dot(delta_low, delta, NT) + d_bias
    dt = jax.nn.softplus(dt_pre)
    dtm = jnp.where(keeping, dt, BIG)
    dx = dt * act
    a2 = rates * math.log2(math.e)
    y, states = scan_forward(dtm, dx, chunked(write), block_diagonal(read), a2)
    scanned = y + skip * act
    sig_g = jax.nn.sigmoid(gate_in)
    gate_act = gate_in * sig_g
    gated = (scanned * gate_act).astype(BF)
    branch = dot(gated, w_out, NT)
    branch = lax.psum_scatter(branch, "rep", scatter_dimension=0, tiled=True)
    mixed = (tokens.astype(F32).reshape(rows * length, width) + branch).astype(BF)

    d_out = dot(cot, gated, TN)
    gated_grad = dot(cot, w_out)
    scan_grad = gated_grad * gate_act
    gate_grad = (gated_grad * scanned * (sig_g * (1.0 + gate_in * (1.0 - sig_g)))).astype(BF)
    d_gate = dot(normed, gate_grad, TN)
    skip_grad = jnp.sum(scan_grad * act, axis=0)

    driven_grad, decay_sum, write_grad, read_grad, rates_grad = scan_backward(
        dtm, scan_grad, dx.astype(BF), chunked(read), block_diagonal(write), a2, states
    )
    write_grad = write_grad.reshape(total, state)
    read_grad = read_grad.reshape(total, state)
    decay_grad = (rates_grad * rates).T
    pre_grad = (driven_grad * act + decay_sum) * jax.nn.sigmoid(dt_pre)
    dbias_grad = jnp.sum(pre_grad, axis=0)
    pre_low = pre_grad.astype(BF)
    delta_grad = dot(pre_low, delta_low, TN)
    x_grad = jnp.concatenate([dot(pre_low, delta), write_grad, read_grad], axis=1)
    x_grad = lax.psum(x_grad, "rep").astype(BF)
    select_grad = dot(act_low, x_grad, TN)
    act_grad = scan_grad * skip + driven_grad * dt + dot(x_grad, select, NT)
    conv_grad = act_grad * (sig_c * (1.0 + conv_out * (1.0 - sig_c)))
    fbias_grad = jnp.sum(conv_grad, axis=0)
    cols = [None] * taps
    inner_grad = 0.0
    for j in range(taps):
        masked = jnp.where(offsets >= j, conv_grad, 0.0)
        cols[taps - 1 - j] = jnp.sum(masked * lag(inner_in, j), axis=0)
        inner_grad = inner_grad + lead(masked, j) * taps_w[:, taps - 1 - j]
    inner_grad = inner_grad.astype(BF)
    d_inner = dot(normed, inner_grad, TN)
    normed_grad = dot(inner_grad, w_inner, NT) + dot(gate_grad, w_gate, NT)
    normed_grad = lax.psum_scatter(normed_grad, "rep", scatter_dimension=0, tiled=True)
    own_f = tokens.astype(F32).reshape(rows * length, width)
    own_inv = lax.rsqrt(jnp.mean(own_f * own_f, axis=-1, keepdims=True) + EPS)
    own_scaled = own_f * own_inv
    gain_grad = jnp.sum(normed_grad * own_scaled, axis=0)
    scaled_grad = normed_grad * gain
    tokens_grad = cotangent.astype(F32).reshape(rows * length, width) + own_inv * (
        scaled_grad - own_scaled * jnp.mean(scaled_grad * own_scaled, axis=-1, keepdims=True)
    )

    def scatter(x):
        return lax.psum_scatter(x.astype(BF), "dp", scatter_dimension=0, tiled=True)

    big = jnp.stack([scatter(d_inner), scatter(d_gate), scatter(d_out)])
    big = lax.all_gather(big, "rep", axis=0)
    in_share = jnp.concatenate([big[0, 0], big[1, 0], big[0, 1], big[1, 1]], axis=1).astype(F32)
    out_share = jnp.concatenate([big[0, 2], big[1, 2]], axis=1).astype(F32)
    small = jnp.concatenate(
        [
            select_grad,
            delta_grad,
            decay_grad,
            jnp.stack(cols, axis=1),
            fbias_grad[:, None],
            dbias_grad[:, None],
            skip_grad[:, None],
        ],
        axis=1,
    )
    small = lax.all_gather(small.astype(BF), "rep", axis=0, tiled=True)
    gain_grad = lax.psum(gain_grad, "rep").reshape(dp, own_d)
    small = jnp.concatenate([small, jnp.pad(gain_grad, ((0, 0), (0, own_e - own_d))).reshape(inner, 1).astype(BF)], axis=1)
    small = jnp.pad(small, ((0, 0), (0, 256 - small.shape[1])))
    small = scatter(small).astype(F32)
    return (
        mixed.reshape(rows, length, width),
        tokens_grad.reshape(rows, length, width),
        small[:own_d, c3 + 3],
        in_share,
        small[:, c2:c3],
        small[:, c3],
        small[:, :c0],
        small[:, c0:c1],
        small[:, c3 + 1],
        small[:, c1:c2],
        small[:, c3 + 2],
        out_share,
    )


def solution(mesh):
    dp_rep = ("dp", "rep")
    one = P("dp")
    two = P("dp", None)
    three = P(dp_rep, None, None)
    return jax.shard_map(
        functools.partial(local, dp=mesh.shape["dp"]),
        mesh=mesh,
        in_specs=(three, P(dp_rep, None), three, one, two, two, one, two, two, one, two, one, two),
        out_specs=(three, three, one, two, two, one, two, two, one, two, one, two),
        check_vma=False,
    )
```

```python
import functools
import math

import jax
import jax.numpy as jnp
from jax import lax
from jax.experimental import pallas as pl
from jax.experimental.pallas import tpu as pltpu
from jax.sharding import PartitionSpec as P

EPS = 1e-05
CH = 16
N = 16
F32 = jnp.float32
BF = jnp.bfloat16
NT = (((1,), (1,)), ((), ()))
TN = (((0,), (0,)), ((), ()))
BIG = 1e30

def dot(a, b, dims=(((1,), (0,)), ((), ()))):
    return lax.dot_general(a, b, dims, preferred_element_type=F32)


MESH = pl.DeviceIdType.MESH


def plane(dp):
    return 4 if dp == 16 else 0


class Links:
    def __init__(self, dp):
        self.dp = dp
        self.depth = plane(dp)
        self.me = lax.axis_index("dp")
        self.core = lax.axis_index("rep")
        if self.depth:
            self.z, self.y, self.x = self.me // 4, (self.me // 2) % 2, self.me % 2
            self.xn = self.at(self.z, self.y, 1 - self.x)
            self.yn = self.at(self.z, 1 - self.y, self.x)
            self.zs = [self.at(self.up(k), self.y, self.x) for k in range(1, self.depth)]
            self.peers = self.zs + [self.xn, self.yn]
        else:
            self.peers = [lax.rem(self.me + k, dp) for k in range(1, dp)]

    def up(self, k):
        return lax.rem(self.z + k, self.depth)

    def down(self, k):
        return lax.rem(self.z + self.depth - k, self.depth)

    def at(self, z, y, x):
        return (z * 2 + y) * 2 + x

    def barrier(self, sibling=True):
        sem = pltpu.get_barrier_semaphore()
        for peer in self.peers:
            pl.semaphore_signal(sem, inc=1, device_id=(peer, self.core), device_id_type=MESH)
        if sibling:
            pl.semaphore_signal(sem, inc=1, device_id=(self.me, 1 - self.core), device_id_type=MESH)
        pl.semaphore_wait(sem, len(self.peers) + int(sibling))

    def send(self, src, dst, send_sem, recv_sem, chip):
        return pltpu.make_async_remote_copy(
            src_ref=src, dst_ref=dst, send_sem=send_sem, recv_sem=recv_sem,
            device_id=(chip, self.core), device_id_type=MESH,
        )

    def swap(self, src, dst, send_sem, recv_sem):
        return pltpu.make_async_remote_copy(
            src_ref=src, dst_ref=dst, send_sem=send_sem, recv_sem=recv_sem,
            device_id=(self.me, 1 - self.core), device_id_type=MESH,
        )


def copies_of(dp):
    return 19 if plane(dp) else dp - 1


def gather_steps(links, src, dst, ss, rs):
    me = links.me
    rows = src.shape[0]

    def part(b, first=0, count=rows):
        return pl.ds(pl.multiple_of(b * rows + first, count), count)

    if not links.depth:
        cps = [links.send(src, dst.at[part(me)], ss.at[k], rs.at[k], p) for k, p in enumerate(links.peers)]

        def begin():
            for c in cps:
                c.start()
            dst[part(me), :] = src[...]

        def end():
            for c in cps:
                c.wait()

        return [begin] + [lambda: None] * 7 + [end]
    depth, half = links.depth, rows // 2
    z, y, x, xn, yn = links.z, links.y, links.x, links.xn, links.yn
    zc = [links.send(src, dst.at[part(me)], ss.at[k], rs.at[k], p) for k, p in enumerate(links.zs)]
    xc, yc, xf, yf = [], [], [], []
    for k in range(depth):
        b = links.at(links.down(k), y, x)
        s = src if k == 0 else dst.at[part(b)]
        n = 3 + 4 * k
        xc.append(links.send(s, dst.at[part(b)], ss.at[n], rs.at[n], xn))
        yc.append(links.send(s, dst.at[part(b)], ss.at[n + 1], rs.at[n + 1], yn))
        bx = links.at(links.down(k), y, 1 - x)
        by = links.at(links.down(k), 1 - y, x)
        lo = dst.at[part(bx, 0, half)]
        hi = dst.at[part(by, half, half)]
        yf.append(links.send(lo, lo, ss.at[n + 2], rs.at[n + 2], yn))
        xf.append(links.send(hi, hi, ss.at[n + 3], rs.at[n + 3], xn))

    def begin():
        for c in zc:
            c.start()
        xc[0].start()
        yc[0].start()
        dst[part(me), :] = src[...]

    def spread(k):
        def run():
            zc[k - 1].wait_recv()
            xc[k].start()
            yc[k].start()
        return run

    def forward(k):
        def run():
            xc[k].wait_recv()
            yf[k].start()
            yc[k].wait_recv()
            xf[k].start()
        return run

    def end():
        for k in range(depth):
            yf[k].wait_recv()
            xf[k].wait_recv()
        for c in zc + xc + yc + xf + yf:
            c.wait_send()

    return [begin, spread(1), spread(2), spread(3), forward(0), forward(1), forward(2), forward(3), end]


def scatter_scratch(dp, rows, cols):
    if not plane(dp):
        return [pltpu.VMEM((dp - 1, rows, cols), BF)]
    d, h = plane(dp), rows // 2
    return [
        pltpu.VMEM((d, 2, h, cols), BF),
        pltpu.VMEM((d, 2, rows, cols), BF),
        pltpu.VMEM((d, 2, rows, cols), BF),
        pltpu.VMEM((d, rows, cols), BF),
        pltpu.VMEM((d - 1, rows, cols), BF),
    ]


def scatter_steps(links, src, out, bufs, ss, rs):
    me = links.me
    if not links.depth:
        (got,) = bufs
        cps = [links.send(src.at[p], got.at[k], ss.at[k], rs.at[k], p) for k, p in enumerate(links.peers)]

        def begin():
            for c in cps:
                c.start()

        def end():
            for c in cps:
                c.wait()

            def add(k, total):
                return total + got[k].astype(F32)

            out[...] = lax.fori_loop(0, links.dp - 1, add, src[me].astype(F32))

        return [begin] + [lambda: None] * 8 + [end]
    halves, to, come, zto, zcome = bufs
    depth, rows = links.depth, src.shape[1]
    h = rows // 2
    z, y, x, xn, yn = links.z, links.y, links.x, links.xn, links.yn
    ac, bc, cc = [], [], []
    for k in range(depth):
        zz = links.up(k)
        diag = links.at(zz, 1 - y, 1 - x)
        n = 4 * k
        ac.append((
            links.send(src.at[diag, pl.ds(0, h)], halves.at[k, 0], ss.at[n], rs.at[n], xn),
            links.send(src.at[diag, pl.ds(h, h)], halves.at[k, 1], ss.at[n + 1], rs.at[n + 1], yn),
        ))
        bc.append((
            links.send(to.at[k, 0], come.at[k, 0], ss.at[n + 2], rs.at[n + 2], xn),
            links.send(to.at[k, 1], come.at[k, 1], ss.at[n + 3], rs.at[n + 3], yn),
        ))
        if k:
            n = 4 * depth + k - 1
            cc.append(links.send(zto.at[k], zcome.at[k - 1], ss.at[n], rs.at[n], links.zs[k - 1]))

    def begin():
        for k in (1, 2, 3, 0):
            ac[k][0].start()
            ac[k][1].start()

    def middle(k):
        def run():
            zz = links.up(k)
            bx = links.at(zz, y, 1 - x)
            by = links.at(zz, 1 - y, x)
            ac[k][0].wait_recv()
            to[k, 1, pl.ds(0, h)] = (src[by, pl.ds(0, h)].astype(F32) + halves[k, 0].astype(F32)).astype(BF)
            to[k, 1, pl.ds(h, h)] = src[by, pl.ds(h, h)]
            bc[k][1].start()
            ac[k][1].wait_recv()
            to[k, 0, pl.ds(h, h)] = (src[bx, pl.ds(h, h)].astype(F32) + halves[k, 1].astype(F32)).astype(BF)
            to[k, 0, pl.ds(0, h)] = src[bx, pl.ds(0, h)]
            bc[k][0].start()
        return run

    def along(k):
        def run():
            bc[k][0].wait_recv()
            bc[k][1].wait_recv()
            own = links.at(links.up(k), y, x)
            total = src[own].astype(F32) + come[k, 0].astype(F32) + come[k, 1].astype(F32)
            if k:
                zto[k] = total.astype(BF)
                cc[k - 1].start()
            else:
                out[...] = total
        return run

    def end():
        for k in range(depth - 1):
            cc[k].wait_recv()
            out[...] += zcome[k].astype(F32)
        for k in range(depth):
            for c in ac[k] + bc[k]:
                c.wait_send()
        for c in cc:
            c.wait_send()

    return [begin, middle(1), middle(2), along(1), middle(3), along(2), middle(0), along(3), along(0), end]


LOG2E = math.log2(math.e)
SEL, RANK_C = 0, 0


def vec(n, d=F32):
    return pltpu.VMEM(n, d)


def sigmoid(v):
    return 0.5 * jnp.tanh(0.5 * v) + 0.5


def softplus(v):
    u = jnp.exp(-jnp.abs(v))
    return jnp.maximum(v, 0.0) + jnp.where(u < 1e-3, u * (1.0 - 0.5 * u), jnp.log(1.0 + u))


def block_mask():
    rows = lax.broadcasted_iota(jnp.int32, (CH, CH * N), 0)
    cols = lax.broadcasted_iota(jnp.int32, (CH, CH * N), 1)
    return (cols // N) == rows


def pick(first):
    rows = lax.broadcasted_iota(jnp.int32, (128, CH * N), 0)
    cols = lax.broadcasted_iota(jnp.int32, (128, CH * N), 1)
    return jnp.where(rows - first == cols % N, 1.0, 0.0).astype(BF)


def forward_kernel(
    lens, tok, w_in, w_o, packed,
    wi, wg, wo, sm, toks, offs, normed, xin, conv, actl, xo, dt, dtm, dx, y, hs,
    par, btc, cblk, a2, st, hbuf, xr, xt,
    ss_i, rs_i, ss_s, rs_s, ss_g, rs_g, ss_o, rs_o, sw_s, sw_r, hsem,
    *, dp, dims,
):
    taps, rank = dims
    links = Links(dp)
    core, me = links.core, links.me
    rows, width = tok.shape
    half = wi.shape[1]
    total = 2 * rows
    own_d = w_in.shape[0]
    own_e = packed.shape[0]
    inner = 2 * half
    hchips = dp // 2

    def cut(ref, start):
        return ref.at[:, pl.ds(pl.multiple_of(start + core * half, 128), half)]

    links.barrier()
    t_idx = lax.broadcasted_iota(jnp.int32, (rows, 128), 0)
    begin = jnp.zeros((rows, 128), jnp.int32)
    start = lens[0, 0]
    for k in range(1, lens.shape[1]):
        begin = jnp.where(t_idx >= start, start, begin)
        start = start + lens[0, k]
    mine = pl.ds(pl.multiple_of(core * rows, rows), rows)
    offs[mine, :] = (t_idx - begin).astype(F32)
    swaps = [
        links.swap(tok, toks.at[mine], sw_s.at[0], sw_r.at[0]),
        links.swap(offs.at[mine], offs.at[mine], sw_s.at[1], sw_r.at[1]),
    ]
    g_i = gather_steps(links, cut(w_in, 0), wi, ss_i, rs_i)
    pk = packed.at[:, pl.ds(pl.multiple_of(core * 128, 128), 128)]
    g_s = gather_steps(links, pk, sm.at[core], ss_s, rs_s)
    g_g = gather_steps(links, cut(w_in, inner), wg, ss_g, rs_g)
    g_o = gather_steps(links, cut(w_o, 0), wo, ss_o, rs_o)
    g_i[0]()
    g_s[0]()
    swaps[0].start()
    swaps[1].start()
    toks[mine, :] = tok[...]
    for k in range(1, len(g_i) - 1):
        g_i[k]()
        g_s[k]()
        if k == 3:
            g_g[0]()
    g_s[-1]()
    theirs = pl.ds(pl.multiple_of((1 - core) * half, half), half)
    s_swap = links.swap(sm.at[core, theirs], sm.at[core, theirs], sw_s.at[2], sw_r.at[2])
    s_swap.start()
    g_i[-1]()
    swaps[0].wait()
    swaps[1].wait()
    g_o[0]()
    s_swap.wait()

    own = pl.multiple_of(core * half, half)
    for b in range(half // 128):
        blk = sm[0, pl.ds(own + b * 128, 128), :].astype(F32)
        par[:, b * 128:(b + 1) * 128] = blk.T
    c1 = rank + 2 * N
    a2[...] = -jnp.exp(par[c1:c1 + N, :]) * LOG2E
    r_taps, r_fb, r_db = c1 + N, c1 + N + taps, c1 + N + taps + 1
    gcol = c1 + N + taps + 3
    pieces = []
    for b in range(2 * half // 128):
        gb = sm[core, pl.ds(b * 128, 128), :].astype(F32).T[gcol:gcol + 1, :]
        pieces.append(gb)
    flat = jnp.concatenate(pieces, axis=1)
    flat = flat.reshape(1, dp, own_e)[:, :, :own_d].reshape(1, width) if False else flat
    gain = jnp.concatenate([flat[:, i * own_e:i * own_e + own_d] for i in range(dp)], axis=1)

    def norm(i, _):
        r = pl.ds(pl.multiple_of(i * 16, 16), 16)
        v = toks[r, :].astype(F32)
        inv = lax.rsqrt(jnp.mean(v * v, axis=-1, keepdims=True) + EPS)
        normed[r, :] = (v * inv * gain).astype(BF)
        return 0

    lax.fori_loop(0, total // 16, norm, 0)
    xin[0:8, :] = jnp.zeros((8, half), F32)

    def in_proj(j, _):
        c = pl.ds(pl.multiple_of(j * 256, 256), 256)
        xin[pl.ds(8, total), c] = dot(normed[...], wi[:, c])
        return 0

    lax.fori_loop(0, half // 256, in_proj, 0)

    def conv_tile(i, _):
        t0 = pl.multiple_of(i * 64, 64)
        o = offs[pl.ds(t0, 64), :]
        for b in range(half // 128):
            c = slice(b * 128, (b + 1) * 128)
            v = xin[pl.ds(t0, 72), c]
            acc = par[r_fb:r_fb + 1, c]
            for j in range(taps):
                s = v[8 - j:72 - j]
                if j:
                    s = jnp.where(o >= float(j), s, 0.0)
                acc = acc + par[r_taps + taps - 1 - j:r_taps + taps - j, c] * s
            conv[pl.ds(t0, 64), c] = acc
            actl[pl.ds(t0, 64), c] = (acc * sigmoid(acc)).astype(BF)
        return 0

    lax.fori_loop(0, total // 64, conv_tile, 0)

    sel = sm.at[0, pl.ds(own, half), :]
    xo[...] = dot(actl[...], sel[...])
    x_swap = links.swap(xo, xr, sw_s.at[3], sw_r.at[3])
    x_swap.start()
    x_swap.wait()
    xo[...] += xr[...]

    dw = sm.at[1, pl.ds(own, half), :]

    def dt_tile(i, _):
        t0 = pl.multiple_of(i * 64, 64)
        o = offs[pl.ds(t0, 64), :]
        low = xo[pl.ds(t0, 64), :].astype(BF)[:, :rank]
        for b in range(half // 256):
            c2 = slice(b * 256, (b + 1) * 256)
            pre2 = dot(low, dw[c2, :][:, :rank], NT)
            for q in range(2):
                c = slice(b * 256 + q * 128, b * 256 + (q + 1) * 128)
                s = softplus(pre2[:, q * 128:(q + 1) * 128] + par[r_db:r_db + 1, c])
                dt[pl.ds(t0, 64), c] = s
                dtm[pl.ds(t0, 64), c] = jnp.where(o > 0.0, s, BIG)
                cv = conv[pl.ds(t0, 64), c]
                dx[pl.ds(t0, 64), c] = s * (cv * sigmoid(cv))
        return 0

    lax.fori_loop(0, total // 64, dt_tile, 0)

    def cols_tile(i, _):
        t0 = pl.multiple_of(i * 128, 128)
        t = xo[pl.ds(t0, 128), :].T
        for q in range(128 // CH):
            btc[i * (128 // CH) + q] = t[rank:rank + N, q * CH:(q + 1) * CH]
        m = jnp.concatenate([block_mask()] * (128 // CH), axis=0)
        cblk[pl.ds(t0, 128), :] = jnp.where(m, dot(xo[pl.ds(t0, 128), :].astype(BF), pick(rank + N)), 0.0).astype(BF)
        return 0

    lax.fori_loop(0, total // 128, cols_tile, 0)

    steps = []
    for a, b in zip(g_g[1:], g_o[1:]):
        steps += [a, b]
    bt_rows = 128 * N
    n_chunks = total // CH
    per = 128 // CH
    st[...] = jnp.zeros_like(st)
    lg = min(512, half)

    def write_out(blk, slot):
        return pltpu.make_async_copy(
            hbuf.at[slot], hs.at[pl.ds(pl.multiple_of(blk * bt_rows, bt_rows), bt_rows)], hsem.at[slot]
        )

    def block(blk, _):
        slot = lax.rem(blk, 2)

        @pl.when(blk >= 2)
        def _():
            write_out(blk - 2, slot).wait()

        def chunk(q, _):
            c = blk * per + q
            t0 = pl.multiple_of(c * CH, CH)
            for k, s in enumerate(steps):
                pl.when(c == 2 + 2 * k)(s)
            bt = btc[c]
            for g in range(half // lg):
                ls = slice(g * lg, (g + 1) * lg)
                a = a2[:, ls]
                h = st[:, ls]
                for k in range(CH):
                    d = jnp.broadcast_to(dtm[pl.ds(t0 + k, 1), ls], (N, lg))
                    v = jnp.broadcast_to(dx[pl.ds(t0 + k, 1), ls], (N, lg))
                    w = jnp.broadcast_to(bt[:, k:k + 1], (N, lg))
                    h = jnp.exp2(d * a) * h + w * v
                    hbuf[slot, pl.ds(pl.multiple_of((q * CH + k) * N, N), N), ls] = h.astype(BF)
                st[:, ls] = h
            hc = hbuf[slot, pl.ds(pl.multiple_of(q * CH * N, CH * N), CH * N), :]
            y[pl.ds(t0, CH), :] = dot(cblk[pl.ds(t0, CH), :], hc)
            return 0

        lax.fori_loop(0, per, chunk, 0)
        write_out(blk, slot).start()
        return 0

    n_blk = total // 128
    lax.fori_loop(0, n_blk, block, 0)
    write_out(n_blk - 2, n_blk % 2).wait()
    write_out(n_blk - 1, (n_blk - 1) % 2).wait()


def forward(lens, tok, w_in, w_o, packed, dp, dims):
    rows, width = tok.shape
    half = w_o.shape[1] // 2
    total = 2 * rows
    n = copies_of(dp)
    sd = jax.ShapeDtypeStruct
    act2 = sd((total, half), F32)
    outs = [
        sd((width, half), BF), sd((width, half), BF), sd((width, half), BF), sd((2, 2 * half, 128), BF),
        sd((total, width), BF), sd((total, 128), F32), sd((total, width), BF), sd((8 + total, half), F32),
        act2, sd((total, half), BF), sd((total, 128), F32), act2, act2, act2, act2, sd((total * N, half), BF),
    ]
    vm = pl.BlockSpec(memory_space=pltpu.VMEM)
    dma = pltpu.SemaphoreType.DMA
    return pl.pallas_call(
        functools.partial(forward_kernel, dp=dp, dims=dims),
        out_shape=outs,
        in_specs=[pl.BlockSpec(memory_space=pltpu.SMEM)] + [vm] * 4,
        out_specs=[vm] * 15 + [pl.BlockSpec(memory_space=pl.ANY)],
        scratch_shapes=[
            vec((128, half)), vec((total // CH, N, CH)), vec((total, CH * N), BF), vec((N, half)), vec((N, half)),
            vec((2, 128 * N, half), BF), vec((total, 128)), vec((128, 128)),
        ] + [dma((n,))] * 8 + [dma((4,)), dma((4,)), dma((2,))],
        compiler_params=pltpu.CompilerParams(collective_id=0, has_side_effects=True, vmem_limit_bytes=58 << 20),
        name="forward",
    )(lens, tok, w_in, w_o, packed)


def bwd_kernel(dt_ref, g_ref, dxl_ref, ct_ref, bblk_ref, a2_ref, h_ref, hp_ref,
               dg_ref, st_ref, wg_ref, rg_ref, ra_ref, carry_ref, sg_s, da_s, *, tb, lg):
    E = dt_ref.shape[1]
    @pl.when(pl.program_id(0) == 0)
    def _():
        carry_ref[...] = jnp.zeros_like(carry_ref)
        ra_ref[...] = jnp.zeros_like(ra_ref)
    rows = lax.broadcasted_iota(jnp.int32, (CH, CH * N), 0)
    cols = lax.broadcasted_iota(jnp.int32, (CH, CH * N), 1)
    mask = (cols // N) == rows
    ones = mask.astype(BF)
    nc = tb // CH
    nt = (((1,), (1,)), ((), ()))

    def do_chunk(c, first):
        t0 = pl.multiple_of(c * CH, CH)
        ct = ct_ref[c]
        for g in range(E // lg):
            ls = slice(g * lg, (g + 1) * lg)
            a2 = a2_ref[:, ls]
            carry = carry_ref[:, ls]
            racc = ra_ref[:, ls]
            for k in range(CH - 1, -1, -1):
                dt = jnp.broadcast_to(dt_ref[pl.ds(t0 + k, 1), ls], (N, lg))
                gg = jnp.broadcast_to(g_ref[pl.ds(t0 + k, 1), ls], (N, lg))
                cc = jnp.broadcast_to(ct[:, k:k + 1], (N, lg))
                if k == 0 and first:
                    hp = hp_ref[:, ls]
                else:
                    hp = h_ref[pl.ds(pl.multiple_of((t0 + k - 1) * N, N), N), ls]
                sg = cc * gg + carry
                carry = jnp.exp2(dt * a2) * sg
                dterm = carry * hp.astype(F32)
                racc = racc + dterm * dt
                sg_s[k * N:(k + 1) * N, ls] = sg.astype(BF)
                da_s[k * N:(k + 1) * N, ls] = (dterm * a2).astype(BF)
            carry_ref[:, ls] = carry
            ra_ref[:, ls] = racc
        sgc = sg_s[...]
        dg_ref[pl.ds(t0, CH), :] = jnp.dot(bblk_ref[pl.ds(t0, CH), :], sgc, preferred_element_type=F32)
        st_ref[pl.ds(t0, CH), :] = jnp.dot(ones, da_s[...], preferred_element_type=F32) * math.log(2.0)
        wo = lax.dot_general(dxl_ref[pl.ds(t0, CH), :], sgc, nt, preferred_element_type=F32)
        wg_ref[0, pl.ds(c, 1), :] = jnp.sum(jnp.where(mask, wo, 0.0), axis=0, keepdims=True)
        hc = h_ref[pl.ds(pl.multiple_of(t0 * N, CH * N), CH * N), :]
        ro = lax.dot_general(g_ref[pl.ds(t0, CH), :].astype(BF), hc, nt, preferred_element_type=F32)
        rg_ref[0, pl.ds(c, 1), :] = jnp.sum(jnp.where(mask, ro, 0.0), axis=0, keepdims=True)

    def chunk(i, _):
        do_chunk(nc - 1 - i, False)
        return 0
    lax.fori_loop(0, nc - 1, chunk, 0)
    do_chunk(0, True)

def scan_backward(dtm, g, dxl, ctc, bblk, a2, h, tb=128, lg=512):
    T, E = dtm.shape
    nb = T // tb
    r = lambda i: (nb - 1 - i, 0)
    nc = tb // CH
    return pl.pallas_call(
        functools.partial(bwd_kernel, tb=tb, lg=lg),
        grid=(nb,),
        in_specs=[pl.BlockSpec((tb, E), r), pl.BlockSpec((tb, E), r), pl.BlockSpec((tb, E), r),
                  pl.BlockSpec((nc, N, CH), lambda i: (nb - 1 - i, 0, 0)), pl.BlockSpec((tb, CH * N), r),
                  pl.BlockSpec((N, E), lambda i: (0, 0)),
                  pl.BlockSpec((tb * N, E), r),
                  pl.BlockSpec((N, E), lambda i: (jnp.maximum((nb - 1 - i) * tb - 1, 0), 0))],
        out_specs=[pl.BlockSpec((tb, E), r), pl.BlockSpec((tb, E), r),
                   pl.BlockSpec((1, nc, CH * N), lambda i: (nb - 1 - i, 0, 0)), pl.BlockSpec((1, nc, CH * N), lambda i: (nb - 1 - i, 0, 0)),
                   pl.BlockSpec((N, E), lambda i: (0, 0))],
        out_shape=[jax.ShapeDtypeStruct((T, E), F32), jax.ShapeDtypeStruct((T, E), F32),
                   jax.ShapeDtypeStruct((nb, nc, CH * N), F32), jax.ShapeDtypeStruct((nb, nc, CH * N), F32),
                   jax.ShapeDtypeStruct((N, E), F32)],
        scratch_shapes=[pltpu.VMEM((N, E), F32), pltpu.VMEM((CH * N, E), BF), pltpu.VMEM((CH * N, E), BF)],
        compiler_params=pltpu.CompilerParams(vmem_limit_bytes=40 << 20),
        name="scan_bwd",
    )(dtm, g, dxl, ctc, bblk, a2, h, h)

def block_diagonal(m):
    T = m.shape[0]
    eye = jnp.tile(jnp.eye(CH, dtype=F32), (T // CH, 1))
    return (eye[:, :, None] * m[:, None, :]).reshape(T, CH * N).astype(BF)

def chunked(m):
    return jnp.swapaxes(m.reshape(m.shape[0] // CH, CH, N), 1, 2)


def lag(v, j):
    return v if j == 0 else jnp.pad(v, ((j, 0), (0, 0)))[: v.shape[0]]


def lead(v, j):
    return v if j == 0 else jnp.pad(v, ((0, j), (0, 0)))[j:]


def local(
    tokens,
    doc_lengths,
    cotangent,
    norm_gain,
    input_weight,
    filter_weight,
    filter_bias,
    select_weight,
    delta_weight,
    delta_bias,
    decay_log,
    skip_gain,
    output_weight,
    *,
    dp,
):
    core = lax.axis_index("rep")
    rows, length, width = tokens.shape
    inner = input_weight.shape[1] // 2
    half = inner // 2
    rank = delta_weight.shape[1]
    state = decay_log.shape[1]
    taps = filter_weight.shape[1]
    own_e = filter_weight.shape[0]
    own_d = norm_gain.shape[0]
    total = 2 * rows * length

    c0 = rank + 2 * state
    c1 = c0 + state
    c2 = c1 + taps
    column = lambda v: v[:, None]
    gain_col = jnp.pad(norm_gain, (0, own_e - own_d))[:, None]
    first = jnp.concatenate([select_weight, decay_log, filter_weight, column(filter_bias), column(delta_bias), column(skip_gain), gain_col], axis=1)
    second = jnp.concatenate([delta_weight, jnp.zeros((own_e, c2 + 3 - rank), BF), gain_col], axis=1)
    packed = jnp.concatenate([jnp.pad(first, ((0, 0), (0, 128 - c2 - 4))), jnp.pad(second, ((0, 0), (0, 128 - c2 - 4)))], axis=1)
    w_inner, w_gate, w_out, sm, toks, offs, normed, xin, conv_out, act_low, x_out, dt, dtm, dx, y, states = forward(
        doc_lengths, tokens.reshape(rows * length, width), input_weight, output_weight, packed, dp, (taps, rank))
    mine = lax.dynamic_slice(sm, (0, core * half, 0), (2, half, 128))
    select = mine[0, :, :c0]
    delta = mine[1, :, :rank]
    rates = -jnp.exp(mine[0, :, c0:c1].astype(F32)).T
    taps_w = mine[0, :, c1:c2].astype(F32)
    skip = mine[0, :, c2 + 2].astype(F32)
    gain = lax.dynamic_slice(sm, (core, 0, c2 + 3), (1, inner, 1)).reshape(dp, own_e)[:, :own_d].reshape(width).astype(F32)
    offsets = offs[:, :1]
    inner_in = xin[8:]
    a2 = rates * LOG2E
    both = lambda x: lax.all_gather(x, "rep", axis=0, tiled=True)
    cot = both(cotangent.reshape(rows * length, width))
    gate_in = dot(normed, w_gate)
    sig_c = jax.nn.sigmoid(conv_out)
    act = conv_out * sig_c
    delta_low = x_out[:, :rank].astype(BF)
    write = x_out[:, rank : rank + state]
    read = x_out[:, rank + state : rank + 2 * state]
    scanned = y + skip * act
    sig_g = jax.nn.sigmoid(gate_in)
    gate_act = gate_in * sig_g
    gated = (scanned * gate_act).astype(BF)
    branch = dot(gated, w_out, NT)
    branch = lax.psum_scatter(branch, "rep", scatter_dimension=0, tiled=True)
    mixed = (tokens.astype(F32).reshape(rows * length, width) + branch).astype(BF)

    d_out = dot(cot, gated, TN)
    gated_grad = dot(cot, w_out)
    scan_grad = gated_grad * gate_act
    gate_grad = (gated_grad * scanned * (sig_g * (1.0 + gate_in * (1.0 - sig_g)))).astype(BF)
    d_gate = dot(normed, gate_grad, TN)
    skip_grad = jnp.sum(scan_grad * act, axis=0)

    driven_grad, decay_sum, write_grad, read_grad, rates_grad = scan_backward(
        dtm, scan_grad, dx.astype(BF), chunked(read), block_diagonal(write), a2, states
    )
    write_grad = write_grad.reshape(total, state)
    read_grad = read_grad.reshape(total, state)
    decay_grad = (rates_grad * rates).T
    pre_grad = (driven_grad * act + decay_sum) * (1.0 - jnp.exp(-dt))
    dbias_grad = jnp.sum(pre_grad, axis=0)
    pre_low = pre_grad.astype(BF)
    delta_grad = dot(pre_low, delta_low, TN)
    x_grad = jnp.concatenate([dot(pre_low, delta), write_grad, read_grad], axis=1)
    x_grad = lax.psum(x_grad, "rep").astype(BF)
    select_grad = dot(act_low, x_grad, TN)
    act_grad = scan_grad * skip + driven_grad * dt + dot(x_grad, select, NT)
    conv_grad = act_grad * (sig_c * (1.0 + conv_out * (1.0 - sig_c)))
    fbias_grad = jnp.sum(conv_grad, axis=0)
    cols = [None] * taps
    inner_grad = 0.0
    for j in range(taps):
        masked = jnp.where(offsets >= j, conv_grad, 0.0)
        cols[taps - 1 - j] = jnp.sum(masked * lag(inner_in, j), axis=0)
        inner_grad = inner_grad + lead(masked, j) * taps_w[:, taps - 1 - j]
    inner_grad = inner_grad.astype(BF)
    d_inner = dot(normed, inner_grad, TN)
    normed_grad = dot(inner_grad, w_inner, NT) + dot(gate_grad, w_gate, NT)
    normed_grad = lax.psum_scatter(normed_grad, "rep", scatter_dimension=0, tiled=True)
    own_f = tokens.astype(F32).reshape(rows * length, width)
    own_inv = lax.rsqrt(jnp.mean(own_f * own_f, axis=-1, keepdims=True) + EPS)
    own_scaled = own_f * own_inv
    gain_grad = jnp.sum(normed_grad * own_scaled, axis=0)
    scaled_grad = normed_grad * gain
    tokens_grad = cotangent.astype(F32).reshape(rows * length, width) + own_inv * (
        scaled_grad - own_scaled * jnp.mean(scaled_grad * own_scaled, axis=-1, keepdims=True)
    )

    c1 = c0 + rank
    c2 = c1 + state
    c3 = c2 + taps
    def scatter(x):
        return lax.psum_scatter(x.astype(BF), "dp", scatter_dimension=0, tiled=True)

    big = jnp.stack([scatter(d_inner), scatter(d_gate), scatter(d_out)])
    big = lax.all_gather(big, "rep", axis=0)
    in_share = jnp.concatenate([big[0, 0], big[1, 0], big[0, 1], big[1, 1]], axis=1).astype(F32)
    out_share = jnp.concatenate([big[0, 2], big[1, 2]], axis=1).astype(F32)
    small = jnp.concatenate(
        [
            select_grad,
            delta_grad,
            decay_grad,
            jnp.stack(cols, axis=1),
            fbias_grad[:, None],
            dbias_grad[:, None],
            skip_grad[:, None],
        ],
        axis=1,
    )
    small = lax.all_gather(small.astype(BF), "rep", axis=0, tiled=True)
    gain_grad = lax.psum(gain_grad, "rep").reshape(dp, own_d)
    small = jnp.concatenate([small, jnp.pad(gain_grad, ((0, 0), (0, own_e - own_d))).reshape(inner, 1).astype(BF)], axis=1)
    small = jnp.pad(small, ((0, 0), (0, 256 - small.shape[1])))
    small = scatter(small).astype(F32)
    return (
        mixed.reshape(rows, length, width),
        tokens_grad.reshape(rows, length, width),
        small[:own_d, c3 + 3],
        in_share,
        small[:, c2:c3],
        small[:, c3],
        small[:, :c0],
        small[:, c0:c1],
        small[:, c3 + 1],
        small[:, c1:c2],
        small[:, c3 + 2],
        out_share,
    )


def solution(mesh):
    dp_rep = ("dp", "rep")
    one = P("dp")
    two = P("dp", None)
    three = P(dp_rep, None, None)
    return jax.shard_map(
        functools.partial(local, dp=mesh.shape["dp"]),
        mesh=mesh,
        in_specs=(three, P(dp_rep, None), three, one, two, two, one, two, two, one, two, one, two),
        out_specs=(three, three, one, two, two, one, two, two, one, two, one, two),
        check_vma=False,
    )
```

```python
import functools
import math

import jax
import jax.numpy as jnp
from jax import lax
from jax.experimental import pallas as pl
from jax.experimental.pallas import tpu as pltpu
from jax.sharding import PartitionSpec as P

EPS = 1e-05
CH = 16
N = 16
F32 = jnp.float32
BF = jnp.bfloat16
NT = (((1,), (1,)), ((), ()))
TN = (((0,), (0,)), ((), ()))
BIG = 1e30
LOG2E = math.log2(math.e)


def dot(a, b, dims=(((1,), (0,)), ((), ()))):
    return lax.dot_general(a, b, dims, preferred_element_type=F32)


MESH = pl.DeviceIdType.MESH


def plane(dp):
    return 4 if dp == 16 else 0


class Links:
    def __init__(self, dp):
        self.dp = dp
        self.depth = plane(dp)
        self.me = lax.axis_index("dp")
        self.core = lax.axis_index("rep")
        if self.depth:
            self.z, self.y, self.x = self.me // 4, (self.me // 2) % 2, self.me % 2
            self.xn = self.at(self.z, self.y, 1 - self.x)
            self.yn = self.at(self.z, 1 - self.y, self.x)
            self.zs = [self.at(self.up(k), self.y, self.x) for k in range(1, self.depth)]
            self.peers = self.zs + [self.xn, self.yn]
        else:
            self.peers = [lax.rem(self.me + k, dp) for k in range(1, dp)]

    def up(self, k):
        return lax.rem(self.z + k, self.depth)

    def down(self, k):
        return lax.rem(self.z + self.depth - k, self.depth)

    def at(self, z, y, x):
        return (z * 2 + y) * 2 + x

    def barrier(self, sibling=True):
        sem = pltpu.get_barrier_semaphore()
        for peer in self.peers:
            pl.semaphore_signal(sem, inc=1, device_id=(peer, self.core), device_id_type=MESH)
        if sibling:
            pl.semaphore_signal(sem, inc=1, device_id=(self.me, 1 - self.core), device_id_type=MESH)
        pl.semaphore_wait(sem, len(self.peers) + int(sibling))

    def send(self, src, dst, send_sem, recv_sem, chip):
        return pltpu.make_async_remote_copy(
            src_ref=src, dst_ref=dst, send_sem=send_sem, recv_sem=recv_sem,
            device_id=(chip, self.core), device_id_type=MESH,
        )

    def swap(self, src, dst, send_sem, recv_sem):
        return pltpu.make_async_remote_copy(
            src_ref=src, dst_ref=dst, send_sem=send_sem, recv_sem=recv_sem,
            device_id=(self.me, 1 - self.core), device_id_type=MESH,
        )


def copies_of(dp):
    return 19 if plane(dp) else dp - 1


def gather_steps(links, src, dst, ss, rs):
    me = links.me
    rows = src.shape[0]

    def part(b, first=0, count=rows):
        return pl.ds(pl.multiple_of(b * rows + first, count), count)

    if not links.depth:
        cps = [links.send(src, dst.at[part(me)], ss.at[k], rs.at[k], p) for k, p in enumerate(links.peers)]

        def begin():
            for c in cps:
                c.start()
            dst[part(me), :] = src[...]

        def end():
            for c in cps:
                c.wait()

        return [begin] + [lambda: None] * 7 + [end]
    depth, half = links.depth, rows // 2
    z, y, x, xn, yn = links.z, links.y, links.x, links.xn, links.yn
    zc = [links.send(src, dst.at[part(me)], ss.at[k], rs.at[k], p) for k, p in enumerate(links.zs)]
    xc, yc, xf, yf = [], [], [], []
    for k in range(depth):
        b = links.at(links.down(k), y, x)
        s = src if k == 0 else dst.at[part(b)]
        n = 3 + 4 * k
        xc.append(links.send(s, dst.at[part(b)], ss.at[n], rs.at[n], xn))
        yc.append(links.send(s, dst.at[part(b)], ss.at[n + 1], rs.at[n + 1], yn))
        bx = links.at(links.down(k), y, 1 - x)
        by = links.at(links.down(k), 1 - y, x)
        lo = dst.at[part(bx, 0, half)]
        hi = dst.at[part(by, half, half)]
        yf.append(links.send(lo, lo, ss.at[n + 2], rs.at[n + 2], yn))
        xf.append(links.send(hi, hi, ss.at[n + 3], rs.at[n + 3], xn))

    def begin():
        for c in zc:
            c.start()
        xc[0].start()
        yc[0].start()
        dst[part(me), :] = src[...]

    def spread(k):
        def run():
            zc[k - 1].wait_recv()
            xc[k].start()
            yc[k].start()
        return run

    def forward(k):
        def run():
            xc[k].wait_recv()
            yf[k].start()
            yc[k].wait_recv()
            xf[k].start()
        return run

    def end():
        for k in range(depth):
            yf[k].wait_recv()
            xf[k].wait_recv()
        for c in zc + xc + yc + xf + yf:
            c.wait_send()

    return [begin, spread(1), spread(2), spread(3), forward(0), forward(1), forward(2), forward(3), end]


def scatter_scratch(dp, rows, cols):
    if not plane(dp):
        return [pltpu.VMEM((dp - 1, rows, cols), BF)] + [pltpu.VMEM((8, 128), BF)] * 2
    d, h = plane(dp), rows // 2
    return [
        pltpu.VMEM((d, 2, h, cols), BF),
        pltpu.VMEM((d, 2, rows, cols), BF),
        pltpu.VMEM((d - 1, rows, cols), BF),
    ]


def scatter_steps(links, src, out, bufs, ss, rs):
    me = links.me
    rows = src.shape[0] // links.dp

    def part(b, first=0, count=rows):
        return pl.ds(pl.multiple_of(b * rows + first, count), count)

    if not links.depth:
        got = bufs[0]
        cps = [links.send(src.at[part(p)], got.at[k], ss.at[k], rs.at[k], p) for k, p in enumerate(links.peers)]

        def begin():
            for c in cps:
                c.start()

        def end():
            for c in cps:
                c.wait()

            def add(k, total):
                return total + got[k].astype(F32)

            out[...] = lax.fori_loop(0, links.dp - 1, add, src[part(me), :].astype(F32))

        return [begin] + [lambda: None] * 8 + [end]
    halves, come, zcome = bufs
    depth = links.depth
    h = rows // 2
    y, x, xn, yn = links.y, links.x, links.xn, links.yn
    ac, bc, cc = [], [], []
    for k in range(depth):
        zz = links.up(k)
        diag = links.at(zz, 1 - y, 1 - x)
        bx = links.at(zz, y, 1 - x)
        by = links.at(zz, 1 - y, x)
        own = links.at(zz, y, x)
        n = 4 * k
        ac.append((
            links.send(src.at[part(diag, 0, h)], halves.at[k, 0], ss.at[n], rs.at[n], xn),
            links.send(src.at[part(diag, h, h)], halves.at[k, 1], ss.at[n + 1], rs.at[n + 1], yn),
        ))
        bc.append((
            links.send(src.at[part(bx)], come.at[k, 0], ss.at[n + 2], rs.at[n + 2], xn),
            links.send(src.at[part(by)], come.at[k, 1], ss.at[n + 3], rs.at[n + 3], yn),
        ))
        if k:
            n = 4 * depth + k - 1
            cc.append(links.send(src.at[part(own)], zcome.at[k - 1], ss.at[n], rs.at[n], links.zs[k - 1]))

    def add(where, more):
        src[where, :] = (src[where, :].astype(F32) + more.astype(F32)).astype(BF)

    def begin():
        for k in (1, 2, 3, 0):
            ac[k][0].start()
            ac[k][1].start()

    def middle(k):
        def run():
            zz = links.up(k)
            ac[k][0].wait_recv()
            add(part(links.at(zz, 1 - y, x), 0, h), halves[k, 0])
            bc[k][1].start()
            ac[k][1].wait_recv()
            add(part(links.at(zz, y, 1 - x), h, h), halves[k, 1])
            bc[k][0].start()
        return run

    def along(k):
        def run():
            bc[k][0].wait_recv()
            bc[k][1].wait_recv()
            own = part(links.at(links.up(k), y, x))
            total = src[own, :].astype(F32) + come[k, 0].astype(F32) + come[k, 1].astype(F32)
            if k:
                src[own, :] = total.astype(BF)
                cc[k - 1].start()
            else:
                out[...] = total
        return run

    def end():
        for k in range(depth - 1):
            cc[k].wait_recv()
            out[...] += zcome[k].astype(F32)
        for k in range(depth):
            for c in ac[k] + bc[k]:
                c.wait_send()
        for c in cc:
            c.wait_send()

    return [begin, middle(1), middle(2), along(1), middle(3), along(2), middle(0), along(3), along(0), end]


def sigmoid(v):
    return 0.5 * jnp.tanh(0.5 * v) + 0.5


def softplus(v):
    u = jnp.exp(-jnp.abs(v))
    return jnp.maximum(v, 0.0) + jnp.where(u < 1e-3, u * (1.0 - 0.5 * u), jnp.log(1.0 + u))


def slope(v, s):
    return s * (1.0 + v * (1.0 - s))


def block_mask(rows=CH):
    r = lax.broadcasted_iota(jnp.int32, (rows, CH * N), 0)
    c = lax.broadcasted_iota(jnp.int32, (rows, CH * N), 1)
    return (c // N) == (r % CH)


def pick(first):
    r = lax.broadcasted_iota(jnp.int32, (128, CH * N), 0)
    c = lax.broadcasted_iota(jnp.int32, (128, CH * N), 1)
    return jnp.where(r - first == c % N, 1.0, 0.0).astype(BF)


def place(first):
    r = lax.broadcasted_iota(jnp.int32, (CH * N, 128), 0)
    c = lax.broadcasted_iota(jnp.int32, (CH * N, 128), 1)
    return jnp.where(c - first == r % N, 1.0, 0.0).astype(BF)


def eighths(v):
    return jnp.sum(v.reshape(v.shape[0] // 8, 8, v.shape[1]), axis=0)


def layer_kernel(*refs, dp, dims, names):
    R = dict(zip(names, refs))
    lens, tok, cot, w_in, w_o, packed = (R[k] for k in ("lens", "tok", "cot", "w_in", "w_o", "packed"))
    wi, wg, wo, sm, toks, cots, normed = (R[k] for k in ("wi", "wg", "wo", "sm", "toks", "cots", "normed"))
    offs, xin, conv, actl, dt, dtm, dx, y = (R[k] for k in ("offs", "xin", "conv", "actl", "dt", "dtm", "dx", "y"))
    ggr, xo, xr, xg, hs, hbuf = (R[k] for k in ("ggr", "xo", "xr", "xg", "hs", "hbuf"))
    par, btc, ctc, cblk, bblk, a2, st, racc = (R[k] for k in ("par", "btc", "ctc", "cblk", "bblk", "a2", "st", "racc"))
    gtmp, qtmp, sgs, das, wgs, rgs, accs = (R[k] for k in ("gtmp", "qtmp", "sgs", "das", "wgs", "rgs", "accs"))
    d_out, d_gate, msend, mrecv, sw_s, sw_r, hsem, lsem = (
        R[k] for k in ("d_out", "d_gate", "msend", "mrecv", "sw_s", "sw_r", "hsem", "lsem"))
    taps, rank = dims
    links = Links(dp)
    core, me = links.core, links.me
    rows, width = tok.shape
    half = wi.shape[1]
    total = 2 * rows
    own_d = w_in.shape[0]
    own_e = packed.shape[0]
    inner = 2 * half
    lanes = half // 128
    c1 = rank + 2 * N
    r_taps, r_fb, r_db, r_sk, gcol = (c1 + N + k for k in (0, taps, taps + 1, taps + 2, taps + 3))
    gated = toks

    def cut(ref, start):
        return ref.at[:, pl.ds(pl.multiple_of(start + core * half, 128), half)]

    def lane(b, n=128):
        return slice(b * n, (b + 1) * n)

    def tiles(n, body, size):
        def run(i, _):
            body(pl.multiple_of(i * size, size))
            return 0
        lax.fori_loop(0, n // size, run, 0)

    links.barrier()
    mine = pl.ds(pl.multiple_of(core * rows, rows), rows)
    other = pl.ds(pl.multiple_of((1 - core) * rows, rows), rows)
    t_idx = lax.broadcasted_iota(jnp.int32, (rows, 128), 0)
    begin = jnp.zeros((rows, 128), jnp.int32)
    start = lens[0, 0]
    for k in range(1, lens.shape[1]):
        begin = jnp.where(t_idx >= start, start, begin)
        start = start + lens[0, k]
    offs[mine, :] = (t_idx - begin).astype(F32)
    offs[pl.ds(total, 8), :] = jnp.zeros((8, 128), F32)
    t_swap = links.swap(tok, toks.at[mine], sw_s.at[0], sw_r.at[0])
    o_swap = links.swap(offs.at[mine], offs.at[mine], sw_s.at[1], sw_r.at[1])
    c_swap = links.swap(cot, cots.at[mine], sw_s.at[2], sw_r.at[2])
    c_copy = pltpu.make_async_copy(cot, cots.at[mine], lsem.at[0])
    g_i = gather_steps(links, cut(w_in, 0), wi, R["gi_s"], R["gi_r"])
    pk = packed.at[:, pl.ds(pl.multiple_of(core * 128, 128), 128)]
    g_s = gather_steps(links, pk, sm.at[core], R["gs_s"], R["gs_r"])
    g_g = gather_steps(links, cut(w_in, inner), wg, R["gg_s"], R["gg_r"])
    g_o = gather_steps(links, cut(w_o, 0), wo, R["go_s"], R["go_r"])
    g_i[0]()
    g_s[0]()
    t_swap.start()
    o_swap.start()
    c_swap.start()
    c_copy.start()
    toks[mine, :] = tok[...]
    for k in range(1, len(g_i) - 1):
        g_i[k]()
        g_s[k]()
        if k == 3:
            g_g[0]()
    g_s[-1]()
    theirs = pl.ds(pl.multiple_of((1 - core) * half, half), half)
    s_swap = links.swap(sm.at[core, theirs], sm.at[core, theirs], sw_s.at[3], sw_r.at[3])
    s_swap.start()
    g_i[-1]()
    t_swap.wait()
    o_swap.wait()
    g_o[0]()

    rowed = []
    for b in range(2 * lanes):
        rowed.append(sm[core, pl.ds(b * 128, 128), :].astype(F32).T[gcol:gcol + 1, :])
    flat = jnp.concatenate(rowed, axis=1)
    gain = jnp.concatenate([flat[:, i * own_e:i * own_e + own_d] for i in range(dp)], axis=1)

    def norm(t0):
        r = pl.ds(t0, 16)
        v = toks[r, :].astype(F32)
        inv = lax.rsqrt(jnp.mean(v * v, axis=-1, keepdims=True) + EPS)
        normed[r, :] = (v * inv * gain).astype(BF)

    tiles(total, norm, 16)
    xin[0:8, :] = jnp.zeros((8, half), F32)

    def in_proj(j):
        xin[pl.ds(8, total), pl.ds(j, 256)] = dot(normed[...], wi[:, pl.ds(j, 256)])

    tiles(half, in_proj, 256)
    s_swap.wait()
    own = pl.multiple_of(core * half, half)
    select = sm.at[0, pl.ds(own, half), :]
    delta = sm.at[1, pl.ds(own, half), :]
    for b in range(lanes):
        par[:, lane(b)] = sm[0, pl.ds(own + b * 128, 128), :].astype(F32).T
    a2[...] = -jnp.exp(par[c1:c1 + N, :]) * LOG2E

    def conv_tile(t0):
        o = offs[pl.ds(t0, 64), :]
        for b in range(lanes):
            c = lane(b)
            v = xin[pl.ds(t0, 72), c]
            acc = par[r_fb:r_fb + 1, c]
            for j in range(taps):
                s = v[8 - j:72 - j]
                if j:
                    s = jnp.where(o >= float(j), s, 0.0)
                acc = acc + par[r_taps + taps - 1 - j:r_taps + taps - j, c] * s
            conv[pl.ds(t0, 64), c] = acc
            actl[pl.ds(t0, 64), c] = (acc * sigmoid(acc)).astype(BF)

    tiles(total, conv_tile, 64)
    xo[...] = dot(actl[...], select[...])
    x_swap = links.swap(xo, xr, sw_s.at[4], sw_r.at[4])
    x_swap.start()
    x_swap.wait()
    xo[...] += xr[...]

    def dt_tile(t0):
        o = offs[pl.ds(t0, 64), :]
        low = xo[pl.ds(t0, 64), :].astype(BF)[:, :rank]
        for b in range(half // 256):
            pre2 = dot(low, delta[lane(b, 256), :][:, :rank], NT)
            for q in range(2):
                c = lane(2 * b + q)
                s = softplus(pre2[:, lane(q)] + par[r_db:r_db + 1, c])
                dt[pl.ds(t0, 64), c] = s
                dtm[pl.ds(t0, 64), c] = jnp.where(o > 0.0, s, BIG)
                cv = conv[pl.ds(t0, 64), c]
                dx[pl.ds(t0, 64), c] = s * (cv * sigmoid(cv))

    tiles(total, dt_tile, 64)
    per = 128 // CH

    def cols_tile(i, _):
        t0 = pl.multiple_of(i * 128, 128)
        x = xo[pl.ds(t0, 128), :]
        t = x.T
        for q in range(per):
            btc[i * per + q] = t[rank:rank + N, q * CH:(q + 1) * CH]
            ctc[i * per + q] = t[rank + N:rank + 2 * N, q * CH:(q + 1) * CH]
        m = block_mask(128)
        cblk[pl.ds(t0, 128), :] = jnp.where(m, dot(x.astype(BF), pick(rank + N)), 0.0).astype(BF)
        bblk[pl.ds(t0, 128), :] = jnp.where(m, dot(x.astype(BF), pick(rank)), 0.0).astype(BF)
        return 0

    lax.fori_loop(0, total // 128, cols_tile, 0)

    steps = []
    for a, b in zip(g_g[1:], g_o[1:]):
        steps += [a, b]
    hp = hbuf.shape[1] // N
    hq = hp // CH
    n_blk = total // hp
    st[...] = jnp.zeros_like(st)
    lg = min(512, half)

    def kept(blk):
        return hs.at[pl.ds(pl.multiple_of(blk * hp * N, hp * N), hp * N)]

    def write_out(blk, slot):
        return pltpu.make_async_copy(hbuf.at[slot], kept(blk), hsem.at[slot])

    def f_block(blk, _):
        slot = lax.rem(blk, 2)

        @pl.when(blk >= 2)
        def _():
            write_out(blk - 2, slot).wait()

        def chunk(q, _):
            c = blk * hq + q
            t0 = pl.multiple_of(c * CH, CH)
            for k, s in enumerate(steps):
                pl.when(c == 2 + 2 * k)(s)
            bt = btc[c]
            for g in range(half // lg):
                ls = lane(g, lg)
                a = a2[:, ls]
                h = st[:, ls]
                for k in range(CH):
                    d = jnp.broadcast_to(dtm[pl.ds(t0 + k, 1), ls], (N, lg))
                    v = jnp.broadcast_to(dx[pl.ds(t0 + k, 1), ls], (N, lg))
                    w = jnp.broadcast_to(bt[:, k:k + 1], (N, lg))
                    h = jnp.exp2(d * a) * h + w * v
                    hbuf[slot, pl.ds(pl.multiple_of((q * CH + k) * N, N), N), ls] = h.astype(BF)
                st[:, ls] = h
            hc = hbuf[slot, pl.ds(pl.multiple_of(q * CH * N, CH * N), CH * N), :]
            y[pl.ds(t0, CH), :] = dot(cblk[pl.ds(t0, CH), :], hc)
            return 0

        lax.fori_loop(0, hq, chunk, 0)

        @pl.when(blk < n_blk - 2)
        def _():
            write_out(blk, slot).start()

        return 0

    lax.fori_loop(0, n_blk, f_block, 0)
    c_copy.wait()
    c_swap.wait()

    accs[...] = jnp.zeros_like(accs)

    def gate_cols(j):
        cj = pl.ds(j, 256)
        gtmp[...] = dot(normed[...], wg[:, cj])
        qtmp[...] = dot(cots[...], wo[:, cj])

        def gate_tile(t0):
            r = pl.ds(t0, 64)
            for q in range(2):
                c = pl.ds(pl.multiple_of(j + q * 128, 128), 128)
                cv = conv[r, c]
                act = cv * sigmoid(cv)
                scanned = y[r, c] + par[r_sk:r_sk + 1, c] * act
                g = gtmp[r, lane(q)]
                sg = sigmoid(g)
                ga = g * sg
                gated[r, c] = (scanned * ga).astype(BF)
                gg = qtmp[r, lane(q)]
                G = gg * ga
                y[r, c] = G
                ggr[r, c] = (gg * scanned * slope(g, sg)).astype(BF)
                accs[0, :, c] += eighths(G * act)

        tiles(total, gate_tile, 64)

    tiles(half, gate_cols, 256)

    def outer(left, right, out):
        def body(i):
            for b in range(half // 512):
                out[pl.ds(i, 256), lane(b, 512)] = dot(left[:, pl.ds(i, 256)], right[:, lane(b, 512)], TN).astype(BF)
        tiles(width, body, 256)

    s_o = scatter_steps(links, d_out, R["red_o"], R["so_b"], R["so_s"], R["so_r"])
    s_g = scatter_steps(links, d_gate, R["red_g"], R["sg_b"], R["sg_s"], R["sg_r"])
    outer(cots, gated, d_out)
    s_o[0]()
    outer(normed, ggr, d_gate)
    s_g[0]()

    def project(which, right, out):
        def body(j):
            out(j, dot(gated[which, :], right[pl.ds(j, 256), :], NT))
        tiles(width, body, 256)

    def put_send(j, v):
        msend[:, pl.ds(j, 256)] = v.astype(BF)

    project(other, wo, put_send)
    m_swap = links.swap(msend, mrecv, sw_s.at[5], sw_r.at[5])
    m_swap.start()

    def put_own(j, v):
        dt0 = tok[:, pl.ds(j, 256)].astype(F32)
        R["mixed_f"][:, pl.ds(j, 256)] = dt0 + v

    project(mine, wo, put_own)
    m_swap.wait()

    def mix_tile(t0):
        r = pl.ds(t0, 16)
        R["mixed"][r, :] = (R["mixed_f"][r, :] + mrecv[r, :].astype(F32)).astype(BF)

    tiles(rows, mix_tile, 16)

    steps_b = s_o[1:9] + s_g[1:3] + [s_o[9]] + [s_g[3], s_g[4], s_g[5], s_g[6], s_g[7], s_g[8], s_g[9]]
    n_chunks = total // CH
    st[...] = jnp.zeros_like(st)
    racc[...] = jnp.zeros_like(racc)

    def read_back(blk, slot):
        return pltpu.make_async_copy(kept(blk), hbuf.at[slot], hsem.at[slot])

    def b_block(i, _):
        blk = n_blk - 1 - i
        slot = lax.rem(blk, 2)

        def chunk(p, _):
            q = hq - 1 - p
            c = blk * hq + q
            t0 = pl.multiple_of(c * CH, CH)
            done = i * hq + p
            for k, s in enumerate(steps_b):
                pl.when(done == 2 + 2 * k)(s)

            @pl.when((q == 0) & (blk >= 1) & (blk <= n_blk - 2))
            def _():
                read_back(blk - 1, 1 - slot).wait()

            before = jnp.where(q == 0, 1 - slot, slot)
            last = pl.multiple_of(jnp.where(q == 0, hp - 1, q * CH - 1) * N, N)
            ct = ctc[c]
            for g in range(half // lg):
                ls = lane(g, lg)
                a = a2[:, ls]
                carry = st[:, ls]
                ra = racc[:, ls]
                for k in range(CH - 1, -1, -1):
                    d = jnp.broadcast_to(dtm[pl.ds(t0 + k, 1), ls], (N, lg))
                    gg = jnp.broadcast_to(y[pl.ds(t0 + k, 1), ls], (N, lg))
                    cc = jnp.broadcast_to(ct[:, k:k + 1], (N, lg))
                    if k:
                        h = hbuf[slot, pl.ds(pl.multiple_of((q * CH + k - 1) * N, N), N), ls]
                    else:
                        h = hbuf[before, pl.ds(last, N), ls]
                    sg = cc * gg + carry
                    carry = jnp.exp2(d * a) * sg
                    term = carry * h.astype(F32)
                    ra = ra + term * d
                    sgs[k * N:(k + 1) * N, ls] = sg.astype(BF)
                    das[k * N:(k + 1) * N, ls] = (term * a).astype(BF)
                st[:, ls] = carry
                racc[:, ls] = ra
            m = block_mask()
            r = pl.ds(t0, CH)
            sgc = sgs[...]
            wout = dot(dx[r, :].astype(BF), sgc, NT)
            wgs[pl.ds(c, 1), :] = jnp.sum(jnp.where(m, wout, 0.0), axis=0, keepdims=True)
            hc = hbuf[slot, pl.ds(pl.multiple_of(q * CH * N, CH * N), CH * N), :]
            rout = dot(y[r, :].astype(BF), hc, NT)
            rgs[pl.ds(c, 1), :] = jnp.sum(jnp.where(m, rout, 0.0), axis=0, keepdims=True)
            dx[r, :] = dot(bblk[r, :], sgc)
            dtm[r, :] = dot(m.astype(BF), das[...])
            return 0

        lax.fori_loop(0, hq, chunk, 0)

        @pl.when(blk >= 2)
        def _():
            read_back(blk - 2, slot).start()

        return 0

    lax.fori_loop(0, n_blk, b_block, 0)
    dg, low_b = dx, gated

    ln2 = math.log(2.0)

    def pre_tile(t0):
        r = pl.ds(t0, 64)
        for b in range(lanes):
            c = lane(b)
            cv = conv[r, c]
            act = cv * sigmoid(cv)
            v = (dg[r, c] * act + dtm[r, c] * ln2) * (1.0 - jnp.exp(-dt[r, c]))
            low_b[r, c] = v.astype(BF)
            accs[1, :, c] += eighths(v)

    tiles(total, pre_tile, 64)

    def xg_tile(i, _):
        t0 = pl.multiple_of(i * 128, 128)
        r = pl.ds(t0, 128)
        m = block_mask(128)
        col = lax.broadcasted_iota(jnp.int32, (128, 128), 1)
        sums = jnp.where(col < rank, dot(low_b[r, :], delta[...]), 0.0)
        for ref, first in ((wgs, rank), (rgs, rank + N)):
            v = ref[pl.ds(pl.multiple_of(i * per, per), per), :]
            v = jnp.broadcast_to(v[:, None, :], (per, CH, CH * N)).reshape(128, CH * N)
            v = jnp.where(m, v, 0.0)
            hi = v.astype(BF)
            lo = (v - hi.astype(F32)).astype(BF)
            p = place(first)
            sums = sums + dot(hi, p) + dot(lo, p)
        xg[r, :] = sums
        return 0

    lax.fori_loop(0, total // 128, xg_tile, 0)
    g_swap = links.swap(xg, xr, sw_s.at[6], sw_r.at[6])
    g_swap.start()
    sgrad = R["sgrad"]
    xob = xo[...].astype(BF)
    for b in range(half // 256):
        sgrad[1, lane(b, 256), :] = dot(low_b[:, lane(b, 256)], xob, TN)
    g_swap.wait()
    xg[...] = xg[...] + xr[...]
    xgb = xg[...].astype(BF)
    for b in range(half // 256):
        sgrad[0, lane(b, 256), :] = dot(actl[:, lane(b, 256)], xgb, TN)

    def cg_tile(t0):
        r = pl.ds(t0, 64)
        low = xg[r, :].astype(BF)
        for b in range(half // 256):
            back = dot(low, select[lane(b, 256), :], NT)
            for q in range(2):
                c = lane(2 * b + q)
                ag = y[r, c] * par[r_sk:r_sk + 1, c] + dg[r, c] * dt[r, c] + back[:, lane(q)]
                cv = conv[r, c]
                v = ag * slope(cv, sigmoid(cv))
                y[r, c] = v
                accs[2, :, c] += eighths(v)

    tiles(total, cg_tile, 64)
    y[pl.ds(total, 8), :] = jnp.zeros((8, half), F32)
    ig = gated

    def ig_tile(t0):
        o = offs[pl.ds(t0, 72), :]
        for b in range(lanes):
            c = lane(b)
            v = y[pl.ds(t0, 72), c]
            x = xin[pl.ds(t0, 72), c]
            acc = jnp.zeros((64, 128), F32)
            for j in range(taps):
                mv = jnp.where(o >= float(j), v, 0.0) if j else v
                accs[3 + taps - 1 - j, :, c] += eighths(mv[0:64] * x[8 - j:72 - j])
                acc = acc + mv[j:64 + j] * par[r_taps + taps - 1 - j:r_taps + taps - j, c]
            ig[pl.ds(t0, 64), c] = acc.astype(BF)

    tiles(total, ig_tile, 64)

    d_in = wo
    s_i = scatter_steps(links, d_in, R["red_i"], R["so_b"], R["si_s"], R["si_r"])
    outer(normed, ig, d_in)
    s_i[0]()

    def back_project(which, out):
        def body(j):
            c = pl.ds(j, 256)
            out(j, dot(ig[which, :], wi[c, :], NT) + dot(ggr[which, :], wg[c, :], NT))
        tiles(width, body, 256)

    back_project(other, put_send)
    n_swap = links.swap(msend, mrecv, sw_s.at[7], sw_r.at[7])
    n_swap.start()
    s_i[1]()
    s_i[2]()
    ng = R["mixed_f"]

    def put_ng(j, v):
        ng[:, pl.ds(j, 256)] = v

    back_project(mine, put_ng)

    gp = par
    vecs = jnp.concatenate(
        [racc[...] * a2[...] * ln2]
        + [jnp.sum(accs[3 + k], axis=0, keepdims=True) for k in range(taps)]
        + [jnp.sum(accs[2], axis=0, keepdims=True), jnp.sum(accs[1], axis=0, keepdims=True),
           jnp.sum(accs[0], axis=0, keepdims=True)], axis=0)
    gp[...] = jnp.zeros_like(gp)
    gp[c1:c1 + N + taps + 3, :] = vecs
    small = R["small"]
    for b in range(lanes):
        col = lax.broadcasted_iota(jnp.int32, (128, 128), 1)
        first = jnp.where(col < c1, sgrad[0, lane(b), :], gp[:, lane(b)].T)
        second = jnp.where(col < rank, sgrad[1, lane(b), :], 0.0)
        ours = jnp.where(core == 0, first, second)
        away = jnp.where(core == 0, second, first)
        small[pl.ds(own + b * 128, 128), :] = ours.astype(BF)
        R["away"][lane(b), :] = away.astype(BF)
    a_swap = links.swap(R["away"], small.at[pl.ds(own, half), :], sw_s.at[8], sw_r.at[8])
    a_swap.start()
    s_i[3]()
    s_i[4]()
    n_swap.wait()
    gacc = R["gacc"]
    gacc[...] = jnp.zeros_like(gacc)

    def tok_tile(t0):
        r = pl.ds(t0, 16)
        v = tok[r, :].astype(F32)
        inv = lax.rsqrt(jnp.mean(v * v, axis=-1, keepdims=True) + EPS)
        sc = v * inv
        n = ng[r, :] + mrecv[r, :].astype(F32)
        p = n * sc
        gacc[...] += p[0:8] + p[8:16]
        sg = n * gain
        ng[r, :] = cots[pl.ds(pl.multiple_of(core * rows + t0, 16), 16), :].astype(F32) + inv * (
            sg - sc * jnp.mean(sg * sc, axis=-1, keepdims=True))

    tiles(rows, tok_tile, 16)
    t_copy = pltpu.make_async_copy(ng, R["tgrad"], lsem.at[1])
    t_copy.start()
    s_i[5]()
    a_swap.wait()
    grow = jnp.sum(gacc[...], axis=0, keepdims=True)
    zero = jnp.zeros((1, own_e - own_d), F32)
    spread = []
    for i in range(dp):
        spread += [grow[:, i * own_d:(i + 1) * own_d], zero]
    spread = jnp.concatenate(spread, axis=1)
    eight = lax.broadcasted_iota(jnp.int32, (8, 128), 0)
    lane8 = lax.broadcasted_iota(jnp.int32, (8, 128), 1)
    unit = jnp.where((eight == 0) & (lane8 == gcol), 1.0, 0.0).astype(BF)
    for b in range(2 * lanes):
        rowb = jnp.broadcast_to(spread[:, lane(b)], (8, 128)).astype(BF)
        small[lane(b), :] = small[lane(b), :] + dot(rowb, unit, TN).astype(BF)
    s_s = scatter_steps(links, small, R["red_s"].at[core], R["ss_b"], R["ss_s"], R["ss_r"])
    s_s[0]()
    s_i[6]()
    s_s[1]()
    s_s[2]()
    s_i[7]()
    s_s[3]()
    s_s[4]()
    s_s[5]()
    s_s[6]()
    s_i[8]()
    s_s[7]()
    s_s[8]()
    s_s[9]()
    fs = links.swap(R["red_s"].at[core], R["red_s"].at[core], sw_s.at[9], sw_r.at[9])
    fs.start()
    s_i[9]()
    t_copy.wait()

    fins = [links.swap(R[k], R[k + "2"], sw_s.at[10 + n], sw_r.at[10 + n])
            for n, k in enumerate(("red_i", "red_g", "red_o"))]
    for f in fins:
        f.start()
    fs.wait()
    red_s = R["red_s"]
    one, two = red_s[0], red_s[1]
    R["o_select"][...] = one[:, :c1]
    R["o_delta"][...] = two[:, :rank]
    R["o_decay"][...] = one[:, c1:c1 + N]
    R["o_filter"][...] = one[:, r_taps:r_taps + taps]
    turned = one.T
    R["o_fb"][...] = turned[r_fb:r_fb + 1, :]
    R["o_db"][...] = turned[r_db:r_db + 1, :]
    R["o_skip"][...] = turned[r_sk:r_sk + 1, :]
    R["o_gain"][...] = (turned[gcol:gcol + 1, :] + two.T[gcol:gcol + 1, :])[:, :own_d]
    for f in fins:
        f.wait()
    for first, k, out in ((0, "red_i", "o_in"), (inner, "red_g", "o_in"), (0, "red_o", "o_out")):
        R[out][:, pl.ds(pl.multiple_of(first + core * half, 128), half)] = R[k][...]
        R[out][:, pl.ds(pl.multiple_of(first + (1 - core) * half, 128), half)] = R[k + "2"][...]


def layer(lens, tok, cot, w_in, w_o, packed, dp, dims):
    rows, width = tok.shape
    half = w_o.shape[1] // 2
    inner = 2 * half
    total = 2 * rows
    taps, rank = dims
    own_d, own_e = w_in.shape[0], packed.shape[0]
    n = copies_of(dp)
    sd = jax.ShapeDtypeStruct
    vm = pl.BlockSpec(memory_space=pltpu.VMEM)
    hbm = pl.BlockSpec(memory_space=pl.ANY)
    dma = pltpu.SemaphoreType.DMA
    V = pltpu.VMEM
    outs = {
        "mixed": sd((rows, width), BF), "tgrad": sd((rows, width), F32), "o_gain": sd((1, own_d), F32),
        "o_in": sd((own_d, 2 * inner), F32), "o_filter": sd((own_e, taps), F32), "o_fb": sd((1, own_e), F32),
        "o_select": sd((own_e, rank + 2 * N), F32), "o_delta": sd((own_e, rank), F32), "o_db": sd((1, own_e), F32),
        "o_decay": sd((own_e, N), F32), "o_skip": sd((1, own_e), F32), "o_out": sd((own_d, inner), F32),
        "hs": sd((total * N, half), BF),
    }
    f2 = V((total, half), F32)
    scratch = {
        "wi": V((width, half), BF), "wg": V((width, half), BF), "wo": V((width, half), BF), "sm": V((2, inner, 128), BF),
        "toks": V((total, width), BF), "cots": V((total, width), BF), "normed": V((total, width), BF),
        "offs": V((total + 8, 128), F32), "xin": V((total + 8, half), F32), "conv": f2, "actl": V((total, half), BF),
        "dt": f2, "dtm": f2, "dx": f2, "y": V((total + 8, half), F32), "ggr": V((total, half), BF),
        "xo": V((total, 128), F32), "xr": V((total, 128), F32), "xg": V((total, 128), F32),
        "hbuf": V((2, 64 * N, half), BF), "par": V((128, half), F32),
        "btc": V((total // CH, N, CH), F32), "ctc": V((total // CH, N, CH), F32),
        "cblk": V((total, CH * N), BF), "bblk": V((total, CH * N), BF),
        "a2": V((N, half), F32), "st": V((N, half), F32), "racc": V((N, half), F32),
        "gtmp": V((total, 256), F32), "qtmp": V((total, 256), F32),
        "sgs": V((CH * N, half), BF), "das": V((CH * N, half), BF),
        "wgs": V((total // CH, CH * N), F32), "rgs": V((total // CH, CH * N), F32),
        "accs": V((3 + taps, 8, half), F32), "d_out": V((width, half), BF), "d_gate": V((width, half), BF),
        "msend": V((rows, width), BF), "mrecv": V((rows, width), BF), "mixed_f": V((rows, width), F32),
        "sgrad": V((2, half, 128), F32), "small": V((inner, 128), BF), "away": V((half, 128), BF), "gacc": V((8, width), F32),
        "red_s": V((2, own_e, 128), F32),
        "so_b": scatter_scratch(dp, own_d, half), "sg_b": scatter_scratch(dp, own_d, half),
        "ss_b": scatter_scratch(dp, own_e, 128),
        "sw_s": dma((13,)), "sw_r": dma((13,)), "hsem": dma((2,)), "lsem": dma((2,)),
    }
    for k in ("i", "g", "o"):
        scratch["red_" + k] = V((own_d, half), F32)
        scratch["red_" + k + "2"] = V((own_d, half), F32)
    for k in ("gi", "gs", "gg", "go", "si", "sg", "so", "ss"):
        scratch[k + "_s"] = dma((n,))
        scratch[k + "_r"] = dma((n,))
    inputs = {"lens": lens, "tok": tok, "cot": cot, "w_in": w_in, "w_o": w_o, "packed": packed}
    names = list(inputs) + list(outs) + list(scratch)
    res = pl.pallas_call(
        functools.partial(layer_kernel, dp=dp, dims=dims, names=names),
        out_shape=list(outs.values()),
        in_specs=[pl.BlockSpec(memory_space=pltpu.SMEM), vm, hbm, vm, vm, vm],
        out_specs=[hbm if k in ("tgrad", "hs") else vm for k in outs],
        scratch_shapes=list(scratch.values()),
        compiler_params=pltpu.CompilerParams(collective_id=0, has_side_effects=True, vmem_limit_bytes=127 << 19),
        name="layer",
    )(*inputs.values())
    return dict(zip(outs, res))


def local(
    tokens,
    doc_lengths,
    cotangent,
    norm_gain,
    input_weight,
    filter_weight,
    filter_bias,
    select_weight,
    delta_weight,
    delta_bias,
    decay_log,
    skip_gain,
    output_weight,
    *,
    dp,
):
    rows, length, width = tokens.shape
    rank = delta_weight.shape[1]
    taps = filter_weight.shape[1]
    own_e = filter_weight.shape[0]
    own_d = norm_gain.shape[0]
    used = rank + 3 * N + taps + 4

    def column(v):
        return v[:, None]

    gain_col = column(jnp.pad(norm_gain, (0, own_e - own_d)))
    packed = jnp.concatenate(
        [
            select_weight, decay_log, filter_weight, column(filter_bias), column(delta_bias), column(skip_gain), gain_col,
            jnp.zeros((own_e, 128 - used), BF),
            delta_weight, jnp.zeros((own_e, used - 1 - rank), BF), gain_col, jnp.zeros((own_e, 128 - used), BF),
        ],
        axis=1,
    )
    r = layer(
        doc_lengths, tokens.reshape(rows * length, width), cotangent.reshape(rows * length, width),
        input_weight, output_weight, packed, dp, (taps, rank),
    )
    return (
        r["mixed"].reshape(rows, length, width),
        r["tgrad"].reshape(rows, length, width),
        r["o_gain"].reshape(own_d),
        r["o_in"],
        r["o_filter"],
        r["o_fb"].reshape(own_e),
        r["o_select"],
        r["o_delta"],
        r["o_db"].reshape(own_e),
        r["o_decay"],
        r["o_skip"].reshape(own_e),
        r["o_out"],
    )


def solution(mesh):
    dp_rep = ("dp", "rep")
    one = P("dp")
    two = P("dp", None)
    three = P(dp_rep, None, None)
    return jax.shard_map(
        functools.partial(local, dp=mesh.shape["dp"]),
        mesh=mesh,
        in_specs=(three, P(dp_rep, None), three, one, two, two, one, two, two, one, two, one, two),
        out_specs=(three, three, one, two, two, one, two, two, one, two, one, two),
        check_vma=False,
    )
```

```python
import functools
import math

import jax
import jax.numpy as jnp
from jax import lax
from jax.experimental import pallas as pl
from jax.experimental.pallas import tpu as pltpu
from jax.sharding import PartitionSpec as P

EPS = 1e-05
CH = 16
N = 16
F32 = jnp.float32
BF = jnp.bfloat16
NT = (((1,), (1,)), ((), ()))
TN = (((0,), (0,)), ((), ()))
BIG = 1e30
LOG2E = math.log2(math.e)


def dot(a, b, dims=(((1,), (0,)), ((), ()))):
    return lax.dot_general(a, b, dims, preferred_element_type=F32)


MESH = pl.DeviceIdType.MESH


def plane(dp):
    return 4 if dp == 16 else 0


class Links:
    def __init__(self, dp):
        self.dp = dp
        self.depth = plane(dp)
        self.me = lax.axis_index("dp")
        self.core = lax.axis_index("rep")
        if self.depth:
            self.z, self.y, self.x = self.me // 4, (self.me // 2) % 2, self.me % 2
            self.xn = self.at(self.z, self.y, 1 - self.x)
            self.yn = self.at(self.z, 1 - self.y, self.x)
            self.zs = [self.at(self.up(k), self.y, self.x) for k in range(1, self.depth)]
            self.peers = self.zs + [self.xn, self.yn]
        else:
            self.peers = [lax.rem(self.me + k, dp) for k in range(1, dp)]

    def up(self, k):
        return lax.rem(self.z + k, self.depth)

    def down(self, k):
        return lax.rem(self.z + self.depth - k, self.depth)

    def at(self, z, y, x):
        return (z * 2 + y) * 2 + x

    def barrier(self, sibling=True):
        sem = pltpu.get_barrier_semaphore()
        for peer in self.peers:
            pl.semaphore_signal(sem, inc=1, device_id=(peer, self.core), device_id_type=MESH)
        if sibling:
            pl.semaphore_signal(sem, inc=1, device_id=(self.me, 1 - self.core), device_id_type=MESH)
        pl.semaphore_wait(sem, len(self.peers) + int(sibling))

    def send(self, src, dst, send_sem, recv_sem, chip):
        return pltpu.make_async_remote_copy(
            src_ref=src, dst_ref=dst, send_sem=send_sem, recv_sem=recv_sem,
            device_id=(chip, self.core), device_id_type=MESH,
        )

    def swap(self, src, dst, send_sem, recv_sem):
        return pltpu.make_async_remote_copy(
            src_ref=src, dst_ref=dst, send_sem=send_sem, recv_sem=recv_sem,
            device_id=(self.me, 1 - self.core), device_id_type=MESH,
        )


def copies_of(dp):
    return 34 if plane(dp) else dp - 1


def gather_steps(links, src, dst, ss, rs):
    me = links.me
    rows = src.shape[0]

    def part(b, first=0, count=rows):
        return pl.ds(pl.multiple_of(b * rows + first, count), count)

    if not links.depth:
        cps = [links.send(src, dst.at[part(me)], ss.at[k], rs.at[k], p) for k, p in enumerate(links.peers)]

        def begin():
            for c in cps:
                c.start()
            dst[part(me), :] = src[...]

        def end():
            for c in cps:
                c.wait()

        return [begin] + [lambda: None] * 13 + [end]
    depth, half = links.depth, rows // 2
    z, y, x, xn, yn = links.z, links.y, links.x, links.xn, links.yn
    origin = [z] + [jnp.maximum(z - d, 0) for d in range(1, depth)] + [jnp.minimum(z + d, depth - 1) for d in range(1, depth)]
    there = [z >= 0] + [z >= d for d in range(1, depth)] + [z + d < depth for d in range(1, depth)]
    up, down, up_on, down_on = {}, {}, {}, {}
    above, below = links.at(jnp.minimum(z + 1, depth - 1), y, x), links.at(jnp.maximum(z - 1, 0), y, x)
    for d in range(1, depth):
        b = links.at(origin[d - 1], y, x)
        s = src if d == 1 else dst.at[part(b)]
        up[d] = links.send(s, dst.at[part(b)], ss.at[d - 1], rs.at[d - 1], above)
        up_on[d] = (z < depth - 1) & (z >= d - 1)
        b = links.at(origin[0 if d == 1 else d + 2], y, x)
        s = src if d == 1 else dst.at[part(b)]
        down[d] = links.send(s, dst.at[part(b)], ss.at[d + 2], rs.at[d + 2], below)
        down_on[d] = (z > 0) & (z + d - 1 < depth)
    xc, yc, xf, yf = [], [], [], []
    for i in range(2 * depth - 1):
        b = links.at(origin[i], y, x)
        s = src if i == 0 else dst.at[part(b)]
        n = 6 + 4 * i
        xc.append(links.send(s, dst.at[part(b)], ss.at[n], rs.at[n], xn))
        yc.append(links.send(s, dst.at[part(b)], ss.at[n + 1], rs.at[n + 1], yn))
        lo = dst.at[part(links.at(origin[i], y, 1 - x), 0, half)]
        hi = dst.at[part(links.at(origin[i], 1 - y, x), half, half)]
        yf.append(links.send(lo, lo, ss.at[n + 2], rs.at[n + 2], yn))
        xf.append(links.send(hi, hi, ss.at[n + 3], rs.at[n + 3], xn))

    def begin():
        pl.when(up_on[1])(up[1].start)
        pl.when(down_on[1])(down[1].start)
        xc[0].start()
        yc[0].start()
        dst[part(me), :] = src[...]

    def spread(i):
        chain, on, d = (up, up_on, i) if i < depth else (down, down_on, i - depth + 1)

        def run():
            @pl.when(there[i])
            def _():
                chain[d].wait_recv()
                if d + 1 < depth:
                    pl.when(on[d + 1])(chain[d + 1].start)
                xc[i].start()
                yc[i].start()
        return run

    def forward(i):
        def run():
            @pl.when(there[i])
            def _():
                xc[i].wait_recv()
                yf[i].start()
                yc[i].wait_recv()
                xf[i].start()
        return run

    def end():
        for i in range(2 * depth - 1):
            @pl.when(there[i])
            def _(i=i):
                yf[i].wait_recv()
                xf[i].wait_recv()
                for c in (xc[i], yc[i], xf[i], yf[i]):
                    c.wait_send()
        for d in range(1, depth):
            pl.when(up_on[d])(up[d].wait_send)
            pl.when(down_on[d])(down[d].wait_send)

    f = forward
    return [begin] + [spread(i) for i in (1, 4, 2, 5, 3, 6)] + [f(i) for i in (0, 1, 4, 2, 5, 3, 6)] + [end]


def scatter_scratch(dp, rows, cols):
    if not plane(dp):
        return [pltpu.VMEM((dp - 1, rows, cols), BF)] + [pltpu.VMEM((8, 128), BF)] * 2
    d, h = plane(dp), rows // 2
    return [
        pltpu.VMEM((d, 2, h, cols), BF),
        pltpu.VMEM((d, 2, rows, cols), BF),
        pltpu.VMEM((d - 1, rows, cols), BF),
    ]


def scatter_steps(links, src, out, bufs, ss, rs):
    me = links.me
    rows = src.shape[0] // links.dp

    def part(b, first=0, count=rows):
        return pl.ds(pl.multiple_of(b * rows + first, count), count)

    if not links.depth:
        got = bufs[0]
        cps = [links.send(src.at[part(p)], got.at[k], ss.at[k], rs.at[k], p) for k, p in enumerate(links.peers)]

        def begin():
            for c in cps:
                c.start()

        def end():
            for c in cps:
                c.wait()

            def add(k, total):
                return total + got[k].astype(F32)

            out[...] = lax.fori_loop(0, links.dp - 1, add, src[part(me), :].astype(F32))

        return [begin] + [lambda: None] * 8 + [end]
    halves, come, zcome = bufs
    depth = links.depth
    h = rows // 2
    y, x, xn, yn = links.y, links.x, links.xn, links.yn
    ac, bc, cc = [], [], []
    for k in range(depth):
        zz = links.up(k)
        diag = links.at(zz, 1 - y, 1 - x)
        bx = links.at(zz, y, 1 - x)
        by = links.at(zz, 1 - y, x)
        own = links.at(zz, y, x)
        n = 4 * k
        ac.append((
            links.send(src.at[part(diag, 0, h)], halves.at[k, 0], ss.at[n], rs.at[n], xn),
            links.send(src.at[part(diag, h, h)], halves.at[k, 1], ss.at[n + 1], rs.at[n + 1], yn),
        ))
        bc.append((
            links.send(src.at[part(bx)], come.at[k, 0], ss.at[n + 2], rs.at[n + 2], xn),
            links.send(src.at[part(by)], come.at[k, 1], ss.at[n + 3], rs.at[n + 3], yn),
        ))
        if k:
            n = 4 * depth + k - 1
            cc.append(links.send(src.at[part(own)], zcome.at[k - 1], ss.at[n], rs.at[n], links.zs[k - 1]))

    def add(where, more):
        src[where, :] = (src[where, :].astype(F32) + more.astype(F32)).astype(BF)

    def begin():
        for k in (1, 2, 3, 0):
            ac[k][0].start()
            ac[k][1].start()

    def middle(k):
        def run():
            zz = links.up(k)
            ac[k][0].wait_recv()
            add(part(links.at(zz, 1 - y, x), 0, h), halves[k, 0])
            bc[k][1].start()
            ac[k][1].wait_recv()
            add(part(links.at(zz, y, 1 - x), h, h), halves[k, 1])
            bc[k][0].start()
        return run

    def along(k):
        def run():
            bc[k][0].wait_recv()
            bc[k][1].wait_recv()
            own = part(links.at(links.up(k), y, x))
            total = src[own, :].astype(F32) + come[k, 0].astype(F32) + come[k, 1].astype(F32)
            if k:
                src[own, :] = total.astype(BF)
                cc[k - 1].start()
            else:
                out[...] = total
        return run

    def end():
        for k in range(depth - 1):
            cc[k].wait_recv()
            out[...] += zcome[k].astype(F32)
        for k in range(depth):
            for c in ac[k] + bc[k]:
                c.wait_send()
        for c in cc:
            c.wait_send()

    return [begin, middle(1), middle(2), along(1), middle(3), along(2), middle(0), along(3), along(0), end]


def sigmoid(v):
    return 0.5 * jnp.tanh(0.5 * v) + 0.5


def softplus(v):
    u = jnp.exp(-jnp.abs(v))
    return jnp.maximum(v, 0.0) + jnp.where(u < 1e-3, u * (1.0 - 0.5 * u), jnp.log(1.0 + u))


def slope(v, s):
    return s * (1.0 + v * (1.0 - s))


def block_mask(rows=CH):
    r = lax.broadcasted_iota(jnp.int32, (rows, CH * N), 0)
    c = lax.broadcasted_iota(jnp.int32, (rows, CH * N), 1)
    return (c // N) == (r % CH)


def pick(first):
    r = lax.broadcasted_iota(jnp.int32, (128, CH * N), 0)
    c = lax.broadcasted_iota(jnp.int32, (128, CH * N), 1)
    return jnp.where(r - first == c % N, 1.0, 0.0).astype(BF)


def place(first):
    r = lax.broadcasted_iota(jnp.int32, (CH * N, 128), 0)
    c = lax.broadcasted_iota(jnp.int32, (CH * N, 128), 1)
    return jnp.where(c - first == r % N, 1.0, 0.0).astype(BF)


def eighths(v):
    return jnp.sum(v.reshape(v.shape[0] // 8, 8, v.shape[1]), axis=0)


def layer_kernel(*refs, dp, dims, names):
    R = dict(zip(names, refs))
    lens, tok, cot, w_in, w_o = (R[k] for k in ("lens", "tok", "cot", "w_in", "w_o"))
    wi, wg, wo, toks, cots, normed = (R[k] for k in ("wi", "wg", "wo", "toks", "cots", "normed"))
    select, delta = R["select"], R["delta"]
    offs, xin, conv, actl, dt, gt, dx, y = (R[k] for k in ("offs", "xin", "conv", "actl", "dt", "gt", "dx", "y"))
    ggr, xo, xr, xg, hs, hbuf = (R[k] for k in ("ggr", "xo", "xr", "xg", "hs", "hbuf"))
    par, btc, ctc, cblk, bblk, a2, st, racc = (R[k] for k in ("par", "btc", "ctc", "cblk", "bblk", "a2", "st", "racc"))
    qtmp, sgs, das, wgs, rgs, accs = (R[k] for k in ("qtmp", "sgs", "das", "wgs", "rgs", "accs"))
    d_out, d_gate, msend, mrecv, sw_s, sw_r, hsem, lsem = (
        R[k] for k in ("d_out", "d_gate", "msend", "mrecv", "sw_s", "sw_r", "hsem", "lsem"))
    taps, rank = dims
    links = Links(dp)
    core, me = links.core, links.me
    rows, width = tok.shape
    half = wi.shape[1]
    total = 2 * rows
    own_d = w_in.shape[0]
    inner = 2 * half
    own_e = inner // dp
    lanes = half // 128
    c1 = rank + 2 * N
    r_taps, r_fb, r_db, r_sk, gcol = (c1 + N + k for k in (0, taps, taps + 1, taps + 2, taps + 3))
    gated = toks

    def cut(ref, start):
        return ref.at[:, pl.ds(pl.multiple_of(start + core * half, 128), half)]

    def lane(b, n=128):
        return slice(b * n, (b + 1) * n)

    def tiles(n, body, size):
        def run(i, _):
            body(pl.multiple_of(i * size, size))
            return 0
        lax.fori_loop(0, n // size, run, 0)

    links.barrier()
    mine = pl.ds(pl.multiple_of(core * rows, rows), rows)
    other = pl.ds(pl.multiple_of((1 - core) * rows, rows), rows)
    t_idx = lax.broadcasted_iota(jnp.int32, (rows, 128), 0)
    begin = jnp.zeros((rows, 128), jnp.int32)
    start = lens[0, 0]
    for k in range(1, lens.shape[1]):
        begin = jnp.where(t_idx >= start, start, begin)
        start = start + lens[0, k]
    offs[mine, :] = (t_idx - begin).astype(F32)
    offs[pl.ds(total, 8), :] = jnp.zeros((8, 128), F32)
    t_swap = links.swap(tok, toks.at[mine], sw_s.at[0], sw_r.at[0])
    o_swap = links.swap(offs.at[mine], offs.at[mine], sw_s.at[1], sw_r.at[1])
    c_swap = links.swap(cot, cots.at[mine], sw_s.at[2], sw_r.at[2])
    c_copy = pltpu.make_async_copy(cot, cots.at[mine], lsem.at[0])
    g_i = gather_steps(links, cut(w_in, 0), wi, R["gi_s"], R["gi_r"])
    near = bool(links.depth)
    if near:
        pk, sm = R["pk"], R["sm"]
        pk[0:c1, :] = R["s_select"][...]
        pk[c1:c1 + N, :] = R["s_decay"][...]
        tail = jnp.concatenate(
            [R[k][...].astype(F32) for k in ("s_filter", "s_fb", "s_db", "s_skip")]
            + [jnp.concatenate([R["s_gain"][...].astype(F32), jnp.zeros((1, own_e - own_d), F32)], axis=1),
               jnp.zeros((16 - taps - 4, own_e), F32)], axis=0).astype(BF)
        pk[c1 + N:128, :] = tail
        pk[128:128 + rank, :] = R["s_delta"][...]
        pk[128 + rank:128 + c1 + N, :] = jnp.zeros((c1 + N - rank, own_e), BF)
        pk[128 + c1 + N:256, :] = tail
        g_s = gather_steps(links, pk.at[pl.ds(pl.multiple_of(core * 128, 128), 128), :], sm.at[core], R["gs_s"], R["gs_r"])
    else:
        g_s = [lambda: None] * 15
    g_g = gather_steps(links, cut(w_in, inner), wg, R["gg_s"], R["gg_r"])
    g_o = gather_steps(links, cut(w_o, 0), wo, R["go_s"], R["go_r"])
    g_s[0]()
    g_i[0]()
    t_swap.start()
    o_swap.start()
    toks[mine, :] = tok[...]
    for k in range(1, 7):
        g_s[k]()
        g_i[k]()
    g_g[0]()
    for k in range(7, 14):
        g_s[k]()
        g_i[k]()
    g_s[14]()
    theirs = pl.ds(pl.multiple_of((1 - core) * half, half), half)
    if near:
        s_swap = links.swap(sm.at[core, theirs], sm.at[core, theirs], sw_s.at[3], sw_r.at[3])
        s_swap.start()
    for k in range(1, 7):
        g_g[k]()
    g_o[0]()
    t_swap.wait()
    o_swap.wait()
    c_swap.start()
    c_copy.start()

    if near:
        gain = jnp.concatenate(
            [sm[core, pl.ds(i * 128 + c1 + N, 16), :].astype(F32)[taps + 3:taps + 4, :own_d] for i in range(dp)], axis=1)
    else:
        gain = R["f_gain"][...].astype(F32)

    def norm(t0):
        r = pl.ds(t0, 64)
        v = toks[r, :].astype(F32)
        inv = lax.rsqrt(jnp.mean(v * v, axis=-1, keepdims=True) + EPS)
        normed[r, :] = (v * inv * gain).astype(BF)

    tiles(total, norm, 64)
    g_i[14]()
    xin[0:8, :] = jnp.zeros((8, half), F32)

    def in_proj(j):
        xin[pl.ds(8, total), pl.ds(j, 256)] = dot(normed[...], wi[:, pl.ds(j, 256)])

    tiles(half, in_proj, 256)
    own = pl.multiple_of(core * half, half)
    row = lax.broadcasted_iota(jnp.int32, (128, 128), 0)
    if near:
        s_swap.wait()
    for b in range(lanes):
        if near:
            one, two = sm[0, pl.ds(own + b * 128, 128), :], sm[1, pl.ds(own + b * 128, 128), :]
        else:
            one, two = R["f_one"][:, lane(b)], R["f_two"][:, lane(b)]
        one, two = one.astype(F32), two.astype(F32)
        par[:, lane(b)] = one
        select[:, lane(b)] = jnp.where(row < c1, one, 0.0).astype(BF)
        delta[:, lane(b)] = jnp.where(row < rank, two, 0.0).astype(BF)
    a2[...] = -jnp.exp(par[c1:c1 + N, :]) * LOG2E

    def conv_tile(t0):
        o = offs[pl.ds(t0, 64), :]
        for b in range(lanes):
            c = lane(b)
            v = xin[pl.ds(t0, 72), c]
            acc = par[r_fb:r_fb + 1, c]
            for j in range(taps):
                s = v[8 - j:72 - j]
                if j:
                    s = jnp.where(o >= float(j), s, 0.0)
                acc = acc + par[r_taps + taps - 1 - j:r_taps + taps - j, c] * s
            conv[pl.ds(t0, 64), c] = acc
            actl[pl.ds(t0, 64), c] = (acc * sigmoid(acc)).astype(BF)

    tiles(total, conv_tile, 64)
    g_g[7]()
    g_g[8]()
    g_g[9]()
    xo[...] = dot(actl[...], select[...], NT)
    x_swap = links.swap(xo, xr, sw_s.at[4], sw_r.at[4])
    x_swap.start()
    g_g[10]()
    g_g[11]()
    x_swap.wait()
    xo[...] += xr[...]

    def dt_tile(t0):
        low = xo[pl.ds(t0, 64), :].astype(BF)
        for b in range(half // 256):
            pre2 = dot(low, delta[:, lane(b, 256)])
            for q in range(2):
                c = lane(2 * b + q)
                s = softplus(pre2[:, lane(q)] + par[r_db:r_db + 1, c])
                dt[pl.ds(t0, 64), c] = s
                cv = conv[pl.ds(t0, 64), c]
                dx[pl.ds(t0, 64), c] = s * (cv * sigmoid(cv))

    tiles(total, dt_tile, 64)
    g_g[12]()
    g_g[13]()
    for k in range(1, 7):
        g_o[k]()
    per = 128 // CH

    def cols_tile(i, _):
        t0 = pl.multiple_of(i * 128, 128)
        x = xo[pl.ds(t0, 128), :]
        t = x.T
        for q in range(per):
            btc[i * per + q] = t[rank:rank + N, q * CH:(q + 1) * CH]
            ctc[i * per + q] = t[rank + N:rank + 2 * N, q * CH:(q + 1) * CH]
        m = block_mask(128)
        cblk[pl.ds(t0, 128), :] = jnp.where(m, dot(x.astype(BF), pick(rank + N)), 0.0).astype(BF)
        bblk[pl.ds(t0, 128), :] = jnp.where(m, dot(x.astype(BF), pick(rank)), 0.0).astype(BF)
        return 0

    lax.fori_loop(0, total // 128, cols_tile, 0)

    steps = [g_g[14]] + g_o[7:14]
    hp = hbuf.shape[1] // N
    hq = hp // CH
    n_blk = total // hp
    st[...] = jnp.zeros_like(st)
    lg = min(512, half)

    def kept(blk):
        return hs.at[pl.ds(pl.multiple_of(blk * hp * N, hp * N), hp * N)]

    def write_out(blk, slot):
        return pltpu.make_async_copy(hbuf.at[slot], kept(blk), hsem.at[slot])

    def f_block(blk, _):
        slot = lax.rem(blk, 2)

        @pl.when(blk >= 2)
        def _():
            write_out(blk - 2, slot).wait()

        def chunk(q, _):
            c = blk * hq + q
            t0 = pl.multiple_of(c * CH, CH)
            for k, s in enumerate(steps):
                pl.when(c == 4 + 4 * k)(s)
            bt = btc[c]
            first = offs[pl.ds(t0, CH), :] == 0.0
            hb = hbuf.at[slot, pl.ds(pl.multiple_of(q * CH * N, CH * N), CH * N), :]
            for g in range(half // lg):
                ls = lane(g, lg)
                a = a2[:, ls]
                h = st[:, ls]
                ds, xs = jnp.where(jnp.concatenate([first] * (lg // 128), axis=1), BIG, dt[pl.ds(t0, CH), ls]), dx[pl.ds(t0, CH), ls]
                for k in range(CH):
                    d = jnp.broadcast_to(ds[k:k + 1], (N, lg))
                    v = jnp.broadcast_to(xs[k:k + 1], (N, lg))
                    w = jnp.broadcast_to(bt[:, k:k + 1], (N, lg))
                    h = jnp.exp2(d * a) * h + w * v
                    hb[k * N:(k + 1) * N, ls] = h.astype(BF)
                st[:, ls] = h
            y[pl.ds(t0, CH), :] = dot(cblk[pl.ds(t0, CH), :], hb[...])
            return 0

        lax.fori_loop(0, hq, chunk, 0)

        @pl.when(blk < n_blk - 2)
        def _():
            write_out(blk, slot).start()

        return 0

    lax.fori_loop(0, n_blk, f_block, 0)
    c_copy.wait()
    c_swap.wait()

    accs[...] = jnp.zeros_like(accs)

    def gate_cols(j):
        gt[:, pl.ds(j, 256)] = dot(normed[...], wg[:, pl.ds(j, 256)])

        def gate_tile(t0):
            r = pl.ds(t0, 64)
            for q in range(2):
                c = pl.ds(pl.multiple_of(j + q * 128, 128), 128)
                cv = conv[r, c]
                scanned = y[r, c] + par[r_sk:r_sk + 1, c] * (cv * sigmoid(cv))
                y[r, c] = scanned
                g = gt[r, c]
                gated[r, c] = (scanned * (g * sigmoid(g))).astype(BF)

        tiles(total, gate_tile, 64)

    tiles(half, gate_cols, 256)

    def outer(left, right, out):
        def body(i):
            for b in range(half // 512):
                out[pl.ds(i, 256), lane(b, 512)] = dot(left[:, pl.ds(i, 256)], right[:, lane(b, 512)], TN).astype(BF)
        tiles(width, body, 256)

    s_o = scatter_steps(links, d_out, R["red_o"], R["so_b"], R["so_s"], R["so_r"])
    s_g = scatter_steps(links, d_gate, R["red_g"], R["sg_b"], R["sg_s"], R["sg_r"])
    outer(cots, gated, d_out)
    s_o[0]()
    g_o[14]()

    def grad_cols(j):
        qtmp[...] = dot(cots[...], wo[:, pl.ds(j, 256)])

        def grad_tile(t0):
            r = pl.ds(t0, 64)
            for q in range(2):
                c = pl.ds(pl.multiple_of(j + q * 128, 128), 128)
                cv = conv[r, c]
                g = gt[r, c]
                sg = sigmoid(g)
                gg = qtmp[r, lane(q)]
                ggr[r, c] = (gg * y[r, c] * slope(g, sg)).astype(BF)
                G = gg * (g * sg)
                y[r, c] = G
                accs[0, :, c] += eighths(G * (cv * sigmoid(cv)))

        tiles(total, grad_tile, 64)

    tiles(half, grad_cols, 256)
    s_o[1]()
    s_o[2]()
    outer(normed, ggr, d_gate)
    s_g[0]()

    def project(which, right, out):
        def body(j):
            out(j, dot(gated[which, :], right[pl.ds(j, 256), :], NT))
        tiles(width, body, 256)

    def put_send(j, v):
        msend[:, pl.ds(j, 256)] = v.astype(BF)

    project(other, wo, put_send)
    m_swap = links.swap(msend, mrecv, sw_s.at[5], sw_r.at[5])
    m_swap.start()

    def put_own(j, v):
        dt0 = tok[:, pl.ds(j, 256)].astype(F32)
        R["mixed_f"][:, pl.ds(j, 256)] = dt0 + v

    project(mine, wo, put_own)
    m_swap.wait()

    def mix_tile(t0):
        r = pl.ds(t0, 16)
        R["mixed"][r, :] = (R["mixed_f"][r, :] + mrecv[r, :].astype(F32)).astype(BF)

    tiles(rows, mix_tile, 16)

    steps_b = s_o[3:9] + s_g[1:3] + [s_o[9]] + [s_g[3], s_g[4], s_g[5], s_g[6], s_g[7], s_g[8], s_g[9]]
    n_chunks = total // CH
    st[...] = jnp.zeros_like(st)
    racc[...] = jnp.zeros_like(racc)

    def read_back(blk, slot):
        return pltpu.make_async_copy(kept(blk), hbuf.at[slot], hsem.at[slot])

    def b_block(i, _):
        blk = n_blk - 1 - i
        slot = lax.rem(blk, 2)

        def chunk(p, _):
            q = hq - 1 - p
            c = blk * hq + q
            t0 = pl.multiple_of(c * CH, CH)
            done = i * hq + p
            for k, s in enumerate(steps_b):
                pl.when(done == 2 + 2 * k)(s)

            @pl.when((q == 0) & (blk >= 1) & (blk <= n_blk - 2))
            def _():
                read_back(blk - 1, 1 - slot).wait()

            before = jnp.where(q == 0, 1 - slot, slot)
            last = pl.multiple_of(jnp.where(q == 0, hp - 1, q * CH - 1) * N, N)
            ct = ctc[c]
            first = offs[pl.ds(t0, CH), :] == 0.0
            hb = hbuf.at[slot, pl.ds(pl.multiple_of(q * CH * N, CH * N), CH * N), :]
            hl = hbuf.at[before, pl.ds(last, N), :]
            for g in range(half // lg):
                ls = lane(g, lg)
                a = a2[:, ls]
                carry = st[:, ls]
                ra = racc[:, ls]
                ds, gs = jnp.where(jnp.concatenate([first] * (lg // 128), axis=1), BIG, dt[pl.ds(t0, CH), ls]), y[pl.ds(t0, CH), ls]
                for k in range(CH - 1, -1, -1):
                    d = jnp.broadcast_to(ds[k:k + 1], (N, lg))
                    gg = jnp.broadcast_to(gs[k:k + 1], (N, lg))
                    cc = jnp.broadcast_to(ct[:, k:k + 1], (N, lg))
                    h = hb[(k - 1) * N:k * N, ls] if k else hl[:, ls]
                    sg = cc * gg + carry
                    carry = jnp.exp2(d * a) * sg
                    term = carry * h.astype(F32)
                    ra = ra + term * d
                    sgs[k * N:(k + 1) * N, ls] = sg.astype(BF)
                    das[k * N:(k + 1) * N, ls] = (term * a).astype(BF)
                st[:, ls] = carry
                racc[:, ls] = ra
            m = block_mask()
            r = pl.ds(t0, CH)
            sgc = sgs[...]
            wout = dot(dx[r, :].astype(BF), sgc, NT)
            wgs[pl.ds(c, 1), :] = jnp.sum(jnp.where(m, wout, 0.0), axis=0, keepdims=True)
            rout = dot(y[r, :].astype(BF), hb[...], NT)
            rgs[pl.ds(c, 1), :] = jnp.sum(jnp.where(m, rout, 0.0), axis=0, keepdims=True)
            dx[r, :] = dot(bblk[r, :], sgc)
            gt[r, :] = dot(m.astype(BF), das[...])
            return 0

        lax.fori_loop(0, hq, chunk, 0)

        @pl.when(blk >= 2)
        def _():
            read_back(blk - 2, slot).start()

        return 0

    lax.fori_loop(0, n_blk, b_block, 0)
    dg, low_b = dx, gated

    ln2 = math.log(2.0)

    def pre_tile(t0):
        r = pl.ds(t0, 64)
        for b in range(lanes):
            c = lane(b)
            cv = conv[r, c]
            act = cv * sigmoid(cv)
            v = (dg[r, c] * act + gt[r, c] * ln2) * (1.0 - jnp.exp(-dt[r, c]))
            low_b[r, c] = v.astype(BF)
            accs[1, :, c] += eighths(v)

    tiles(total, pre_tile, 64)

    def xg_tile(i, _):
        t0 = pl.multiple_of(i * 128, 128)
        r = pl.ds(t0, 128)
        m = block_mask(128)
        sums = dot(low_b[r, :], delta[...], NT)
        for ref, first in ((wgs, rank), (rgs, rank + N)):
            v = ref[pl.ds(pl.multiple_of(i * per, per), per), :]
            v = jnp.broadcast_to(v[:, None, :], (per, CH, CH * N)).reshape(128, CH * N)
            v = jnp.where(m, v, 0.0)
            hi = v.astype(BF)
            lo = (v - hi.astype(F32)).astype(BF)
            p = place(first)
            sums = sums + dot(hi, p) + dot(lo, p)
        xg[r, :] = sums
        return 0

    lax.fori_loop(0, total // 128, xg_tile, 0)
    g_swap = links.swap(xg, xr, sw_s.at[6], sw_r.at[6])
    g_swap.start()
    sgrad = R["sgrad"]
    xob = xo[...].astype(BF)
    for b in range(half // 256):
        sgrad[1, :, lane(b, 256)] = dot(xob, low_b[:, lane(b, 256)], TN)
    g_swap.wait()
    xg[...] = xg[...] + xr[...]
    xgb = xg[...].astype(BF)
    for b in range(half // 256):
        sgrad[0, :, lane(b, 256)] = dot(xgb, actl[:, lane(b, 256)], TN)

    def cg_tile(t0):
        r = pl.ds(t0, 64)
        low = xg[r, :].astype(BF)
        for b in range(half // 256):
            back = dot(low, select[:, lane(b, 256)])
            for q in range(2):
                c = lane(2 * b + q)
                ag = y[r, c] * par[r_sk:r_sk + 1, c] + dg[r, c] * dt[r, c] + back[:, lane(q)]
                cv = conv[r, c]
                v = ag * slope(cv, sigmoid(cv))
                y[r, c] = v
                accs[2, :, c] += eighths(v)

    tiles(total, cg_tile, 64)
    y[pl.ds(total, 8), :] = jnp.zeros((8, half), F32)
    ig = gated

    def ig_tile(t0):
        o = offs[pl.ds(t0, 72), :]
        for b in range(lanes):
            c = lane(b)
            v = y[pl.ds(t0, 72), c]
            x = xin[pl.ds(t0, 72), c]
            acc = jnp.zeros((64, 128), F32)
            for j in range(taps):
                mv = jnp.where(o >= float(j), v, 0.0) if j else v
                accs[3 + taps - 1 - j, :, c] += eighths(mv[0:64] * x[8 - j:72 - j])
                acc = acc + mv[j:64 + j] * par[r_taps + taps - 1 - j:r_taps + taps - j, c]
            ig[pl.ds(t0, 64), c] = acc.astype(BF)

    tiles(total, ig_tile, 64)

    d_in = wo
    s_i = scatter_steps(links, d_in, R["red_i"], R["so_b"], R["si_s"], R["si_r"])
    outer(normed, ig, d_in)
    s_i[0]()

    def back_project(which, out):
        def body(j):
            c = pl.ds(j, 256)
            out(j, dot(ig[which, :], wi[c, :], NT) + dot(ggr[which, :], wg[c, :], NT))
        tiles(width, body, 256)

    back_project(other, put_send)
    n_swap = links.swap(msend, mrecv, sw_s.at[7], sw_r.at[7])
    n_swap.start()
    s_i[1]()
    s_i[2]()
    ng = R["mixed_f"]

    def put_ng(j, v):
        ng[:, pl.ds(j, 256)] = v

    back_project(mine, put_ng)

    vecs = jnp.concatenate(
        [racc[...] * a2[...] * ln2]
        + [jnp.sum(accs[3 + k], axis=0, keepdims=True) for k in range(taps)]
        + [jnp.sum(accs[2], axis=0, keepdims=True), jnp.sum(accs[1], axis=0, keepdims=True),
           jnp.sum(accs[0], axis=0, keepdims=True), jnp.zeros((16 - taps - 3, half), F32)], axis=0)
    sgrad[0, c1:128, :] = vecs
    sgrad[1, rank:128, :] = jnp.zeros((128 - rank, half), F32)
    if near:
        small, away = R["small"], R["away"]
        for b in range(lanes):
            small[pl.ds(own + b * 128, 128), :] = sgrad[core, :, lane(b)].astype(BF)
            away[lane(b), :] = sgrad[1 - core, :, lane(b)].astype(BF)
        a_swap = links.swap(away, small.at[pl.ds(own, half), :], sw_s.at[8], sw_r.at[8])
        a_swap.start()
    s_i[3]()
    s_i[4]()
    n_swap.wait()
    gacc = R["gacc"]
    gacc[...] = jnp.zeros_like(gacc)

    def tok_tile(t0):
        r = pl.ds(t0, 32)
        v = tok[r, :].astype(F32)
        inv = lax.rsqrt(jnp.mean(v * v, axis=-1, keepdims=True) + EPS)
        sc = v * inv
        n = ng[r, :] + mrecv[r, :].astype(F32)
        p = n * sc
        gacc[...] += jnp.sum(p.reshape(4, 8, width), axis=0)
        sg = n * gain
        ng[r, :] = cots[pl.ds(pl.multiple_of(core * rows + t0, 32), 32), :].astype(F32) + inv * (
            sg - sc * jnp.mean(sg * sc, axis=-1, keepdims=True))

    tiles(rows, tok_tile, 32)
    t_copy = pltpu.make_async_copy(ng, R["tgrad"], lsem.at[1])
    t_copy.start()
    s_i[5]()
    grow = jnp.sum(gacc[...], axis=0, keepdims=True)
    if near:
        a_swap.wait()
        low16 = lax.broadcasted_iota(jnp.int32, (16, own_e), 0)
        zero = jnp.zeros((1, own_e - own_d), F32)
        for i in range(dp):
            piece = jnp.concatenate([grow[:, i * own_d:(i + 1) * own_d], zero], axis=1)
            r = pl.ds(i * 128 + c1 + N, 16)
            small[r, :] = jnp.where(low16 == taps + 3, jnp.broadcast_to(piece, (16, own_e)), small[r, :].astype(F32)).astype(BF)
    else:
        R["f_grow"][...] = grow
        R["f_grad"][...] = sgrad[...]
    if near:
        red_s = R["o_small"]
        s_s = scatter_steps(links, small, red_s.at[core], R["ss_b"], R["ss_s"], R["ss_r"])
    else:
        s_s = [lambda: None] * 10
    s_s[0]()
    s_i[6]()
    s_s[1]()
    s_s[2]()
    s_i[7]()
    s_s[3]()
    s_s[4]()
    s_s[5]()
    s_s[6]()
    s_i[8]()
    s_s[7]()
    s_s[8]()
    s_s[9]()
    if near:
        fs = links.swap(red_s.at[core], red_s.at[core], sw_s.at[9], sw_r.at[9])
        fs.start()
    s_i[9]()
    t_copy.wait()

    fins = [links.swap(R[k], R[k + "2"], sw_s.at[10 + n], sw_r.at[10 + n])
            for n, k in enumerate(("red_i", "red_g", "red_o"))]
    for f in fins:
        f.start()
    if near:
        fs.wait()
    for f in fins:
        f.wait()
    for first, k, out in ((0, "red_i", "o_in"), (inner, "red_g", "o_in"), (0, "red_o", "o_out")):
        R[out][:, pl.ds(pl.multiple_of(first + core * half, 128), half)] = R[k][...]
        R[out][:, pl.ds(pl.multiple_of(first + (1 - core) * half, 128), half)] = R[k + "2"][...]


def layer(inputs, dp, dims):
    rows, width = inputs["tok"].shape
    half = inputs["w_o"].shape[1] // 2
    inner = 2 * half
    total = 2 * rows
    taps, rank = dims
    own_d, own_e = width // dp, inner // dp
    n = copies_of(dp)
    near = bool(plane(dp))
    sd = jax.ShapeDtypeStruct
    vm = pl.BlockSpec(memory_space=pltpu.VMEM)
    hbm = pl.BlockSpec(memory_space=pl.ANY)
    dma = pltpu.SemaphoreType.DMA
    V = pltpu.VMEM
    outs = {
        "mixed": sd((rows, width), BF), "tgrad": sd((rows, width), F32),
        "o_in": sd((own_d, 2 * inner), F32), "o_out": sd((own_d, inner), F32), "hs": sd((total * N, half), BF),
    }
    if near:
        outs["o_small"] = sd((2, 128, own_e), F32)
    else:
        outs["f_grad"], outs["f_grow"] = sd((2, 128, half), F32), sd((1, width), F32)
    f2 = V((total, half), F32)
    scratch = {
        "wi": V((width, half), BF), "wg": V((width, half), BF), "wo": V((width, half), BF), "select": V((128, half), BF), "delta": V((128, half), BF),
        "toks": V((total, width), BF), "cots": V((total, width), BF), "normed": V((total, width), BF),
        "offs": V((total + 8, 128), F32), "xin": V((total + 8, half), F32), "conv": f2, "actl": V((total, half), BF),
        "dt": f2, "gt": f2, "dx": f2, "y": V((total + 8, half), F32), "ggr": V((total, half), BF),
        "xo": V((total, 128), F32), "xr": V((total, 128), F32), "xg": V((total, 128), F32),
        "hbuf": V((2, 64 * N, half), BF), "par": V((128, half), F32),
        "btc": V((total // CH, N, CH), F32), "ctc": V((total // CH, N, CH), F32),
        "cblk": V((total, CH * N), BF), "bblk": V((total, CH * N), BF),
        "a2": V((N, half), F32), "st": V((N, half), F32), "racc": V((N, half), F32),
        "qtmp": V((total, 256), F32),
        "sgs": V((CH * N, half), BF), "das": V((CH * N, half), BF),
        "wgs": V((total // CH, CH * N), F32), "rgs": V((total // CH, CH * N), F32),
        "accs": V((3 + taps, 8, half), F32), "d_out": V((width, half), BF), "d_gate": V((width, half), BF),
        "msend": V((rows, width), BF), "mrecv": V((rows, width), BF), "mixed_f": V((rows, width), F32),
        "sgrad": V((2, 128, half), F32), "gacc": V((8, width), F32),
        "so_b": scatter_scratch(dp, own_d, half), "sg_b": scatter_scratch(dp, own_d, half),
        "sw_s": dma((13,)), "sw_r": dma((13,)), "hsem": dma((2,)), "lsem": dma((2,)),
    }
    for k in ("i", "g", "o"):
        scratch["red_" + k] = V((own_d, half), F32)
        scratch["red_" + k + "2"] = V((own_d, half), F32)
    if near:
        scratch["sm"], scratch["pk"] = V((2, inner, own_e), BF), V((256, own_e), BF)
        scratch["small"], scratch["away"] = V((inner, own_e), BF), V((half, own_e), BF)
        scratch["ss_b"] = scatter_scratch(dp, 128, own_e)
    for k in ("gi", "gs", "gg", "go", "si", "sg", "so", "ss"):
        scratch[k + "_s"] = dma((n,))
        scratch[k + "_r"] = dma((n,))
    names = list(inputs) + list(outs) + list(scratch)
    res = pl.pallas_call(
        functools.partial(layer_kernel, dp=dp, dims=dims, names=names),
        out_shape=list(outs.values()),
        in_specs=[pl.BlockSpec(memory_space=pltpu.SMEM) if k == "lens" else hbm if k == "cot" else vm for k in inputs],
        out_specs=[hbm if k in ("tgrad", "hs") else vm for k in outs],
        scratch_shapes=list(scratch.values()),
        compiler_params=pltpu.CompilerParams(collective_id=0, has_side_effects=True, vmem_limit_bytes=127 << 19),
        name="layer",
    )(*inputs.values())
    return dict(zip(outs, res))


def local(
    tokens,
    doc_lengths,
    cotangent,
    norm_gain,
    input_weight,
    filter_weight,
    filter_bias,
    select_weight,
    delta_weight,
    delta_bias,
    decay_log,
    skip_gain,
    output_weight,
    *,
    dp,
):
    rows, length, width = tokens.shape
    rank = delta_weight.shape[1]
    taps = filter_weight.shape[1]
    own_e = filter_weight.shape[0]
    own_d = norm_gain.shape[0]
    inner = own_e * dp
    c1 = rank + 2 * N
    inputs = {
        "lens": doc_lengths, "tok": tokens.reshape(rows * length, width), "cot": cotangent.reshape(rows * length, width),
        "w_in": input_weight, "w_o": output_weight,
    }
    if plane(dp):
        inputs.update(
            s_select=select_weight.T, s_decay=decay_log.T, s_delta=delta_weight.T, s_filter=filter_weight.T,
            s_fb=filter_bias[None], s_db=delta_bias[None], s_skip=skip_gain[None], s_gain=norm_gain[None],
        )
    else:
        core = lax.axis_index("rep")
        vectors = jnp.stack([filter_bias, delta_bias, skip_gain])
        tail = jnp.concatenate([filter_weight.T, vectors, jnp.zeros((16 - taps - 3, own_e), BF)], axis=0)
        one = jnp.concatenate([select_weight.T, decay_log.T, tail], axis=0)
        two = jnp.concatenate([delta_weight.T, jnp.zeros((128 - rank, own_e), BF)], axis=0)
        both = lax.all_gather(jnp.stack([one, two]), "dp", axis=2, tiled=True)
        both = lax.dynamic_slice(both, (0, 0, core * (inner // 2)), (2, 128, inner // 2))
        inputs.update(f_one=both[0], f_two=both[1], f_gain=lax.all_gather(norm_gain, "dp", axis=0, tiled=True)[None])
    r = layer(inputs, dp, (taps, rank))
    if plane(dp):
        small = r["o_small"]
    else:
        small = lax.all_gather(r["f_grad"], "rep", axis=2, tiled=True)
        small = lax.psum_scatter(small, "dp", scatter_dimension=2, tiled=True)
        grow = lax.psum_scatter(lax.psum(r["f_grow"], "rep"), "dp", scatter_dimension=1, tiled=True)
        small = small.at[:, c1 + N + taps + 3, :].set(0.0).at[0, c1 + N + taps + 3, :own_d].set(grow[0])
    o = finish(r["mixed"], r["tgrad"], r["o_in"], r["o_out"], small, (taps, rank), own_d)
    return (
        o[0].reshape(rows, length, width),
        o[1].reshape(rows, length, width),
        o[4].reshape(own_d),
        o[2],
        o[5].T,
        o[6].reshape(own_e),
        o[7].T,
        o[8].T,
        o[9].reshape(own_e),
        o[10].T,
        o[11].reshape(own_e),
        o[3],
    )


def finish(mixed, tgrad, o_in, o_out, small, dims, own_d):
    taps, rank = dims
    c1 = rank + 2 * N
    own_e = small.shape[2]
    sd = jax.ShapeDtypeStruct
    big = [mixed, tgrad, o_in, o_out]

    def kernel(*refs):
        ins, small_ref, outs = refs[:4], refs[4], refs[5:17]
        for i, o in zip(ins, outs[:4]):
            o[...] = i[...]
        g = c1 + N + taps + 3

        @pl.when(pl.program_id(0) == 0)
        def _():
            outs[4][...] = (small_ref[0, g:g + 1, :] + small_ref[1, g:g + 1, :])[:, :own_d]
            outs[5][...] = small_ref[0, c1 + N:c1 + N + taps, :]
            outs[6][...] = small_ref[0, g - 3:g - 2, :]
            outs[7][...] = small_ref[0, 0:c1, :]
            outs[8][...] = small_ref[1, 0:rank, :]
            outs[9][...] = small_ref[0, g - 2:g - 1, :]
            outs[10][...] = small_ref[0, c1:c1 + N, :]
            outs[11][...] = small_ref[0, g - 1:g, :]

    shapes = [sd(b.shape, b.dtype) for b in big] + [
        sd(s, F32) for s in ((1, own_d), (taps, own_e), (1, own_e), (c1, own_e), (rank, own_e), (1, own_e), (N, own_e), (1, own_e))]
    parts = 4
    specs = [pl.BlockSpec((b.shape[0], b.shape[1] // parts), lambda i: (0, i)) for b in big]
    whole = [pl.BlockSpec(s.shape, lambda i, n=len(s.shape): (0,) * n) for s in [small] + shapes[4:]]
    return pl.pallas_call(
        kernel, grid=(parts,), out_shape=shapes, in_specs=specs + whole[:1], out_specs=specs + whole[1:], name="finish",
    )(*big, small)


def solution(mesh):
    dp_rep = ("dp", "rep")
    one = P("dp")
    two = P("dp", None)
    three = P(dp_rep, None, None)
    return jax.shard_map(
        functools.partial(local, dp=mesh.shape["dp"]),
        mesh=mesh,
        in_specs=(three, P(dp_rep, None), three, one, two, two, one, two, two, one, two, one, two),
        out_specs=(three, three, one, two, two, one, two, two, one, two, one, two),
        check_vma=False,
    )
```

```python
import functools
import math

import jax
import jax.numpy as jnp
from jax import lax
from jax.experimental import pallas as pl
from jax.experimental.pallas import tpu as pltpu
from jax.sharding import PartitionSpec as P

EPS = 1e-05
CH = 16
N = 16
F32 = jnp.float32
BF = jnp.bfloat16
NT = (((1,), (1,)), ((), ()))
TN = (((0,), (0,)), ((), ()))
BIG = 1e30
LOG2E = math.log2(math.e)


def dot(a, b, dims=(((1,), (0,)), ((), ()))):
    return lax.dot_general(a, b, dims, preferred_element_type=F32)


MESH = pl.DeviceIdType.MESH


def plane(dp):
    return 4 if dp == 16 else 0


class Links:
    def __init__(self, dp):
        self.dp = dp
        self.depth = plane(dp)
        self.me = lax.axis_index("dp")
        self.core = lax.axis_index("rep")
        if self.depth:
            self.z, self.y, self.x = self.me // 4, (self.me // 2) % 2, self.me % 2
            self.xn = self.at(self.z, self.y, 1 - self.x)
            self.yn = self.at(self.z, 1 - self.y, self.x)
            self.zs = [self.at(self.up(k), self.y, self.x) for k in range(1, self.depth)]
            self.peers = self.zs + [self.xn, self.yn]
        else:
            self.peers = [lax.rem(self.me + k, dp) for k in range(1, dp)]

    def up(self, k):
        return lax.rem(self.z + k, self.depth)

    def down(self, k):
        return lax.rem(self.z + self.depth - k, self.depth)

    def at(self, z, y, x):
        return (z * 2 + y) * 2 + x

    def barrier(self, sibling=True):
        sem = pltpu.get_barrier_semaphore()
        for peer in self.peers:
            pl.semaphore_signal(sem, inc=1, device_id=(peer, self.core), device_id_type=MESH)
        if sibling:
            pl.semaphore_signal(sem, inc=1, device_id=(self.me, 1 - self.core), device_id_type=MESH)
        pl.semaphore_wait(sem, len(self.peers) + int(sibling))

    def send(self, src, dst, send_sem, recv_sem, chip):
        return pltpu.make_async_remote_copy(
            src_ref=src, dst_ref=dst, send_sem=send_sem, recv_sem=recv_sem,
            device_id=(chip, self.core), device_id_type=MESH,
        )

    def swap(self, src, dst, send_sem, recv_sem):
        return pltpu.make_async_remote_copy(
            src_ref=src, dst_ref=dst, send_sem=send_sem, recv_sem=recv_sem,
            device_id=(self.me, 1 - self.core), device_id_type=MESH,
        )


def copies_of(dp):
    return 34 if plane(dp) else dp - 1


def gather_steps(links, src, dst, ss, rs):
    me = links.me
    rows = src.shape[0]

    def part(b, first=0, count=rows):
        return pl.ds(pl.multiple_of(b * rows + first, math.gcd(rows, count)), count)

    if not links.depth:
        cps = [links.send(src, dst.at[part(me)], ss.at[k], rs.at[k], p) for k, p in enumerate(links.peers)]

        def begin():
            for c in cps:
                c.start()
            dst[part(me), :] = src[...]

        def end():
            for c in cps:
                c.wait()

        return [begin] + [lambda: None] * 14 + [end]
    depth, half = links.depth, rows // 2
    cuts = [half if half % 16 == 0 else half + (8 if i % 2 else -8) for i in range(2 * depth - 1)]
    z, y, x, xn, yn = links.z, links.y, links.x, links.xn, links.yn
    origin = [z] + [jnp.maximum(z - d, 0) for d in range(1, depth)] + [jnp.minimum(z + d, depth - 1) for d in range(1, depth)]
    there = [z >= 0] + [z >= d for d in range(1, depth)] + [z + d < depth for d in range(1, depth)]
    up, down, up_on, down_on = {}, {}, {}, {}
    above, below = links.at(jnp.minimum(z + 1, depth - 1), y, x), links.at(jnp.maximum(z - 1, 0), y, x)
    for d in range(1, depth):
        b = links.at(origin[d - 1], y, x)
        s = src if d == 1 else dst.at[part(b)]
        up[d] = links.send(s, dst.at[part(b)], ss.at[d - 1], rs.at[d - 1], above)
        up_on[d] = (z < depth - 1) & (z >= d - 1)
        b = links.at(origin[0 if d == 1 else d + 2], y, x)
        s = src if d == 1 else dst.at[part(b)]
        down[d] = links.send(s, dst.at[part(b)], ss.at[d + 2], rs.at[d + 2], below)
        down_on[d] = (z > 0) & (z + d - 1 < depth)
    xc, yc, xf, yf = [], [], [], []
    for i in range(2 * depth - 1):
        b = links.at(origin[i], y, x)
        s = src if i == 0 else dst.at[part(b)]
        n = 6 + 4 * i
        xc.append(links.send(s, dst.at[part(b)], ss.at[n], rs.at[n], xn))
        yc.append(links.send(s, dst.at[part(b)], ss.at[n + 1], rs.at[n + 1], yn))
        lo = dst.at[part(links.at(origin[i], y, 1 - x), 0, cuts[i])]
        hi = dst.at[part(links.at(origin[i], 1 - y, x), cuts[i], rows - cuts[i])]
        yf.append(links.send(lo, lo, ss.at[n + 2], rs.at[n + 2], yn))
        xf.append(links.send(hi, hi, ss.at[n + 3], rs.at[n + 3], xn))

    def begin():
        pl.when(up_on[1])(up[1].start)
        pl.when(down_on[1])(down[1].start)

    def beside():
        xc[0].start()
        yc[0].start()
        dst[part(me), :] = src[...]

    def spread(i):
        chain, on, d = (up, up_on, i) if i < depth else (down, down_on, i - depth + 1)

        def run():
            @pl.when(there[i])
            def _():
                chain[d].wait_recv()
                if d + 1 < depth:
                    pl.when(on[d + 1])(chain[d + 1].start)
                xc[i].start()
                yc[i].start()
        return run

    def forward(i):
        def run():
            @pl.when(there[i])
            def _():
                xc[i].wait_recv()
                yf[i].start()
                yc[i].wait_recv()
                xf[i].start()
        return run

    def end():
        for i in range(2 * depth - 1):
            @pl.when(there[i])
            def _(i=i):
                yf[i].wait_recv()
                xf[i].wait_recv()
                for c in (xc[i], yc[i], xf[i], yf[i]):
                    c.wait_send()
        for d in range(1, depth):
            pl.when(up_on[d])(up[d].wait_send)
            pl.when(down_on[d])(down[d].wait_send)

    f = forward
    return [begin, beside] + [spread(i) for i in (1, 4, 2, 5, 3, 6)] + [f(i) for i in (0, 1, 4, 2, 5, 3, 6)] + [end]


def scatter_scratch(dp, rows, cols):
    if not plane(dp):
        return [pltpu.VMEM((dp - 1, rows, cols), BF)] + [pltpu.VMEM((8, 128), BF)] * 2
    d, h = plane(dp), rows // 2
    return [
        pltpu.VMEM((d, 2, h, cols), BF),
        pltpu.VMEM((d, 2, rows, cols), BF),
        pltpu.VMEM((d - 1, rows, cols), BF),
    ]


def scatter_steps(links, src, out, bufs, ss, rs, offset=0):
    me = links.me
    rows = out.shape[0]
    pitch = src.shape[0] // links.dp

    def part(b, first=0, count=rows):
        return pl.ds(pl.multiple_of(b * pitch + offset + first, math.gcd(math.gcd(pitch, offset + first), count)), count)

    if not links.depth:
        got = bufs[0]
        cps = [links.send(src.at[part(p)], got.at[k], ss.at[k], rs.at[k], p) for k, p in enumerate(links.peers)]

        def begin():
            for c in cps:
                c.start()

        def end():
            for c in cps:
                c.wait()

            def add(k, total):
                return total + got[k].astype(F32)

            out[...] = lax.fori_loop(0, links.dp - 1, add, src[part(me), :].astype(F32))

        return [begin] + [lambda: None] * 8 + [end]
    halves, come, zcome = bufs
    depth = links.depth
    h = rows // 2
    y, x, xn, yn = links.y, links.x, links.xn, links.yn
    ac, bc, cc = [], [], []
    for k in range(depth):
        zz = links.up(k)
        diag = links.at(zz, 1 - y, 1 - x)
        bx = links.at(zz, y, 1 - x)
        by = links.at(zz, 1 - y, x)
        own = links.at(zz, y, x)
        n = 4 * k
        ac.append((
            links.send(src.at[part(diag, 0, h)], halves.at[k, 0], ss.at[n], rs.at[n], xn),
            links.send(src.at[part(diag, h, h)], halves.at[k, 1], ss.at[n + 1], rs.at[n + 1], yn),
        ))
        bc.append((
            links.send(src.at[part(bx)], come.at[k, 0], ss.at[n + 2], rs.at[n + 2], xn),
            links.send(src.at[part(by)], come.at[k, 1], ss.at[n + 3], rs.at[n + 3], yn),
        ))
        if k:
            n = 4 * depth + k - 1
            cc.append(links.send(src.at[part(own)], zcome.at[k - 1], ss.at[n], rs.at[n], links.zs[k - 1]))

    def add(where, more):
        src[where, :] = (src[where, :].astype(F32) + more.astype(F32)).astype(BF)

    def begin():
        for k in (1, 2, 3, 0):
            ac[k][0].start()
            ac[k][1].start()

    def middle(k):
        def run():
            zz = links.up(k)
            ac[k][0].wait_recv()
            add(part(links.at(zz, 1 - y, x), 0, h), halves[k, 0])
            bc[k][1].start()
            ac[k][1].wait_recv()
            add(part(links.at(zz, y, 1 - x), h, h), halves[k, 1])
            bc[k][0].start()
        return run

    def along(k):
        def run():
            bc[k][0].wait_recv()
            bc[k][1].wait_recv()
            own = part(links.at(links.up(k), y, x))
            total = src[own, :].astype(F32) + come[k, 0].astype(F32) + come[k, 1].astype(F32)
            if k:
                src[own, :] = total.astype(BF)
                cc[k - 1].start()
            else:
                out[...] = total
        return run

    def end():
        for k in range(depth - 1):
            cc[k].wait_recv()
            out[...] += zcome[k].astype(F32)
        for k in range(depth):
            for c in ac[k] + bc[k]:
                c.wait_send()
        for c in cc:
            c.wait_send()

    return [begin, middle(1), middle(2), along(1), middle(3), along(2), middle(0), along(3), along(0), end]


def sigmoid(v):
    return 0.5 * jnp.tanh(0.5 * v) + 0.5


def softplus(v):
    u = jnp.exp(-jnp.abs(v))
    return jnp.maximum(v, 0.0) + jnp.where(u < 1e-3, u * (1.0 - 0.5 * u), jnp.log(1.0 + u))


def slope(v, s):
    return s * (1.0 + v * (1.0 - s))


def block_mask(rows=CH):
    r = lax.broadcasted_iota(jnp.int32, (rows, CH * N), 0)
    c = lax.broadcasted_iota(jnp.int32, (rows, CH * N), 1)
    return (c // N) == (r % CH)


def pick(first):
    r = lax.broadcasted_iota(jnp.int32, (128, CH * N), 0)
    c = lax.broadcasted_iota(jnp.int32, (128, CH * N), 1)
    return jnp.where(r - first == c % N, 1.0, 0.0).astype(BF)


def place(first):
    r = lax.broadcasted_iota(jnp.int32, (CH * N, 128), 0)
    c = lax.broadcasted_iota(jnp.int32, (CH * N, 128), 1)
    return jnp.where(c - first == r % N, 1.0, 0.0).astype(BF)


def eighths(v):
    return jnp.sum(v.reshape(v.shape[0] // 8, 8, v.shape[1]), axis=0)


def layer_kernel(*refs, dp, dims, names):
    R = dict(zip(names, refs))
    lens, tok, cot, w_in, w_o = (R[k] for k in ("lens", "tok", "cot", "w_in", "w_o"))
    wi, ww, toks, cots, normed = (R[k] for k in ("wi", "ww", "toks", "cots", "normed"))
    select, delta = R["select"], R["delta"]
    offs, xin, conv, actl, dt, gt, dx, y = (R[k] for k in ("offs", "xin", "conv", "actl", "dt", "gt", "dx", "y"))
    ggr, xo, xr, xg, hs, hbuf = (R[k] for k in ("ggr", "xo", "xr", "xg", "hs", "hbuf"))
    par, btc, ctc, cblk, bblk, a2, st, racc = (R[k] for k in ("par", "btc", "ctc", "cblk", "bblk", "a2", "st", "racc"))
    qtmp, sgs, das, wgs, rgs, accs = (R[k] for k in ("qtmp", "sgs", "das", "wgs", "rgs", "accs"))
    d_out, d_gate, msend, mrecv, sw_s, sw_r, hsem, lsem = (
        R[k] for k in ("d_out", "d_gate", "msend", "mrecv", "sw_s", "sw_r", "hsem", "lsem"))
    taps, rank = dims
    links = Links(dp)
    core, me = links.core, links.me
    rows, width = tok.shape
    half = wi.shape[1]
    total = 2 * rows
    own_d = w_in.shape[0]
    inner = 2 * half
    own_e = inner // dp
    lanes = half // 128
    c1 = rank + 2 * N
    r_taps, r_fb, r_db, r_sk, gcol = (c1 + N + k for k in (0, taps, taps + 1, taps + 2, taps + 3))
    gated = toks

    def cut(ref, start):
        return ref[:, pl.ds(pl.multiple_of(start + core * half, 128), half)]

    pitch_i, pitch_w = wi.shape[0] // dp, 2 * own_d

    def cols_of(ref, first, c):
        v = ref[:, c]
        return v.reshape(dp, ref.shape[0] // dp, v.shape[1])[:, first:first + own_d].reshape(width, v.shape[1])

    def rows_of(ref, first, i):
        n = 256 // own_d
        p = ref.shape[0] // dp
        v = ref[pl.ds(pl.multiple_of(i * n * p, n * p), n * p), :]
        return v.reshape(n, p, half)[:, first:first + own_d].reshape(256, half)

    def lane(b, n=128):
        return slice(b * n, (b + 1) * n)

    def tiles(n, body, size):
        def run(i, _):
            body(pl.multiple_of(i * size, size))
            return 0
        lax.fori_loop(0, n // size, run, 0)

    near = bool(links.depth)
    part_i, part_w = R["part_i"], R["part_w"]
    part_i[0:own_d, :] = cut(w_in, 0)
    part_w[0:own_d, :] = cut(w_in, inner)
    part_w[own_d:, :] = cut(w_o, 0)
    if near:
        sm = R["sm"]
        tail = jnp.concatenate(
            [R[k][...].astype(F32) for k in ("s_filter", "s_fb", "s_db", "s_skip")]
            + [jnp.concatenate([R["s_gain"][...].astype(F32), jnp.zeros((1, own_e - own_d), F32)], axis=1),
               jnp.zeros((16 - taps - 4, own_e), F32)], axis=0).astype(BF)
        for q in range(8):
            one = R["s_select"][q * 16:q * 16 + 16, :] if q < c1 // 16 else R["s_decay"][...] if q < 7 else tail
            two = R["s_delta"][q * 16:q * 16 + 16, :] if q < rank // 16 else tail
            part_i[own_d:own_d + 16, lane(q)] = jnp.where(core == 0, one.astype(F32), two.astype(F32)).astype(BF)
    links.barrier()
    mine = pl.ds(pl.multiple_of(core * rows, rows), rows)
    other = pl.ds(pl.multiple_of((1 - core) * rows, rows), rows)
    t_idx = lax.broadcasted_iota(jnp.int32, (rows, 128), 0)
    begin = jnp.zeros((rows, 128), jnp.int32)
    start = lens[0, 0]
    for k in range(1, lens.shape[1]):
        begin = jnp.where(t_idx >= start, start, begin)
        start = start + lens[0, k]
    offs[mine, :] = (t_idx - begin).astype(F32)
    offs[pl.ds(total, 8), :] = jnp.zeros((8, 128), F32)
    t_swap = links.swap(tok, toks.at[mine], sw_s.at[0], sw_r.at[0])
    o_swap = links.swap(offs.at[mine], offs.at[mine], sw_s.at[1], sw_r.at[1])
    c_swap = links.swap(cot, cots.at[mine], sw_s.at[2], sw_r.at[2])
    c_copy = pltpu.make_async_copy(cot, cots.at[mine], lsem.at[0])
    g_i = gather_steps(links, part_i, wi, R["gi_s"], R["gi_r"])
    g_w = gather_steps(links, part_w, ww, R["gw_s"], R["gw_r"])
    g_i[0]()
    g_i[1]()
    t_swap.start()
    o_swap.start()
    toks[mine, :] = tok[...]
    for k in range(2, 8):
        g_i[k]()
    g_w[0]()
    for k in range(8, 15):
        g_i[k]()
    for k in range(1, 8):
        g_w[k]()
    g_i[15]()
    if near:
        for i in range(dp):
            for q in range(8):
                sm[core, i * 128 + q * 16:i * 128 + q * 16 + 16, :] = wi[i * pitch_i + own_d:i * pitch_i + own_d + 16, lane(q)]
        theirs = pl.ds(pl.multiple_of((1 - core) * half, half), half)
        s_swap = links.swap(sm.at[core, theirs], sm.at[core, theirs], sw_s.at[3], sw_r.at[3])
        s_swap.start()
    t_swap.wait()
    o_swap.wait()
    c_swap.start()
    c_copy.start()

    if near:
        gain = jnp.concatenate(
            [sm[core, pl.ds(i * 128 + c1 + N, 16), :].astype(F32)[taps + 3:taps + 4, :own_d] for i in range(dp)], axis=1)
    else:
        gain = R["f_gain"][...].astype(F32)

    def norm(t0):
        r = pl.ds(t0, 64)
        v = toks[r, :].astype(F32)
        inv = lax.rsqrt(jnp.mean(v * v, axis=-1, keepdims=True) + EPS)
        normed[r, :] = (v * inv * gain).astype(BF)

    tiles(total, norm, 64)
    xin[0:8, :] = jnp.zeros((8, half), F32)

    def in_proj(j):
        xin[pl.ds(8, total), pl.ds(j, 256)] = dot(normed[...], cols_of(wi, 0, pl.ds(j, 256)))

    tiles(half, in_proj, 256)
    own = pl.multiple_of(core * half, half)
    row = lax.broadcasted_iota(jnp.int32, (128, 128), 0)
    if near:
        s_swap.wait()
    for b in range(lanes):
        if near:
            one, two = sm[0, pl.ds(own + b * 128, 128), :], sm[1, pl.ds(own + b * 128, 128), :]
        else:
            one, two = R["f_one"][:, lane(b)], R["f_two"][:, lane(b)]
        one, two = one.astype(F32), two.astype(F32)
        par[:, lane(b)] = one
        select[:, lane(b)] = jnp.where(row < c1, one, 0.0).astype(BF)
        delta[:, lane(b)] = jnp.where(row < rank, two, 0.0).astype(BF)
    a2[...] = -jnp.exp(par[c1:c1 + N, :]) * LOG2E

    def conv_tile(t0):
        o = offs[pl.ds(t0, 64), :]
        for b in range(lanes):
            c = lane(b)
            v = xin[pl.ds(t0, 72), c]
            acc = par[r_fb:r_fb + 1, c]
            for j in range(taps):
                s = v[8 - j:72 - j]
                if j:
                    s = jnp.where(o >= float(j), s, 0.0)
                acc = acc + par[r_taps + taps - 1 - j:r_taps + taps - j, c] * s
            conv[pl.ds(t0, 64), c] = acc
            actl[pl.ds(t0, 64), c] = (acc * sigmoid(acc)).astype(BF)

    tiles(total, conv_tile, 64)
    xo[...] = dot(actl[...], select[...], NT)
    x_swap = links.swap(xo, xr, sw_s.at[4], sw_r.at[4])
    x_swap.start()
    x_swap.wait()
    xo[...] += xr[...]

    def dt_tile(t0):
        low = xo[pl.ds(t0, 64), :].astype(BF)
        for b in range(half // 256):
            pre2 = dot(low, delta[:, lane(b, 256)])
            for q in range(2):
                c = lane(2 * b + q)
                s = softplus(pre2[:, lane(q)] + par[r_db:r_db + 1, c])
                dt[pl.ds(t0, 64), c] = s
                cv = conv[pl.ds(t0, 64), c]
                dx[pl.ds(t0, 64), c] = s * (cv * sigmoid(cv))

    tiles(total, dt_tile, 64)
    per = 128 // CH

    def cols_tile(i, _):
        t0 = pl.multiple_of(i * 128, 128)
        x = xo[pl.ds(t0, 128), :]
        t = x.T
        for q in range(per):
            btc[i * per + q] = t[rank:rank + N, q * CH:(q + 1) * CH]
            ctc[i * per + q] = t[rank + N:rank + 2 * N, q * CH:(q + 1) * CH]
        m = block_mask(128)
        cblk[pl.ds(t0, 128), :] = jnp.where(m, dot(x.astype(BF), pick(rank + N)), 0.0).astype(BF)
        bblk[pl.ds(t0, 128), :] = jnp.where(m, dot(x.astype(BF), pick(rank)), 0.0).astype(BF)
        return 0

    lax.fori_loop(0, total // 128, cols_tile, 0)

    steps = g_w[8:15]
    hp = hbuf.shape[1] // N
    hq = hp // CH
    n_blk = total // hp
    st[...] = jnp.zeros_like(st)
    lg = min(512, half)

    def kept(blk):
        return hs.at[pl.ds(pl.multiple_of(blk * hp * N, hp * N), hp * N)]

    def write_out(blk, slot):
        return pltpu.make_async_copy(hbuf.at[slot], kept(blk), hsem.at[slot])

    def f_block(blk, _):
        slot = lax.rem(blk, 2)

        @pl.when(blk >= 2)
        def _():
            write_out(blk - 2, slot).wait()

        def chunk(q, _):
            c = blk * hq + q
            t0 = pl.multiple_of(c * CH, CH)
            for k, s in enumerate(steps):
                pl.when(c == 6 + 4 * k)(s)
            bt = btc[c]
            first = offs[pl.ds(t0, CH), :] == 0.0
            hb = hbuf.at[slot, pl.ds(pl.multiple_of(q * CH * N, CH * N), CH * N), :]
            for g in range(half // lg):
                ls = lane(g, lg)
                a = a2[:, ls]
                h = st[:, ls]
                ds, xs = jnp.where(jnp.concatenate([first] * (lg // 128), axis=1), BIG, dt[pl.ds(t0, CH), ls]), dx[pl.ds(t0, CH), ls]
                for k in range(CH):
                    d = jnp.broadcast_to(ds[k:k + 1], (N, lg))
                    v = jnp.broadcast_to(xs[k:k + 1], (N, lg))
                    w = jnp.broadcast_to(bt[:, k:k + 1], (N, lg))
                    h = jnp.exp2(d * a) * h + w * v
                    hb[k * N:(k + 1) * N, ls] = h.astype(BF)
                st[:, ls] = h
            y[pl.ds(t0, CH), :] = dot(cblk[pl.ds(t0, CH), :], hb[...])
            return 0

        lax.fori_loop(0, hq, chunk, 0)

        @pl.when(blk < n_blk - 2)
        def _():
            write_out(blk, slot).start()

        return 0

    lax.fori_loop(0, n_blk, f_block, 0)
    c_copy.wait()
    c_swap.wait()

    accs[...] = jnp.zeros_like(accs)

    def gate_cols(j):
        gt[:, pl.ds(j, 256)] = dot(normed[...], cols_of(ww, 0, pl.ds(j, 256)))

        def gate_tile(t0):
            r = pl.ds(t0, 64)
            for q in range(2):
                c = pl.ds(pl.multiple_of(j + q * 128, 128), 128)
                cv = conv[r, c]
                scanned = y[r, c] + par[r_sk:r_sk + 1, c] * (cv * sigmoid(cv))
                y[r, c] = scanned
                g = gt[r, c]
                gated[r, c] = (scanned * (g * sigmoid(g))).astype(BF)

        tiles(total, gate_tile, 64)

    g_w[15]()
    tiles(half, gate_cols, 256)

    def outer(left, right, out):
        def body(i):
            for b in range(half // 512):
                out[pl.ds(i, 256), lane(b, 512)] = dot(left[:, pl.ds(i, 256)], right[:, lane(b, 512)], TN).astype(BF)
        tiles(width, body, 256)

    s_o = scatter_steps(links, d_out, R["red_o"], R["so_b"], R["so_s"], R["so_r"])
    s_g = scatter_steps(links, d_gate, R["red_g"], R["sg_b"], R["sg_s"], R["sg_r"])
    outer(cots, gated, d_out)
    s_o[0]()

    def grad_cols(j):
        qtmp[...] = dot(cots[...], cols_of(ww, own_d, pl.ds(j, 256)))

        def grad_tile(t0):
            r = pl.ds(t0, 64)
            for q in range(2):
                c = pl.ds(pl.multiple_of(j + q * 128, 128), 128)
                cv = conv[r, c]
                g = gt[r, c]
                sg = sigmoid(g)
                gg = qtmp[r, lane(q)]
                ggr[r, c] = (gg * y[r, c] * slope(g, sg)).astype(BF)
                G = gg * (g * sg)
                y[r, c] = G
                accs[0, :, c] += eighths(G * (cv * sigmoid(cv)))

        tiles(total, grad_tile, 64)

    tiles(half, grad_cols, 256)
    outer(normed, ggr, d_gate)
    s_g[0]()

    def project(which, out):
        def body(i, _):
            out(pl.multiple_of(i * 256, 256), dot(gated[which, :], rows_of(ww, own_d, i), NT))
            return 0
        lax.fori_loop(0, width // 256, body, 0)

    def put_send(j, v):
        msend[:, pl.ds(j, 256)] = v.astype(BF)

    project(other, put_send)
    m_swap = links.swap(msend, mrecv, sw_s.at[5], sw_r.at[5])
    m_swap.start()

    def put_own(j, v):
        dt0 = tok[:, pl.ds(j, 256)].astype(F32)
        R["mixed_f"][:, pl.ds(j, 256)] = dt0 + v

    project(mine, put_own)
    m_swap.wait()

    def mix_tile(t0):
        r = pl.ds(t0, 16)
        R["mixed"][r, :] = (R["mixed_f"][r, :] + mrecv[r, :].astype(F32)).astype(BF)

    tiles(rows, mix_tile, 16)

    steps_b = s_o[1:9] + s_g[1:3] + [s_o[9]] + [s_g[3], s_g[4], s_g[5], s_g[6], s_g[7], s_g[8], s_g[9]]
    n_chunks = total // CH
    st[...] = jnp.zeros_like(st)
    racc[...] = jnp.zeros_like(racc)

    def read_back(blk, slot):
        return pltpu.make_async_copy(kept(blk), hbuf.at[slot], hsem.at[slot])

    def b_block(i, _):
        blk = n_blk - 1 - i
        slot = lax.rem(blk, 2)

        def chunk(p, _):
            q = hq - 1 - p
            c = blk * hq + q
            t0 = pl.multiple_of(c * CH, CH)
            done = i * hq + p
            for k, s in enumerate(steps_b):
                pl.when(done == 1 + (5 * k) // 2)(s)

            @pl.when((q == 0) & (blk >= 1) & (blk <= n_blk - 2))
            def _():
                read_back(blk - 1, 1 - slot).wait()

            before = jnp.where(q == 0, 1 - slot, slot)
            last = pl.multiple_of(jnp.where(q == 0, hp - 1, q * CH - 1) * N, N)
            ct = ctc[c]
            first = offs[pl.ds(t0, CH), :] == 0.0
            hb = hbuf.at[slot, pl.ds(pl.multiple_of(q * CH * N, CH * N), CH * N), :]
            hl = hbuf.at[before, pl.ds(last, N), :]
            for g in range(half // lg):
                ls = lane(g, lg)
                a = a2[:, ls]
                carry = st[:, ls]
                ra = racc[:, ls]
                ds, gs = jnp.where(jnp.concatenate([first] * (lg // 128), axis=1), BIG, dt[pl.ds(t0, CH), ls]), y[pl.ds(t0, CH), ls]
                for k in range(CH - 1, -1, -1):
                    d = jnp.broadcast_to(ds[k:k + 1], (N, lg))
                    gg = jnp.broadcast_to(gs[k:k + 1], (N, lg))
                    cc = jnp.broadcast_to(ct[:, k:k + 1], (N, lg))
                    h = hb[(k - 1) * N:k * N, ls] if k else hl[:, ls]
                    sg = cc * gg + carry
                    carry = jnp.exp2(d * a) * sg
                    term = carry * h.astype(F32)
                    ra = ra + term * d
                    sgs[k * N:(k + 1) * N, ls] = sg.astype(BF)
                    part = term * a
                    part = part[:N // 2] + part[N // 2:]
                    if k % 2:
                        odd = part
                    else:
                        das[k * N // 2:(k + 2) * N // 2, ls] = jnp.concatenate([part, odd], axis=0).astype(BF)
                st[:, ls] = carry
                racc[:, ls] = ra
            m = block_mask()
            m8 = jnp.where(lax.broadcasted_iota(jnp.int32, (CH, CH * N // 2), 1) // (N // 2)
                           == lax.broadcasted_iota(jnp.int32, (CH, CH * N // 2), 0), 1.0, 0.0).astype(BF)
            r = pl.ds(t0, CH)
            sgc = sgs[...]
            wout = dot(dx[r, :].astype(BF), sgc, NT)
            wgs[pl.ds(c, 1), :] = jnp.sum(jnp.where(m, wout, 0.0), axis=0, keepdims=True)
            rout = dot(y[r, :].astype(BF), hb[...], NT)
            rgs[pl.ds(c, 1), :] = jnp.sum(jnp.where(m, rout, 0.0), axis=0, keepdims=True)
            dx[r, :] = dot(bblk[r, :], sgc)
            gt[r, :] = dot(m8, das[...])
            return 0

        lax.fori_loop(0, hq, chunk, 0)

        @pl.when(blk >= 2)
        def _():
            read_back(blk - 2, slot).start()

        return 0

    lax.fori_loop(0, n_blk, b_block, 0)
    dg, low_b = dx, gated

    fins = [links.swap(R[k], R[k + "2"], sw_s.at[10 + n], sw_r.at[10 + n])
            for n, k in enumerate(("red_i", "red_g", "red_o"))]
    fins[1].start()
    fins[2].start()

    ln2 = math.log(2.0)

    def pre_tile(t0):
        r = pl.ds(t0, 64)
        for b in range(lanes):
            c = lane(b)
            cv = conv[r, c]
            act = cv * sigmoid(cv)
            v = (dg[r, c] * act + gt[r, c] * ln2) * (1.0 - jnp.exp(-dt[r, c]))
            low_b[r, c] = v.astype(BF)
            accs[1, :, c] += eighths(v)

    tiles(total, pre_tile, 64)

    def xg_tile(i, _):
        t0 = pl.multiple_of(i * 128, 128)
        r = pl.ds(t0, 128)
        m = block_mask(128)
        sums = dot(low_b[r, :], delta[...], NT)
        for ref, first in ((wgs, rank), (rgs, rank + N)):
            v = ref[pl.ds(pl.multiple_of(i * per, per), per), :]
            v = jnp.broadcast_to(v[:, None, :], (per, CH, CH * N)).reshape(128, CH * N)
            v = jnp.where(m, v, 0.0)
            hi = v.astype(BF)
            lo = (v - hi.astype(F32)).astype(BF)
            p = place(first)
            sums = sums + dot(hi, p) + dot(lo, p)
        xg[r, :] = sums
        return 0

    lax.fori_loop(0, total // 128, xg_tile, 0)
    g_swap = links.swap(xg, xr, sw_s.at[6], sw_r.at[6])
    g_swap.start()
    sgrad = R["sgrad"]
    xob = xo[...].astype(BF)
    for b in range(half // 256):
        sgrad[1, :, lane(b, 256)] = dot(xob, low_b[:, lane(b, 256)], TN)
    g_swap.wait()
    xg[...] = xg[...] + xr[...]
    xgb = xg[...].astype(BF)
    for b in range(half // 256):
        sgrad[0, :, lane(b, 256)] = dot(xgb, actl[:, lane(b, 256)], TN)

    quarter = half // 2
    ig = gated
    d_in = ww
    y[pl.ds(total, 8), :] = jnp.zeros((8, half), F32)

    def conv_back(h):
        def cg_tile(t0):
            r = pl.ds(t0, 64)
            low = xg[r, :].astype(BF)
            for b in range(h * quarter // 256, (h + 1) * quarter // 256):
                back = dot(low, select[:, lane(b, 256)])
                for q in range(2):
                    c = lane(2 * b + q)
                    ag = y[r, c] * par[r_sk:r_sk + 1, c] + dg[r, c] * dt[r, c] + back[:, lane(q)]
                    cv = conv[r, c]
                    v = ag * slope(cv, sigmoid(cv))
                    y[r, c] = v
                    accs[2, :, c] += eighths(v)

        tiles(total, cg_tile, 64)

        def ig_tile(t0):
            o = offs[pl.ds(t0, 72), :]
            for b in range(h * quarter // 128, (h + 1) * quarter // 128):
                c = lane(b)
                v = y[pl.ds(t0, 72), c]
                x = xin[pl.ds(t0, 72), c]
                acc = jnp.zeros((64, 128), F32)
                for j in range(taps):
                    mv = jnp.where(o >= float(j), v, 0.0) if j else v
                    accs[3 + taps - 1 - j, :, c] += eighths(mv[0:64] * x[8 - j:72 - j])
                    acc = acc + mv[j:64 + j] * par[r_taps + taps - 1 - j:r_taps + taps - j, c]
                ig[pl.ds(t0, 64), c] = acc.astype(BF)

        tiles(total, ig_tile, 64)

        def outer_tile(i, _):
            v = dot(normed[:, pl.ds(pl.multiple_of(i * 256, 256), 256)], ig[:, lane(h, quarter)], TN).astype(BF)
            n = 256 // own_d
            for q in range(n):
                r = pl.ds(pl.multiple_of((i * n + q) * pitch_w, pitch_w) + own_d, own_d)
                d_in[r, lane(h, quarter)] = v[q * own_d:(q + 1) * own_d]
            return 0

        lax.fori_loop(0, width // 256, outer_tile, 0)

    def half_scatter(h):
        def part(ref):
            return ref.at[(slice(None),) * (len(ref.shape) - 1) + (lane(h, quarter),)]
        bufs = [part(b) for b in R["so_b"]] if near else [R[("so_b", "sg_b")[h]][0].at[:, :, lane(h, quarter)], None, None]
        return scatter_steps(links, part(d_in), part(R["red_i"]), bufs, R["si_s" if h == 0 else "sj_s"], R["si_r" if h == 0 else "sj_r"], own_d)

    s_i, s_j = half_scatter(0), half_scatter(1)
    conv_back(0)
    s_i[0]()
    conv_back(1)
    s_j[0]()
    s_i[1]()
    s_i[2]()
    s_i[3]()
    s_i[4]()

    def back_project(which, out):
        def body(i, _):
            out(pl.multiple_of(i * 256, 256),
                dot(ig[which, :], rows_of(wi, 0, i), NT) + dot(ggr[which, :], rows_of(ww, 0, i), NT))
            return 0
        lax.fori_loop(0, width // 256, body, 0)

    back_project(other, put_send)
    n_swap = links.swap(msend, mrecv, sw_s.at[7], sw_r.at[7])
    n_swap.start()
    s_i[5]()
    s_i[6]()
    s_j[1]()
    s_j[2]()
    ng = R["mixed_f"]

    def put_ng(j, v):
        ng[:, pl.ds(j, 256)] = v

    back_project(mine, put_ng)

    vecs = jnp.concatenate(
        [racc[...] * a2[...] * ln2]
        + [jnp.sum(accs[3 + k], axis=0, keepdims=True) for k in range(taps)]
        + [jnp.sum(accs[2], axis=0, keepdims=True), jnp.sum(accs[1], axis=0, keepdims=True),
           jnp.sum(accs[0], axis=0, keepdims=True), jnp.zeros((16 - taps - 3, half), F32)], axis=0)
    sgrad[0, c1:128, :] = vecs
    sgrad[1, rank:128, :] = jnp.zeros((128 - rank, half), F32)
    if near:
        small, away = R["small"], R["away"]
        for b in range(lanes):
            small[pl.ds(own + b * 128, 128), :] = sgrad[core, :, lane(b)].astype(BF)
            away[lane(b), :] = sgrad[1 - core, :, lane(b)].astype(BF)
        a_swap = links.swap(away, small.at[pl.ds(own, half), :], sw_s.at[8], sw_r.at[8])
        a_swap.start()
        red_s = R["o_small"]
        s_s = scatter_steps(links, small, red_s.at[core], R["ss_b"], R["ss_s"], R["ss_r"])
    else:
        s_s = [lambda: None] * 10
    s_i[7]()
    s_i[8]()
    s_j[3]()
    s_j[4]()
    if near:
        a_swap.wait()
    s_s[0]()
    n_swap.wait()
    def tok_tile(t0):
        r = pl.ds(t0, 32)
        v = tok[r, :].astype(F32)
        inv = lax.rsqrt(jnp.mean(v * v, axis=-1, keepdims=True) + EPS)
        sc = v * inv
        n = ng[r, :] + mrecv[r, :].astype(F32)
        sg = n * gain
        ng[r, :] = cots[pl.ds(pl.multiple_of(core * rows + t0, 32), 32), :].astype(F32) + inv * (
            sg - sc * jnp.mean(sg * sc, axis=-1, keepdims=True))

    tiles(rows, tok_tile, 32)
    t_copy = pltpu.make_async_copy(ng, R["tgrad"], lsem.at[1])
    t_copy.start()
    s_j[5]()
    s_s[1]()
    s_s[2]()
    s_j[6]()
    if not near:
        R["f_grad"][...] = sgrad[...]
    s_i[9]()
    s_j[7]()
    for k in range(3, 7):
        s_s[k]()
    s_j[8]()
    for k in range(7, 10):
        s_s[k]()
    if near:
        fs = links.swap(red_s.at[core], red_s.at[core], sw_s.at[9], sw_r.at[9])
        fs.start()
    s_j[9]()
    t_copy.wait()

    fins[0].start()

    def share(first, k, out):
        R[out][:, pl.ds(pl.multiple_of(first + core * half, 128), half)] = R[k][...]
        R[out][:, pl.ds(pl.multiple_of(first + (1 - core) * half, 128), half)] = R[k + "2"][...]

    fins[1].wait()
    share(inner, "red_g", "o_in")
    fins[2].wait()
    share(0, "red_o", "o_out")
    if near:
        fs.wait()
    fins[0].wait()
    share(0, "red_i", "o_in")


def layer(inputs, dp, dims):
    rows, width = inputs["tok"].shape
    half = inputs["w_o"].shape[1] // 2
    inner = 2 * half
    total = 2 * rows
    taps, rank = dims
    own_d, own_e = width // dp, inner // dp
    n = copies_of(dp)
    near = bool(plane(dp))
    extra = 16 if near else 0
    sd = jax.ShapeDtypeStruct
    vm = pl.BlockSpec(memory_space=pltpu.VMEM)
    hbm = pl.BlockSpec(memory_space=pl.ANY)
    dma = pltpu.SemaphoreType.DMA
    V = pltpu.VMEM
    outs = {
        "mixed": sd((rows, width), BF), "tgrad": sd((rows, width), F32),
        "o_in": sd((own_d, 2 * inner), F32), "o_out": sd((own_d, inner), F32), "hs": sd((total * N, half), BF),
    }
    if near:
        outs["o_small"] = sd((2, 128, own_e), F32)
    else:
        outs["f_grad"] = sd((2, 128, half), F32)
    f2 = V((total, half), F32)
    scratch = {
        "part_i": V((own_d + extra, half), BF), "part_w": V((2 * own_d, half), BF),
        "wi": V((dp * (own_d + extra), half), BF), "ww": V((2 * width, half), BF), "select": V((128, half), BF), "delta": V((128, half), BF),
        "toks": V((total, width), BF), "cots": V((total, width), BF), "normed": V((total, width), BF),
        "offs": V((total + 8, 128), F32), "xin": V((total + 8, half), F32), "conv": f2, "actl": V((total, half), BF),
        "dt": f2, "gt": f2, "dx": f2, "y": V((total + 8, half), F32), "ggr": V((total, half), BF),
        "xo": V((total, 128), F32), "xr": V((total, 128), F32), "xg": V((total, 128), F32),
        "hbuf": V((2, 64 * N, half), BF), "par": V((128, half), F32),
        "btc": V((total // CH, N, CH), F32), "ctc": V((total // CH, N, CH), F32),
        "cblk": V((total, CH * N), BF), "bblk": V((total, CH * N), BF),
        "a2": V((N, half), F32), "st": V((N, half), F32), "racc": V((N, half), F32),
        "qtmp": V((total, 256), F32),
        "sgs": V((CH * N, half), BF), "das": V((CH * N // 2, half), BF),
        "wgs": V((total // CH, CH * N), F32), "rgs": V((total // CH, CH * N), F32),
        "accs": V((3 + taps, 8, half), F32), "d_out": V((width, half), BF), "d_gate": V((width, half), BF),
        "msend": V((rows, width), BF), "mrecv": V((rows, width), BF), "mixed_f": V((rows, width), F32),
        "sgrad": V((2, 128, half), F32),
        "so_b": scatter_scratch(dp, own_d, half), "sg_b": scatter_scratch(dp, own_d, half),
        "sw_s": dma((13,)), "sw_r": dma((13,)), "hsem": dma((2,)), "lsem": dma((2,)),
    }
    for k in ("i", "g", "o"):
        scratch["red_" + k] = V((own_d, half), F32)
        scratch["red_" + k + "2"] = V((own_d, half), F32)
    if near:
        scratch["sm"] = V((2, inner, own_e), BF)
        scratch["small"], scratch["away"] = V((inner, own_e), BF), V((half, own_e), BF)
        scratch["ss_b"] = scatter_scratch(dp, 128, own_e)
    for k in ("gi", "gw", "si", "sj", "sg", "so", "ss"):
        scratch[k + "_s"] = dma((n,))
        scratch[k + "_r"] = dma((n,))
    names = list(inputs) + list(outs) + list(scratch)
    res = pl.pallas_call(
        functools.partial(layer_kernel, dp=dp, dims=dims, names=names),
        out_shape=list(outs.values()),
        in_specs=[pl.BlockSpec(memory_space=pltpu.SMEM) if k == "lens" else hbm if k == "cot" else vm for k in inputs],
        out_specs=[hbm if k in ("tgrad", "hs") else vm for k in outs],
        scratch_shapes=list(scratch.values()),
        compiler_params=pltpu.CompilerParams(collective_id=0, has_side_effects=True, vmem_limit_bytes=127 << 19),
        name="layer",
    )(*inputs.values())
    return dict(zip(outs, res))


def local(
    tokens,
    doc_lengths,
    cotangent,
    norm_gain,
    input_weight,
    filter_weight,
    filter_bias,
    select_weight,
    delta_weight,
    delta_bias,
    decay_log,
    skip_gain,
    output_weight,
    *,
    dp,
):
    rows, length, width = tokens.shape
    rank = delta_weight.shape[1]
    taps = filter_weight.shape[1]
    own_e = filter_weight.shape[0]
    own_d = norm_gain.shape[0]
    inner = own_e * dp
    c1 = rank + 2 * N
    inputs = {
        "lens": doc_lengths, "tok": tokens.reshape(rows * length, width), "cot": cotangent.reshape(rows * length, width),
        "w_in": input_weight, "w_o": output_weight,
    }
    if plane(dp):
        inputs.update(
            s_select=select_weight.T, s_decay=decay_log.T, s_delta=delta_weight.T, s_filter=filter_weight.T,
            s_fb=filter_bias[None], s_db=delta_bias[None], s_skip=skip_gain[None], s_gain=norm_gain[None],
        )
    else:
        core = lax.axis_index("rep")
        vectors = jnp.stack([filter_bias, delta_bias, skip_gain])
        tail = jnp.concatenate([filter_weight.T, vectors, jnp.zeros((16 - taps - 3, own_e), BF)], axis=0)
        one = jnp.concatenate([select_weight.T, decay_log.T, tail], axis=0)
        two = jnp.concatenate([delta_weight.T, jnp.zeros((128 - rank, own_e), BF)], axis=0)
        both = lax.all_gather(jnp.stack([one, two]), "dp", axis=2, tiled=True)
        both = lax.dynamic_slice(both, (0, 0, core * (inner // 2)), (2, 128, inner // 2))
        inputs.update(f_one=both[0], f_two=both[1], f_gain=lax.all_gather(norm_gain, "dp", axis=0, tiled=True)[None])
    r = layer(inputs, dp, (taps, rank))
    if plane(dp):
        small = r["o_small"]
    else:
        small = lax.all_gather(r["f_grad"], "rep", axis=2, tiled=True)
        small = lax.psum_scatter(small, "dp", scatter_dimension=2, tiled=True)
    o = finish(r["mixed"], r["tgrad"], r["o_in"], r["o_out"], small, input_weight, norm_gain[None], (taps, rank))
    return (
        o[0].reshape(rows, length, width),
        o[1].reshape(rows, length, width),
        o[4].reshape(own_d),
        o[2],
        o[5].T,
        o[6].reshape(own_e),
        o[7].T,
        o[8].T,
        o[9].reshape(own_e),
        o[10].T,
        o[11].reshape(own_e),
        o[3],
    )


def finish(mixed, tgrad, o_in, o_out, small, w_in, gain, dims):
    taps, rank = dims
    c1 = rank + 2 * N
    own_e, own_d = small.shape[2], w_in.shape[0]
    sd = jax.ShapeDtypeStruct
    big = [mixed, tgrad, o_in, o_out]
    parts = 4

    def kernel(*refs):
        ins, small_ref, w_ref, gain_ref, outs, acc = refs[:4], refs[4], refs[5], refs[6], refs[7:19], refs[19]
        for i, o in zip(ins, outs[:4]):
            o[...] = i[...]
        p = w_ref[...].astype(F32) * ins[2][...]
        total = p[:, 0:128]
        for b in range(1, p.shape[1] // 128):
            total = total + p[:, b * 128:(b + 1) * 128]
        g = c1 + N + taps + 3

        @pl.when(pl.program_id(0) == 0)
        def _():
            acc[...] = jnp.zeros_like(acc)
            outs[5][...] = small_ref[0, c1 + N:c1 + N + taps, :]
            outs[6][...] = small_ref[0, g - 3:g - 2, :]
            outs[7][...] = small_ref[0, 0:c1, :]
            outs[8][...] = small_ref[1, 0:rank, :]
            outs[9][...] = small_ref[0, g - 2:g - 1, :]
            outs[10][...] = small_ref[0, c1:c1 + N, :]
            outs[11][...] = small_ref[0, g - 1:g, :]

        acc[0:own_d, :] += total

        @pl.when(pl.program_id(0) == parts - 1)
        def _():
            row = jnp.sum(acc[...].T, axis=0, keepdims=True)[:, :own_d]
            outs[4][...] = row / gain_ref[...].astype(F32)

    shapes = [sd(b.shape, b.dtype) for b in big] + [
        sd(s, F32) for s in ((1, own_d), (taps, own_e), (1, own_e), (c1, own_e), (rank, own_e), (1, own_e), (N, own_e), (1, own_e))]
    specs = [pl.BlockSpec((b.shape[0], b.shape[1] // parts), lambda i: (0, i)) for b in big]

    def whole(s):
        return pl.BlockSpec(s.shape, lambda i, n=len(s.shape): (0,) * n)

    wide = pl.BlockSpec((own_d, w_in.shape[1] // parts), lambda i: (0, i))
    return pl.pallas_call(
        kernel, grid=(parts,), out_shape=shapes, in_specs=specs + [whole(small), wide, whole(gain)],
        out_specs=specs + [whole(s) for s in shapes[4:]], scratch_shapes=[pltpu.VMEM((128, 128), F32)], name="finish",
    )(*big, small, w_in, gain)


def solution(mesh):
    dp_rep = ("dp", "rep")
    one = P("dp")
    two = P("dp", None)
    three = P(dp_rep, None, None)
    return jax.shard_map(
        functools.partial(local, dp=mesh.shape["dp"]),
        mesh=mesh,
        in_specs=(three, P(dp_rep, None), three, one, two, two, one, two, two, one, two, one, two),
        out_specs=(three, three, one, two, two, one, two, two, one, two, one, two),
        check_vma=False,
    )
```

```python
import functools
import math

import jax
import jax.numpy as jnp
from jax import lax
from jax.experimental import pallas as pl
from jax.experimental.pallas import tpu as pltpu
from jax.sharding import PartitionSpec as P

EPS = 1e-05
CH = 16
N = 16
F32 = jnp.float32
BF = jnp.bfloat16
NT = (((1,), (1,)), ((), ()))
TN = (((0,), (0,)), ((), ()))
BIG = 1e30
LOG2E = math.log2(math.e)


def dot(a, b, dims=(((1,), (0,)), ((), ()))):
    return lax.dot_general(a, b, dims, preferred_element_type=F32)


MESH = pl.DeviceIdType.MESH


def plane(dp):
    return 4 if dp == 16 else 0


class Links:
    def __init__(self, dp):
        self.dp = dp
        self.depth = plane(dp)
        self.me = lax.axis_index("dp")
        self.core = lax.axis_index("rep")
        if self.depth:
            self.z, self.y, self.x = self.me // 4, (self.me // 2) % 2, self.me % 2
            self.xn = self.at(self.z, self.y, 1 - self.x)
            self.yn = self.at(self.z, 1 - self.y, self.x)
            self.zs = [self.at(self.up(k), self.y, self.x) for k in range(1, self.depth)]
            self.peers = self.zs + [self.xn, self.yn]
        else:
            self.peers = [lax.rem(self.me + k, dp) for k in range(1, dp)]

    def up(self, k):
        return lax.rem(self.z + k, self.depth)

    def down(self, k):
        return lax.rem(self.z + self.depth - k, self.depth)

    def at(self, z, y, x):
        return (z * 2 + y) * 2 + x

    def barrier(self, sibling=True):
        sem = pltpu.get_barrier_semaphore()
        for peer in self.peers:
            pl.semaphore_signal(sem, inc=1, device_id=(peer, self.core), device_id_type=MESH)
        if sibling:
            pl.semaphore_signal(sem, inc=1, device_id=(self.me, 1 - self.core), device_id_type=MESH)
        pl.semaphore_wait(sem, len(self.peers) + int(sibling))

    def send(self, src, dst, send_sem, recv_sem, chip):
        return pltpu.make_async_remote_copy(
            src_ref=src, dst_ref=dst, send_sem=send_sem, recv_sem=recv_sem,
            device_id=(chip, self.core), device_id_type=MESH,
        )

    def swap(self, src, dst, send_sem, recv_sem):
        return pltpu.make_async_remote_copy(
            src_ref=src, dst_ref=dst, send_sem=send_sem, recv_sem=recv_sem,
            device_id=(self.me, 1 - self.core), device_id_type=MESH,
        )


def copies_of(dp):
    return 34 if plane(dp) else dp - 1


def gather_steps(links, src, dst, ss, rs):
    me = links.me
    rows = src.shape[0]

    def part(b, first=0, count=rows):
        return pl.ds(pl.multiple_of(b * rows + first, math.gcd(rows, count)), count)

    if not links.depth:
        cps = [links.send(src, dst.at[part(me)], ss.at[k], rs.at[k], p) for k, p in enumerate(links.peers)]

        def begin():
            for c in cps:
                c.start()
            dst[part(me), :] = src[...]

        def end():
            for c in cps:
                c.wait()

        return [begin] + [lambda: None] * 14 + [end]
    depth, half = links.depth, rows // 2
    cuts = [half if half % 16 == 0 else half + (8 if i % 2 else -8) for i in range(2 * depth - 1)]
    z, y, x, xn, yn = links.z, links.y, links.x, links.xn, links.yn
    origin = [z] + [jnp.maximum(z - d, 0) for d in range(1, depth)] + [jnp.minimum(z + d, depth - 1) for d in range(1, depth)]
    there = [z >= 0] + [z >= d for d in range(1, depth)] + [z + d < depth for d in range(1, depth)]
    up, down, up_on, down_on = {}, {}, {}, {}
    above, below = links.at(jnp.minimum(z + 1, depth - 1), y, x), links.at(jnp.maximum(z - 1, 0), y, x)
    for d in range(1, depth):
        b = links.at(origin[d - 1], y, x)
        s = src if d == 1 else dst.at[part(b)]
        up[d] = links.send(s, dst.at[part(b)], ss.at[d - 1], rs.at[d - 1], above)
        up_on[d] = (z < depth - 1) & (z >= d - 1)
        b = links.at(origin[0 if d == 1 else d + 2], y, x)
        s = src if d == 1 else dst.at[part(b)]
        down[d] = links.send(s, dst.at[part(b)], ss.at[d + 2], rs.at[d + 2], below)
        down_on[d] = (z > 0) & (z + d - 1 < depth)
    xc, yc, xf, yf = [], [], [], []
    for i in range(2 * depth - 1):
        b = links.at(origin[i], y, x)
        s = src if i == 0 else dst.at[part(b)]
        n = 6 + 4 * i
        xc.append(links.send(s, dst.at[part(b)], ss.at[n], rs.at[n], xn))
        yc.append(links.send(s, dst.at[part(b)], ss.at[n + 1], rs.at[n + 1], yn))
        lo = dst.at[part(links.at(origin[i], y, 1 - x), 0, cuts[i])]
        hi = dst.at[part(links.at(origin[i], 1 - y, x), cuts[i], rows - cuts[i])]
        yf.append(links.send(lo, lo, ss.at[n + 2], rs.at[n + 2], yn))
        xf.append(links.send(hi, hi, ss.at[n + 3], rs.at[n + 3], xn))

    def begin():
        pl.when(up_on[1])(up[1].start)
        pl.when(down_on[1])(down[1].start)

    def beside():
        xc[0].start()
        yc[0].start()
        dst[part(me), :] = src[...]

    def spread(i):
        chain, on, d = (up, up_on, i) if i < depth else (down, down_on, i - depth + 1)

        def run():
            @pl.when(there[i])
            def _():
                chain[d].wait_recv()
                if d + 1 < depth:
                    pl.when(on[d + 1])(chain[d + 1].start)
                xc[i].start()
                yc[i].start()
        return run

    def forward(i):
        def run():
            @pl.when(there[i])
            def _():
                xc[i].wait_recv()
                yf[i].start()
                yc[i].wait_recv()
                xf[i].start()
        return run

    def end():
        for i in range(2 * depth - 1):
            @pl.when(there[i])
            def _(i=i):
                yf[i].wait_recv()
                xf[i].wait_recv()
                for c in (xc[i], yc[i], xf[i], yf[i]):
                    c.wait_send()
        for d in range(1, depth):
            pl.when(up_on[d])(up[d].wait_send)
            pl.when(down_on[d])(down[d].wait_send)

    f = forward
    return [begin, beside] + [spread(i) for i in (1, 4, 2, 5, 3, 6)] + [f(i) for i in (0, 1, 4, 2, 5, 3, 6)] + [end]


def scatter_scratch(dp, rows, cols):
    if not plane(dp):
        return [pltpu.VMEM((dp - 1, rows, cols), BF)] + [pltpu.VMEM((8, 128), BF)] * 2
    d, h = plane(dp), rows // 2
    return [
        pltpu.VMEM((d, 2, h, cols), BF),
        pltpu.VMEM((d, 2, rows, cols), BF),
        pltpu.VMEM((d - 1, rows, cols), BF),
    ]


def scatter_steps(links, src, out, bufs, ss, rs, offset=0):
    me = links.me
    rows = out.shape[0]
    pitch = src.shape[0] // links.dp

    def part(b, first=0, count=rows):
        return pl.ds(pl.multiple_of(b * pitch + offset + first, math.gcd(math.gcd(pitch, offset + first), count)), count)

    if not links.depth:
        got = bufs[0]
        cps = [links.send(src.at[part(p)], got.at[k], ss.at[k], rs.at[k], p) for k, p in enumerate(links.peers)]

        def begin():
            for c in cps:
                c.start()

        def end():
            for c in cps:
                c.wait()

            def add(k, total):
                return total + got[k].astype(F32)

            out[...] = lax.fori_loop(0, links.dp - 1, add, src[part(me), :].astype(F32))

        return [begin] + [lambda: None] * 8 + [end]
    halves, come, zcome = bufs
    depth = links.depth
    h = rows // 2
    y, x, xn, yn = links.y, links.x, links.xn, links.yn
    ac, bc, cc = [], [], []
    for k in range(depth):
        zz = links.up(k)
        diag = links.at(zz, 1 - y, 1 - x)
        bx = links.at(zz, y, 1 - x)
        by = links.at(zz, 1 - y, x)
        own = links.at(zz, y, x)
        n = 4 * k
        ac.append((
            links.send(src.at[part(diag, 0, h)], halves.at[k, 0], ss.at[n], rs.at[n], xn),
            links.send(src.at[part(diag, h, h)], halves.at[k, 1], ss.at[n + 1], rs.at[n + 1], yn),
        ))
        bc.append((
            links.send(src.at[part(bx)], come.at[k, 0], ss.at[n + 2], rs.at[n + 2], xn),
            links.send(src.at[part(by)], come.at[k, 1], ss.at[n + 3], rs.at[n + 3], yn),
        ))
        if k:
            n = 4 * depth + k - 1
            cc.append(links.send(src.at[part(own)], zcome.at[k - 1], ss.at[n], rs.at[n], links.zs[k - 1]))

    def add(where, more):
        src[where, :] = (src[where, :].astype(F32) + more.astype(F32)).astype(BF)

    def begin():
        for k in (1, 2, 3, 0):
            ac[k][0].start()
            ac[k][1].start()

    def middle(k):
        def run():
            zz = links.up(k)
            ac[k][0].wait_recv()
            add(part(links.at(zz, 1 - y, x), 0, h), halves[k, 0])
            bc[k][1].start()
            ac[k][1].wait_recv()
            add(part(links.at(zz, y, 1 - x), h, h), halves[k, 1])
            bc[k][0].start()
        return run

    def along(k):
        def run():
            bc[k][0].wait_recv()
            bc[k][1].wait_recv()
            own = part(links.at(links.up(k), y, x))
            total = src[own, :].astype(F32) + come[k, 0].astype(F32) + come[k, 1].astype(F32)
            if k:
                src[own, :] = total.astype(BF)
                cc[k - 1].start()
            else:
                out[...] = total
        return run

    def end():
        for k in range(depth - 1):
            cc[k].wait_recv()
            out[...] += zcome[k].astype(F32)
        for k in range(depth):
            for c in ac[k] + bc[k]:
                c.wait_send()
        for c in cc:
            c.wait_send()

    return [begin, middle(1), middle(2), along(1), middle(3), along(2), middle(0), along(3), along(0), end]


def sigmoid(v):
    return 0.5 * jnp.tanh(0.5 * v) + 0.5


def softplus(v):
    u = jnp.exp(-jnp.abs(v))
    return jnp.maximum(v, 0.0) + jnp.where(u < 1e-3, u * (1.0 - 0.5 * u), jnp.log(1.0 + u))


def slope(v, s):
    return s * (1.0 + v * (1.0 - s))


def block_mask(rows=CH):
    r = lax.broadcasted_iota(jnp.int32, (rows, CH * N), 0)
    c = lax.broadcasted_iota(jnp.int32, (rows, CH * N), 1)
    return (c // N) == (r % CH)


def pick(first):
    r = lax.broadcasted_iota(jnp.int32, (128, CH * N), 0)
    c = lax.broadcasted_iota(jnp.int32, (128, CH * N), 1)
    return jnp.where(r - first == c % N, 1.0, 0.0).astype(BF)


def place(first):
    r = lax.broadcasted_iota(jnp.int32, (CH * N, 128), 0)
    c = lax.broadcasted_iota(jnp.int32, (CH * N, 128), 1)
    return jnp.where(c - first == r % N, 1.0, 0.0).astype(BF)


def eighths(v):
    return jnp.sum(v.reshape(v.shape[0] // 8, 8, v.shape[1]), axis=0)


def layer_kernel(*refs, dp, dims, names):
    R = dict(zip(names, refs))
    lens, tok, cot, w_in, w_o = (R[k] for k in ("lens", "tok", "cot", "w_in", "w_o"))
    wi, ww, toks, cots, normed = (R[k] for k in ("wi", "ww", "toks", "cots", "normed"))
    select, delta = R["select"], R["delta"]
    offs, xin, conv, actl, dt, gt, dx, y = (R[k] for k in ("offs", "xin", "conv", "actl", "dt", "gt", "dx", "y"))
    ggr, xo, xr, hs, hbuf = (R[k] for k in ("ggr", "xo", "xr", "hs", "hbuf"))
    par, btc, ctc, cblk, bblk, a2, st, racc = (R[k] for k in ("par", "btc", "ctc", "cblk", "bblk", "a2", "st", "racc"))
    qtmp, sgs, das, wgs, rgs, accs = (R[k] for k in ("qtmp", "sgs", "das", "wgs", "rgs", "accs"))
    d_out, d_gate, msend, mrecv, sw_s, sw_r, hsem, lsem = (
        R[k] for k in ("d_out", "d_gate", "msend", "mrecv", "sw_s", "sw_r", "hsem", "lsem"))
    taps, rank = dims
    links = Links(dp)
    core, me = links.core, links.me
    rows, width = tok.shape
    half = wi.shape[1]
    total = 2 * rows
    own_d = w_in.shape[0]
    inner = 2 * half
    own_e = inner // dp
    lanes = half // 128
    c1 = rank + 2 * N
    r_taps, r_fb, r_db, r_sk, gcol = (c1 + N + k for k in (0, taps, taps + 1, taps + 2, taps + 3))
    gated = toks

    def cut(ref, start):
        return ref[:, pl.ds(pl.multiple_of(start + core * half, 128), half)]

    pitch_i, pitch_w = wi.shape[0] // dp, 2 * own_d

    def cols_of(ref, first, c):
        v = ref[:, c]
        return v.reshape(dp, ref.shape[0] // dp, v.shape[1])[:, first:first + own_d].reshape(width, v.shape[1])

    def rows_of(ref, first, i):
        n = 256 // own_d
        p = ref.shape[0] // dp
        v = ref[pl.ds(pl.multiple_of(i * n * p, n * p), n * p), :]
        return v.reshape(n, p, half)[:, first:first + own_d].reshape(256, half)

    def lane(b, n=128):
        return slice(b * n, (b + 1) * n)

    def tiles(n, body, size, start=0):
        def run(i, _):
            body(pl.multiple_of(i * size, size))
            return 0
        lax.fori_loop(start // size, n // size, run, 0)

    near = bool(links.depth)
    part_i, part_w = R["part_i"], R["part_w"]
    part_i[0:own_d, :] = cut(w_in, 0)
    part_w[0:own_d, :] = cut(w_in, inner)
    part_w[own_d:, :] = cut(w_o, 0)
    if near:
        sm = R["sm"]
        tail = jnp.concatenate(
            [R[k][...].astype(F32) for k in ("s_filter", "s_fb", "s_db", "s_skip")]
            + [jnp.concatenate([R["s_gain"][...].astype(F32), jnp.zeros((1, own_e - own_d), F32)], axis=1),
               jnp.zeros((16 - taps - 4, own_e), F32)], axis=0).astype(BF)
        for q in range(8):
            one = R["s_select"][q * 16:q * 16 + 16, :] if q < c1 // 16 else R["s_decay"][...] if q < 7 else tail
            two = R["s_delta"][q * 16:q * 16 + 16, :] if q < rank // 16 else tail
            part_i[own_d:own_d + 16, lane(q)] = jnp.where(core == 0, one.astype(F32), two.astype(F32)).astype(BF)
    links.barrier()
    mine = pl.ds(pl.multiple_of(core * rows, rows), rows)
    other = pl.ds(pl.multiple_of((1 - core) * rows, rows), rows)
    t_idx = lax.broadcasted_iota(jnp.int32, (rows, 128), 0)
    begin = jnp.zeros((rows, 128), jnp.int32)
    start = lens[0, 0]
    for k in range(1, lens.shape[1]):
        begin = jnp.where(t_idx >= start, start, begin)
        start = start + lens[0, k]
    offs[mine, :] = (t_idx - begin).astype(F32)
    offs[pl.ds(total, 8), :] = jnp.zeros((8, 128), F32)
    t_swap = links.swap(tok, toks.at[mine], sw_s.at[0], sw_r.at[0])
    o_swap = links.swap(offs.at[mine], offs.at[mine], sw_s.at[1], sw_r.at[1])
    c_swap = links.swap(cot, cots.at[mine], sw_s.at[2], sw_r.at[2])
    c_copy = pltpu.make_async_copy(cot, cots.at[mine], lsem.at[0])
    g_i = gather_steps(links, part_i, wi, R["gi_s"], R["gi_r"])
    g_w = gather_steps(links, part_w, ww, R["gw_s"], R["gw_r"])
    g_i[0]()
    g_i[1]()
    t_swap.start()
    o_swap.start()
    toks[mine, :] = tok[...]
    for k in range(2, 8):
        g_i[k]()
    g_w[0]()
    for k in range(8, 15):
        g_i[k]()
    for k in range(1, 8):
        g_w[k]()
    g_i[15]()
    if near:
        for i in range(dp):
            for q in range(8):
                sm[core, i * 128 + q * 16:i * 128 + q * 16 + 16, :] = wi[i * pitch_i + own_d:i * pitch_i + own_d + 16, lane(q)]
        theirs = pl.ds(pl.multiple_of((1 - core) * half, half), half)
        s_swap = links.swap(sm.at[core, theirs], sm.at[core, theirs], sw_s.at[3], sw_r.at[3])
        s_swap.start()
    t_swap.wait()
    o_swap.wait()
    c_swap.start()
    c_copy.start()

    if near:
        gain = jnp.concatenate(
            [sm[core, pl.ds(i * 128 + c1 + N, 16), :].astype(F32)[taps + 3:taps + 4, :own_d] for i in range(dp)], axis=1)
    else:
        gain = R["f_gain"][...].astype(F32)

    def norm(t0):
        r = pl.ds(t0, 64)
        v = toks[r, :].astype(F32)
        inv = lax.rsqrt(jnp.mean(v * v, axis=-1, keepdims=True) + EPS)
        normed[r, :] = (v * inv * gain).astype(BF)

    tiles(total, norm, 64)
    xin[0:8, :] = jnp.zeros((8, half), F32)

    def in_proj(j):
        xin[pl.ds(8, total), pl.ds(j, 256)] = dot(normed[...], cols_of(wi, 0, pl.ds(j, 256)))

    tiles(half, in_proj, 256)
    own = pl.multiple_of(core * half, half)
    row = lax.broadcasted_iota(jnp.int32, (128, 128), 0)
    if near:
        s_swap.wait()
    for b in range(lanes):
        if near:
            one, two = sm[0, pl.ds(own + b * 128, 128), :], sm[1, pl.ds(own + b * 128, 128), :]
        else:
            one, two = R["f_one"][:, lane(b)], R["f_two"][:, lane(b)]
        one, two = one.astype(F32), two.astype(F32)
        par[:, lane(b)] = one
        select[:, lane(b)] = jnp.where(row < c1, one, 0.0).astype(BF)
        delta[:, lane(b)] = jnp.where(row < rank, two, 0.0).astype(BF)
    a2[...] = -jnp.exp(par[c1:c1 + N, :]) * LOG2E

    def conv_tile(t0):
        o = offs[pl.ds(t0, 64), :]
        for b in range(lanes):
            c = lane(b)
            v = xin[pl.ds(t0, 72), c]
            acc = par[r_fb:r_fb + 1, c]
            for j in range(taps):
                s = v[8 - j:72 - j]
                if j:
                    s = jnp.where(o >= float(j), s, 0.0)
                acc = acc + par[r_taps + taps - 1 - j:r_taps + taps - j, c] * s
            conv[pl.ds(t0, 64), c] = acc
            actl[pl.ds(t0, 64), c] = (acc * sigmoid(acc)).astype(BF)

    x_swaps = []
    for p in range(2):
        r = pl.ds(p * rows, rows)
        tiles((p + 1) * rows, conv_tile, 64, p * rows)
        xo[r, :] = dot(actl[r, :], select[...], NT)
        x_swaps.append(links.swap(xo.at[r], xr.at[r], sw_s.at[4 + 9 * p], sw_r.at[4 + 9 * p]))
        x_swaps[p].start()

    def dt_tile(t0):
        low = xo[pl.ds(t0, 64), :].astype(BF)
        for b in range(half // 256):
            pre2 = dot(low, delta[:, lane(b, 256)])
            for q in range(2):
                c = lane(2 * b + q)
                s = softplus(pre2[:, lane(q)] + par[r_db:r_db + 1, c])
                dt[pl.ds(t0, 64), c] = s
                cv = conv[pl.ds(t0, 64), c]
                dx[pl.ds(t0, 64), c] = s * (cv * sigmoid(cv))

    per = 128 // CH

    def cols_tile(i, _):
        t0 = pl.multiple_of(i * 128, 128)
        x = xo[pl.ds(t0, 128), :]
        t = x.T
        for q in range(per):
            btc[i * per + q] = t[rank:rank + N, q * CH:(q + 1) * CH]
            ctc[i * per + q] = t[rank + N:rank + 2 * N, q * CH:(q + 1) * CH]
        m = block_mask(128)
        cblk[pl.ds(t0, 128), :] = jnp.where(m, dot(x.astype(BF), pick(rank + N)), 0.0).astype(BF)
        bblk[pl.ds(t0, 128), :] = jnp.where(m, dot(x.astype(BF), pick(rank)), 0.0).astype(BF)
        return 0

    for p in range(2):
        r = pl.ds(p * rows, rows)
        x_swaps[p].wait()
        xo[r, :] += xr[r, :]
        tiles((p + 1) * rows, dt_tile, 64, p * rows)
        lax.fori_loop(p * rows // 128, (p + 1) * rows // 128, cols_tile, 0)

    steps = g_w[8:15]
    hp = hbuf.shape[1] // N
    hq = hp // CH
    n_blk = total // hp
    st[...] = jnp.zeros_like(st)
    lg = min(512, half)

    def kept(blk):
        return hs.at[pl.ds(pl.multiple_of(blk * hp * N, hp * N), hp * N)]

    def write_out(blk, slot):
        return pltpu.make_async_copy(hbuf.at[slot], kept(blk), hsem.at[slot])

    def f_block(blk, _):
        slot = lax.rem(blk, 2)

        @pl.when(blk >= 2)
        def _():
            write_out(blk - 2, slot).wait()

        def chunk(q):
            c = blk * hq + q
            t0 = pl.multiple_of(c * CH, CH)
            bt = btc[c]
            first = offs[pl.ds(t0, CH), :] == 0.0
            hb = hbuf.at[slot, pl.ds(pl.multiple_of(q * CH * N, CH * N), CH * N), :]
            for g in range(half // lg):
                ls = lane(g, lg)
                a = a2[:, ls]
                h = st[:, ls]
                ds, xs = jnp.where(jnp.concatenate([first] * (lg // 128), axis=1), BIG, dt[pl.ds(t0, CH), ls]), dx[pl.ds(t0, CH), ls]
                for k in range(CH):
                    d = jnp.broadcast_to(ds[k:k + 1], (N, lg))
                    v = jnp.broadcast_to(xs[k:k + 1], (N, lg))
                    w = jnp.broadcast_to(bt[:, k:k + 1], (N, lg))
                    h = jnp.exp2(d * a) * h + w * v
                    hb[k * N:(k + 1) * N, ls] = h.astype(BF)
                st[:, ls] = h
            y[pl.ds(t0, CH), :] = dot(cblk[pl.ds(t0, CH), :], hb[...])

        def several(p, _):
            for k, s in enumerate(steps):
                pl.when(blk * (hq // 2) + p == (6 + 4 * k) // 2)(s)
            for u in range(2):
                chunk(p * 2 + u)
            return 0

        lax.fori_loop(0, hq // 2, several, 0)

        @pl.when(blk < n_blk - 2)
        def _():
            write_out(blk, slot).start()

        return 0

    lax.fori_loop(0, n_blk, f_block, 0)
    c_copy.wait()
    c_swap.wait()

    accs[...] = jnp.zeros_like(accs)

    def gate_cols(j):
        gt[:, pl.ds(j, 256)] = dot(normed[...], cols_of(ww, 0, pl.ds(j, 256)))

        def gate_tile(t0):
            r = pl.ds(t0, 64)
            for q in range(2):
                c = pl.ds(pl.multiple_of(j + q * 128, 128), 128)
                cv = conv[r, c]
                scanned = y[r, c] + par[r_sk:r_sk + 1, c] * (cv * sigmoid(cv))
                y[r, c] = scanned
                g = gt[r, c]
                gated[r, c] = (scanned * (g * sigmoid(g))).astype(BF)

        tiles(total, gate_tile, 64)

    g_w[15]()
    tiles(half, gate_cols, 256)

    def outer(left, right, out):
        def body(i):
            for b in range(half // 512):
                out[pl.ds(i, 256), lane(b, 512)] = dot(left[:, pl.ds(i, 256)], right[:, lane(b, 512)], TN).astype(BF)
        tiles(width, body, 256)

    s_o = scatter_steps(links, d_out, R["red_o"], R["so_b"], R["so_s"], R["so_r"])
    s_g = scatter_steps(links, d_gate, R["red_g"], R["sg_b"], R["sg_s"], R["sg_r"])
    outer(cots, gated, d_out)
    s_o[0]()

    def grad_cols(j):
        qtmp[...] = dot(cots[...], cols_of(ww, own_d, pl.ds(j, 256)))

        def grad_tile(t0):
            r = pl.ds(t0, 64)
            for q in range(2):
                c = pl.ds(pl.multiple_of(j + q * 128, 128), 128)
                cv = conv[r, c]
                g = gt[r, c]
                sg = sigmoid(g)
                gg = qtmp[r, lane(q)]
                ggr[r, c] = (gg * y[r, c] * slope(g, sg)).astype(BF)
                G = gg * (g * sg)
                y[r, c] = G
                accs[0, :, c] += eighths(G * (cv * sigmoid(cv)))

        tiles(total, grad_tile, 64)

    tiles(half, grad_cols, 256)
    outer(normed, ggr, d_gate)
    s_g[0]()

    steps_b = s_o[1:9] + s_g[1:3] + [s_o[9]] + [s_g[3], s_g[4], s_g[5], s_g[6], s_g[7], s_g[8], s_g[9]]
    n_chunks = total // CH
    st[...] = jnp.zeros_like(st)
    racc[...] = jnp.zeros_like(racc)

    def read_back(blk, slot):
        return pltpu.make_async_copy(kept(blk), hbuf.at[slot], hsem.at[slot])

    def b_block(i, _):
        blk = n_blk - 1 - i
        slot = lax.rem(blk, 2)

        def chunk(q):
            c = blk * hq + q
            t0 = pl.multiple_of(c * CH, CH)
            before = jnp.where(q == 0, 1 - slot, slot)
            last = pl.multiple_of(jnp.where(q == 0, hp - 1, q * CH - 1) * N, N)
            ct = ctc[c]
            first = offs[pl.ds(t0, CH), :] == 0.0
            hb = hbuf.at[slot, pl.ds(pl.multiple_of(q * CH * N, CH * N), CH * N), :]
            hl = hbuf.at[before, pl.ds(last, N), :]
            for g in range(half // lg):
                ls = lane(g, lg)
                a = a2[:, ls]
                carry = st[:, ls]
                ra = racc[:, ls]
                ds, gs = jnp.where(jnp.concatenate([first] * (lg // 128), axis=1), BIG, dt[pl.ds(t0, CH), ls]), y[pl.ds(t0, CH), ls]
                for k in range(CH - 1, -1, -1):
                    d = jnp.broadcast_to(ds[k:k + 1], (N, lg))
                    gg = jnp.broadcast_to(gs[k:k + 1], (N, lg))
                    cc = jnp.broadcast_to(ct[:, k:k + 1], (N, lg))
                    h = hb[(k - 1) * N:k * N, ls] if k else hl[:, ls]
                    sg = cc * gg + carry
                    carry = jnp.exp2(d * a) * sg
                    term = carry * h.astype(F32)
                    ra = ra + term * d
                    sgs[k * N:(k + 1) * N, ls] = sg.astype(BF)
                    part = term * a
                    part = part[:N // 2] + part[N // 2:]
                    if k % 2:
                        odd = part
                    else:
                        das[k * N // 2:(k + 2) * N // 2, ls] = jnp.concatenate([part, odd], axis=0).astype(BF)
                st[:, ls] = carry
                racc[:, ls] = ra
            m = block_mask()
            m8 = jnp.where(lax.broadcasted_iota(jnp.int32, (CH, CH * N // 2), 1) // (N // 2)
                           == lax.broadcasted_iota(jnp.int32, (CH, CH * N // 2), 0), 1.0, 0.0).astype(BF)
            r = pl.ds(t0, CH)
            sgc = sgs[...]
            wout = dot(dx[r, :].astype(BF), sgc, NT)
            wgs[pl.ds(c, 1), :] = jnp.sum(jnp.where(m, wout, 0.0), axis=0, keepdims=True)
            rout = dot(y[r, :].astype(BF), hb[...], NT)
            rgs[pl.ds(c, 1), :] = jnp.sum(jnp.where(m, rout, 0.0), axis=0, keepdims=True)
            dx[r, :] = dot(bblk[r, :], sgc)
            gt[r, :] = dot(m8, das[...])

        def several(p, _):
            done = i * (hq ) + p
            for k, s in enumerate(steps_b):
                pl.when(done == 6 + (9 * k) // 4)(s)

            @pl.when((p == hq  - 1) & (blk >= 1) & (blk <= n_blk - 2))
            def _():
                read_back(blk - 1, 1 - slot).wait()

            for u in range(1):
                chunk(hq - 1 - (p  + u))
            return 0

        lax.fori_loop(0, hq , several, 0)

        @pl.when(blk >= 2)
        def _():
            read_back(blk - 2, slot).start()

        return 0

    lax.fori_loop(0, n_blk, b_block, 0)
    dg, low_b = dx, d_gate

    fins = [links.swap(R[k], R[k + "2"], sw_s.at[10 + n], sw_r.at[10 + n])
            for n, k in enumerate(("red_i", "red_g", "red_o"))]
    fins[1].start()
    fins[2].start()

    ln2 = math.log(2.0)

    def pre_tile(t0):
        r = pl.ds(t0, 64)
        for b in range(lanes):
            c = lane(b)
            cv = conv[r, c]
            act = cv * sigmoid(cv)
            v = (dg[r, c] * act + gt[r, c] * ln2) * (1.0 - jnp.exp(-dt[r, c]))
            low_b[r, c] = v.astype(BF)
            accs[1, :, c] += eighths(v)

    xg = qtmp.at[:, 0:128]

    def xg_tile(i, _):
        t0 = pl.multiple_of(i * 128, 128)
        r = pl.ds(t0, 128)
        m = block_mask(128)
        sums = dot(low_b[r, :], delta[...], NT)
        for ref, first in ((wgs, rank), (rgs, rank + N)):
            v = ref[pl.ds(pl.multiple_of(i * per, per), per), :]
            v = jnp.broadcast_to(v[:, None, :], (per, CH, CH * N)).reshape(128, CH * N)
            v = jnp.where(m, v, 0.0)
            hi = v.astype(BF)
            lo = (v - hi.astype(F32)).astype(BF)
            p = place(first)
            sums = sums + dot(hi, p) + dot(lo, p)
        xg[r, :] = sums
        return 0

    g_swaps = []
    for p in range(2):
        r = pl.ds(p * rows, rows)
        tiles((p + 1) * rows, pre_tile, 64, p * rows)
        lax.fori_loop(p * rows // 128, (p + 1) * rows // 128, xg_tile, 0)
        g_swaps.append(links.swap(xg.at[r], R["xr2"].at[r], sw_s.at[6 + 8 * p], sw_r.at[6 + 8 * p]))
        g_swaps[p].start()
    sgrad = R["sgrad"]
    xob = xo[...].astype(BF)
    for b in range(half // 256):
        sgrad[1, :, lane(b, 256)] = dot(xob, low_b[0:total, lane(b, 256)], TN)
    def project(which, out):
        def body(i, _):
            out(pl.multiple_of(i * 256, 256), dot(gated[which, :], rows_of(ww, own_d, i), NT))
            return 0
        lax.fori_loop(0, width // 256, body, 0)

    msent, mcame = hbuf.at[0, pl.ds(0, rows), :], hbuf.at[1, pl.ds(0, rows), :]

    def put_mixed(j, v):
        msent[:, pl.ds(j, 256)] = v.astype(BF)

    project(other, put_mixed)
    for p in range(2):
        g_swaps[p].wait()
    xg[...] = xg[...] + R["xr2"][...]
    m_swap = links.swap(msent, mcame, sw_s.at[5], sw_r.at[5])
    m_swap.start()
    xgb = xg[...].astype(BF)
    for b in range(half // 256):
        sgrad[0, :, lane(b, 256)] = dot(xgb, actl[:, lane(b, 256)], TN)

    quarter = half // 2
    ig = d_gate
    d_in = d_out
    y[pl.ds(total, 8), :] = jnp.zeros((8, half), F32)

    def conv_back(h):
        def cg_tile(t0):
            r = pl.ds(t0, 64)
            low = xg[r, :].astype(BF)
            for b in range(h * quarter // 256, (h + 1) * quarter // 256):
                back = dot(low, select[:, lane(b, 256)])
                for q in range(2):
                    c = lane(2 * b + q)
                    ag = y[r, c] * par[r_sk:r_sk + 1, c] + dg[r, c] * dt[r, c] + back[:, lane(q)]
                    cv = conv[r, c]
                    v = ag * slope(cv, sigmoid(cv))
                    y[r, c] = v
                    accs[2, :, c] += eighths(v)

        tiles(total, cg_tile, 64)

        def ig_tile(t0):
            o = offs[pl.ds(t0, 72), :]
            for b in range(h * quarter // 128, (h + 1) * quarter // 128):
                c = lane(b)
                v = y[pl.ds(t0, 72), c]
                x = xin[pl.ds(t0, 72), c]
                acc = jnp.zeros((64, 128), F32)
                for j in range(taps):
                    mv = jnp.where(o >= float(j), v, 0.0) if j else v
                    accs[3 + taps - 1 - j, :, c] += eighths(mv[0:64] * x[8 - j:72 - j])
                    acc = acc + mv[j:64 + j] * par[r_taps + taps - 1 - j:r_taps + taps - j, c]
                ig[pl.ds(t0, 64), c] = acc.astype(BF)

        tiles(total, ig_tile, 64)

        def outer_tile(i, _):
            v = dot(normed[:, pl.ds(pl.multiple_of(i * 256, 256), 256)], ig[0:total, lane(h, quarter)], TN).astype(BF)
            d_in[pl.ds(pl.multiple_of(i * 256, 256), 256), lane(h, quarter)] = v
            return 0

        lax.fori_loop(0, width // 256, outer_tile, 0)

    def half_scatter(h):
        def part(ref):
            return ref.at[(slice(None),) * (len(ref.shape) - 1) + (lane(h, quarter),)]
        bufs = [part(b) for b in R["so_b"]] if near else [R[("so_b", "sg_b")[h]][0].at[:, :, lane(h, quarter)], None, None]
        return scatter_steps(links, part(d_in), part(R["red_i"]), bufs, R["si_s" if h == 0 else "sj_s"], R["si_r" if h == 0 else "sj_r"])

    s_i, s_j = half_scatter(0), half_scatter(1)
    conv_back(0)
    s_i[0]()
    conv_back(1)
    s_j[0]()
    s_i[1]()
    s_i[2]()
    s_i[3]()
    s_i[4]()

    def back_project(which, out):
        def body(i, _):
            out(pl.multiple_of(i * 256, 256),
                dot(ig[which, :], rows_of(wi, 0, i), NT) + dot(ggr[which, :], rows_of(ww, 0, i), NT))
            return 0
        lax.fori_loop(0, width // 256, body, 0)

    def put_send(j, v):
        msend[:, pl.ds(j, 256)] = v.astype(BF)

    back_project(other, put_send)
    n_swap = links.swap(msend, mrecv, sw_s.at[7], sw_r.at[7])
    n_swap.start()
    s_i[5]()
    s_i[6]()
    s_j[1]()
    s_j[2]()
    ng = R["mixed_f"]

    def put_ng(j, v):
        ng[:, pl.ds(j, 256)] = v

    back_project(mine, put_ng)

    vecs = jnp.concatenate(
        [racc[...] * a2[...] * ln2]
        + [jnp.sum(accs[3 + k], axis=0, keepdims=True) for k in range(taps)]
        + [jnp.sum(accs[2], axis=0, keepdims=True), jnp.sum(accs[1], axis=0, keepdims=True),
           jnp.sum(accs[0], axis=0, keepdims=True), jnp.zeros((16 - taps - 3, half), F32)], axis=0)
    sgrad[0, c1:128, :] = vecs
    sgrad[1, rank:128, :] = jnp.zeros((128 - rank, half), F32)
    if near:
        small, away = R["small"], R["away"]
        for b in range(lanes):
            small[pl.ds(own + b * 128, 128), :] = sgrad[core, :, lane(b)].astype(BF)
            away[lane(b), :] = sgrad[1 - core, :, lane(b)].astype(BF)
        a_swap = links.swap(away, small.at[pl.ds(own, half), :], sw_s.at[8], sw_r.at[8])
        a_swap.start()
        red_s = R["o_small"]
        s_s = scatter_steps(links, small, red_s.at[core], R["ss_b"], R["ss_s"], R["ss_r"])
    else:
        s_s = [lambda: None] * 10
    s_i[7]()
    s_i[8]()
    s_j[3]()
    s_j[4]()
    if near:
        a_swap.wait()
    s_s[0]()
    n_swap.wait()
    def tok_tile(t0):
        r = pl.ds(t0, 32)
        v = tok[r, :].astype(F32)
        inv = lax.rsqrt(jnp.mean(v * v, axis=-1, keepdims=True) + EPS)
        sc = v * inv
        n = ng[r, :] + mrecv[r, :].astype(F32)
        sg = n * gain
        ng[r, :] = cots[pl.ds(pl.multiple_of(core * rows + t0, 32), 32), :].astype(F32) + inv * (
            sg - sc * jnp.mean(sg * sc, axis=-1, keepdims=True))

    tiles(rows, tok_tile, 32)
    t_copy = pltpu.make_async_copy(ng, R["tgrad"], lsem.at[1])
    t_copy.start()
    s_j[5]()
    s_i[9]()
    m_swap.wait()
    def put_own(j, v):
        R["mixed"][:, pl.ds(j, 256)] = (
            tok[:, pl.ds(j, 256)].astype(F32) + v + mcame[:, pl.ds(j, 256)].astype(F32)).astype(BF)

    project(mine, put_own)
    s_s[1]()
    s_s[2]()
    s_j[6]()
    if not near:
        R["f_grad"][...] = sgrad[...]
    s_j[7]()
    for k in range(3, 7):
        s_s[k]()
    s_j[8]()
    for k in range(7, 10):
        s_s[k]()
    if near:
        fs = links.swap(red_s.at[core], red_s.at[core], sw_s.at[9], sw_r.at[9])
        fs.start()
    s_j[9]()
    t_copy.wait()

    fins[0].start()

    def share(first, k, out):
        R[out][:, pl.ds(pl.multiple_of(first + core * half, 128), half)] = R[k][...]
        R[out][:, pl.ds(pl.multiple_of(first + (1 - core) * half, 128), half)] = R[k + "2"][...]

    fins[1].wait()
    share(inner, "red_g", "o_in")
    fins[2].wait()
    share(0, "red_o", "o_out")
    if near:
        fs.wait()
    fins[0].wait()
    share(0, "red_i", "o_in")


def layer(inputs, dp, dims):
    rows, width = inputs["tok"].shape
    half = inputs["w_o"].shape[1] // 2
    inner = 2 * half
    total = 2 * rows
    taps, rank = dims
    own_d, own_e = width // dp, inner // dp
    n = copies_of(dp)
    near = bool(plane(dp))
    extra = 16 if near else 0
    sd = jax.ShapeDtypeStruct
    vm = pl.BlockSpec(memory_space=pltpu.VMEM)
    hbm = pl.BlockSpec(memory_space=pl.ANY)
    dma = pltpu.SemaphoreType.DMA
    V = pltpu.VMEM
    outs = {
        "mixed": sd((rows, width), BF), "tgrad": sd((rows, width), F32),
        "o_in": sd((own_d, 2 * inner), F32), "o_out": sd((own_d, inner), F32), "hs": sd((total * N, half), BF),
    }
    if near:
        outs["o_small"] = sd((2, 128, own_e), F32)
    else:
        outs["f_grad"] = sd((2, 128, half), F32)
    f2 = V((total, half), F32)
    scratch = {
        "part_i": V((own_d + extra, half), BF), "part_w": V((2 * own_d, half), BF),
        "wi": V((dp * (own_d + extra), half), BF), "ww": V((2 * width, half), BF), "select": V((128, half), BF), "delta": V((128, half), BF),
        "toks": V((total, width), BF), "cots": V((total, width), BF), "normed": V((total, width), BF),
        "offs": V((total + 8, 128), F32), "xin": V((total + 8, half), F32), "conv": f2, "actl": V((total, half), BF),
        "dt": f2, "gt": f2, "dx": f2, "y": V((total + 8, half), F32), "ggr": V((total, half), BF),
        "xo": V((total, 128), F32), "xr": V((total, 128), F32), "xr2": V((total, 128), F32),
        "hbuf": V((2, 64 * N, half), BF), "par": V((128, half), F32),
        "btc": V((total // CH, N, CH), F32), "ctc": V((total // CH, N, CH), F32),
        "cblk": V((total, CH * N), BF), "bblk": V((total, CH * N), BF),
        "a2": V((N, half), F32), "st": V((N, half), F32), "racc": V((N, half), F32),
        "qtmp": V((total, 256), F32),
        "sgs": V((CH * N, half), BF), "das": V((CH * N // 2, half), BF),
        "wgs": V((total // CH, CH * N), F32), "rgs": V((total // CH, CH * N), F32),
        "accs": V((3 + taps, 8, half), F32), "d_out": V((width, half), BF), "d_gate": V((width, half), BF),
        "msend": V((rows, width), BF), "mrecv": V((rows, width), BF), "mixed_f": V((rows, width), F32),
        "sgrad": V((2, 128, half), F32),
        "so_b": scatter_scratch(dp, own_d, half), "sg_b": scatter_scratch(dp, own_d, half),
        "sw_s": dma((15,)), "sw_r": dma((15,)), "hsem": dma((2,)), "lsem": dma((2,)),
    }
    for k in ("i", "g", "o"):
        scratch["red_" + k] = V((own_d, half), F32)
        scratch["red_" + k + "2"] = V((own_d, half), F32)
    if near:
        scratch["sm"] = V((2, inner, own_e), BF)
        scratch["small"], scratch["away"] = V((inner, own_e), BF), V((half, own_e), BF)
        scratch["ss_b"] = scatter_scratch(dp, 128, own_e)
    for k in ("gi", "gw", "si", "sj", "sg", "so", "ss"):
        scratch[k + "_s"] = dma((n,))
        scratch[k + "_r"] = dma((n,))
    names = list(inputs) + list(outs) + list(scratch)
    res = pl.pallas_call(
        functools.partial(layer_kernel, dp=dp, dims=dims, names=names),
        out_shape=list(outs.values()),
        in_specs=[pl.BlockSpec(memory_space=pltpu.SMEM) if k == "lens" else hbm if k == "cot" else vm for k in inputs],
        out_specs=[hbm if k in ("tgrad", "hs") else vm for k in outs],
        scratch_shapes=list(scratch.values()),
        compiler_params=pltpu.CompilerParams(collective_id=0, has_side_effects=True, vmem_limit_bytes=127 << 19),
        name="layer",
    )(*inputs.values())
    return dict(zip(outs, res))


def local(
    tokens,
    doc_lengths,
    cotangent,
    norm_gain,
    input_weight,
    filter_weight,
    filter_bias,
    select_weight,
    delta_weight,
    delta_bias,
    decay_log,
    skip_gain,
    output_weight,
    *,
    dp,
):
    rows, length, width = tokens.shape
    rank = delta_weight.shape[1]
    taps = filter_weight.shape[1]
    own_e = filter_weight.shape[0]
    own_d = norm_gain.shape[0]
    inner = own_e * dp
    c1 = rank + 2 * N
    inputs = {
        "lens": doc_lengths, "tok": tokens.reshape(rows * length, width), "cot": cotangent.reshape(rows * length, width),
        "w_in": input_weight, "w_o": output_weight,
    }
    if plane(dp):
        inputs.update(
            s_select=select_weight.T, s_decay=decay_log.T, s_delta=delta_weight.T, s_filter=filter_weight.T,
            s_fb=filter_bias[None], s_db=delta_bias[None], s_skip=skip_gain[None], s_gain=norm_gain[None],
        )
    else:
        core = lax.axis_index("rep")
        vectors = jnp.stack([filter_bias, delta_bias, skip_gain])
        tail = jnp.concatenate([filter_weight.T, vectors, jnp.zeros((16 - taps - 3, own_e), BF)], axis=0)
        one = jnp.concatenate([select_weight.T, decay_log.T, tail], axis=0)
        two = jnp.concatenate([delta_weight.T, jnp.zeros((128 - rank, own_e), BF)], axis=0)
        both = lax.all_gather(jnp.stack([one, two]), "dp", axis=2, tiled=True)
        both = lax.dynamic_slice(both, (0, 0, core * (inner // 2)), (2, 128, inner // 2))
        inputs.update(f_one=both[0], f_two=both[1], f_gain=lax.all_gather(norm_gain, "dp", axis=0, tiled=True)[None])
    r = layer(inputs, dp, (taps, rank))
    if plane(dp):
        small = r["o_small"]
    else:
        small = lax.all_gather(r["f_grad"], "rep", axis=2, tiled=True)
        small = lax.psum_scatter(small, "dp", scatter_dimension=2, tiled=True)
    o = finish(r["mixed"], r["tgrad"], r["o_in"], r["o_out"], small, input_weight, norm_gain[None], (taps, rank))
    return (
        o[0].reshape(rows, length, width),
        o[1].reshape(rows, length, width),
        o[4].reshape(own_d),
        o[2],
        o[5].T,
        o[6].reshape(own_e),
        o[7].T,
        o[8].T,
        o[9].reshape(own_e),
        o[10].T,
        o[11].reshape(own_e),
        o[3],
    )


def finish(mixed, tgrad, o_in, o_out, small, w_in, gain, dims):
    taps, rank = dims
    c1 = rank + 2 * N
    own_e, own_d = small.shape[2], w_in.shape[0]
    sd = jax.ShapeDtypeStruct
    big = [mixed, tgrad, o_in, o_out]
    parts = 4

    def kernel(*refs):
        ins, small_ref, w_ref, gain_ref, outs, acc = refs[:4], refs[4], refs[5], refs[6], refs[7:19], refs[19]
        for i, o in zip(ins, outs[:4]):
            o[...] = i[...]
        p = w_ref[...].astype(F32) * ins[2][...]
        total = p[:, 0:128]
        for b in range(1, p.shape[1] // 128):
            total = total + p[:, b * 128:(b + 1) * 128]
        g = c1 + N + taps + 3

        @pl.when(pl.program_id(0) == 0)
        def _():
            acc[...] = jnp.zeros_like(acc)
            outs[5][...] = small_ref[0, c1 + N:c1 + N + taps, :]
            outs[6][...] = small_ref[0, g - 3:g - 2, :]
            outs[7][...] = small_ref[0, 0:c1, :]
            outs[8][...] = small_ref[1, 0:rank, :]
            outs[9][...] = small_ref[0, g - 2:g - 1, :]
            outs[10][...] = small_ref[0, c1:c1 + N, :]
            outs[11][...] = small_ref[0, g - 1:g, :]

        acc[0:own_d, :] += total

        @pl.when(pl.program_id(0) == parts - 1)
        def _():
            row = jnp.sum(acc[...].T, axis=0, keepdims=True)[:, :own_d]
            outs[4][...] = row / gain_ref[...].astype(F32)

    shapes = [sd(b.shape, b.dtype) for b in big] + [
        sd(s, F32) for s in ((1, own_d), (taps, own_e), (1, own_e), (c1, own_e), (rank, own_e), (1, own_e), (N, own_e), (1, own_e))]
    specs = [pl.BlockSpec((b.shape[0], b.shape[1] // parts), lambda i: (0, i)) for b in big]

    def whole(s):
        return pl.BlockSpec(s.shape, lambda i, n=len(s.shape): (0,) * n)

    wide = pl.BlockSpec((own_d, w_in.shape[1] // parts), lambda i: (0, i))
    return pl.pallas_call(
        kernel, grid=(parts,), out_shape=shapes, in_specs=specs + [whole(small), wide, whole(gain)],
        out_specs=specs + [whole(s) for s in shapes[4:]], scratch_shapes=[pltpu.VMEM((128, 128), F32)], name="finish",
    )(*big, small, w_in, gain)


def solution(mesh):
    dp_rep = ("dp", "rep")
    one = P("dp")
    two = P("dp", None)
    three = P(dp_rep, None, None)
    return jax.shard_map(
        functools.partial(local, dp=mesh.shape["dp"]),
        mesh=mesh,
        in_specs=(three, P(dp_rep, None), three, one, two, two, one, two, two, one, two, one, two),
        out_specs=(three, three, one, two, two, one, two, two, one, two, one, two),
        check_vma=False,
    )
```

```python
import functools
import math

import jax
import jax.numpy as jnp
from jax import lax
from jax.experimental import pallas as pl
from jax.experimental.pallas import tpu as pltpu
from jax.sharding import PartitionSpec as P

EPS = 1e-05
CH = 16
N = 16
F32 = jnp.float32
BF = jnp.bfloat16
NT = (((1,), (1,)), ((), ()))
TN = (((0,), (0,)), ((), ()))
BIG = 1e30
LOG2E = math.log2(math.e)


def dot(a, b, dims=(((1,), (0,)), ((), ()))):
    return lax.dot_general(a, b, dims, preferred_element_type=F32)


MESH = pl.DeviceIdType.MESH


def plane(dp):
    return 4 if dp == 16 else 0


class Links:
    def __init__(self, dp):
        self.dp = dp
        self.depth = plane(dp)
        self.me = lax.axis_index("dp")
        self.core = lax.axis_index("rep")
        if self.depth:
            self.z, self.y, self.x = self.me // 4, (self.me // 2) % 2, self.me % 2
            self.xn = self.at(self.z, self.y, 1 - self.x)
            self.yn = self.at(self.z, 1 - self.y, self.x)
            self.zs = [self.at(self.up(k), self.y, self.x) for k in range(1, self.depth)]
            self.peers = self.zs + [self.xn, self.yn]
        else:
            self.peers = [lax.rem(self.me + k, dp) for k in range(1, dp)]

    def up(self, k):
        return lax.rem(self.z + k, self.depth)

    def down(self, k):
        return lax.rem(self.z + self.depth - k, self.depth)

    def at(self, z, y, x):
        return (z * 2 + y) * 2 + x

    def barrier(self, sibling=True):
        sem = pltpu.get_barrier_semaphore()
        for peer in self.peers:
            pl.semaphore_signal(sem, inc=1, device_id=(peer, self.core), device_id_type=MESH)
        if sibling:
            pl.semaphore_signal(sem, inc=1, device_id=(self.me, 1 - self.core), device_id_type=MESH)
        pl.semaphore_wait(sem, len(self.peers) + int(sibling))

    def send(self, src, dst, send_sem, recv_sem, chip):
        return pltpu.make_async_remote_copy(
            src_ref=src, dst_ref=dst, send_sem=send_sem, recv_sem=recv_sem,
            device_id=(chip, self.core), device_id_type=MESH,
        )

    def swap(self, src, dst, send_sem, recv_sem):
        return pltpu.make_async_remote_copy(
            src_ref=src, dst_ref=dst, send_sem=send_sem, recv_sem=recv_sem,
            device_id=(self.me, 1 - self.core), device_id_type=MESH,
        )


def copies_of(dp):
    return 34 if plane(dp) else dp - 1


def gather_steps(links, src, dst, ss, rs):
    me = links.me
    rows = src.shape[0]

    def part(b, first=0, count=rows):
        return pl.ds(pl.multiple_of(b * rows + first, math.gcd(rows, count)), count)

    if not links.depth:
        cps = [links.send(src, dst.at[part(me)], ss.at[k], rs.at[k], p) for k, p in enumerate(links.peers)]

        def begin():
            for c in cps:
                c.start()
            dst[part(me), :] = src[...]

        def end():
            for c in cps:
                c.wait()

        return [begin] + [lambda: None] * 14 + [end]
    depth, half = links.depth, rows // 2
    cuts = [half if half % 16 == 0 else half + (8 if i % 2 else -8) for i in range(2 * depth - 1)]
    z, y, x, xn, yn = links.z, links.y, links.x, links.xn, links.yn
    origin = [z] + [jnp.maximum(z - d, 0) for d in range(1, depth)] + [jnp.minimum(z + d, depth - 1) for d in range(1, depth)]
    there = [z >= 0] + [z >= d for d in range(1, depth)] + [z + d < depth for d in range(1, depth)]
    up, down, up_on, down_on = {}, {}, {}, {}
    above, below = links.at(jnp.minimum(z + 1, depth - 1), y, x), links.at(jnp.maximum(z - 1, 0), y, x)
    for d in range(1, depth):
        b = links.at(origin[d - 1], y, x)
        s = src if d == 1 else dst.at[part(b)]
        up[d] = links.send(s, dst.at[part(b)], ss.at[d - 1], rs.at[d - 1], above)
        up_on[d] = (z < depth - 1) & (z >= d - 1)
        b = links.at(origin[0 if d == 1 else d + 2], y, x)
        s = src if d == 1 else dst.at[part(b)]
        down[d] = links.send(s, dst.at[part(b)], ss.at[d + 2], rs.at[d + 2], below)
        down_on[d] = (z > 0) & (z + d - 1 < depth)
    xc, yc, xf, yf = [], [], [], []
    for i in range(2 * depth - 1):
        b = links.at(origin[i], y, x)
        s = src if i == 0 else dst.at[part(b)]
        n = 6 + 4 * i
        xc.append(links.send(s, dst.at[part(b)], ss.at[n], rs.at[n], xn))
        yc.append(links.send(s, dst.at[part(b)], ss.at[n + 1], rs.at[n + 1], yn))
        lo = dst.at[part(links.at(origin[i], y, 1 - x), 0, cuts[i])]
        hi = dst.at[part(links.at(origin[i], 1 - y, x), cuts[i], rows - cuts[i])]
        yf.append(links.send(lo, lo, ss.at[n + 2], rs.at[n + 2], yn))
        xf.append(links.send(hi, hi, ss.at[n + 3], rs.at[n + 3], xn))

    def begin():
        pl.when(up_on[1])(up[1].start)
        pl.when(down_on[1])(down[1].start)

    def beside():
        xc[0].start()
        yc[0].start()
        dst[part(me), :] = src[...]

    def spread(i):
        chain, on, d = (up, up_on, i) if i < depth else (down, down_on, i - depth + 1)

        def run():
            @pl.when(there[i])
            def _():
                chain[d].wait_recv()
                if d + 1 < depth:
                    pl.when(on[d + 1])(chain[d + 1].start)
                xc[i].start()
                yc[i].start()
        return run

    def forward(i):
        def run():
            @pl.when(there[i])
            def _():
                xc[i].wait_recv()
                yf[i].start()
                yc[i].wait_recv()
                xf[i].start()
        return run

    def end():
        for i in range(2 * depth - 1):
            @pl.when(there[i])
            def _(i=i):
                yf[i].wait_recv()
                xf[i].wait_recv()
                for c in (xc[i], yc[i], xf[i], yf[i]):
                    c.wait_send()
        for d in range(1, depth):
            pl.when(up_on[d])(up[d].wait_send)
            pl.when(down_on[d])(down[d].wait_send)

    f = forward
    return [begin, beside] + [spread(i) for i in (1, 4, 2, 5, 3, 6)] + [f(i) for i in (0, 1, 4, 2, 5, 3, 6)] + [end]


def scatter_scratch(dp, rows, cols):
    if not plane(dp):
        return [pltpu.VMEM((dp - 1, rows, cols), BF)] + [pltpu.VMEM((8, 128), BF)] * 2
    d, h = plane(dp), rows // 2
    return [
        pltpu.VMEM((d, 2, h, cols), BF),
        pltpu.VMEM((d, 2, rows, cols), BF),
        pltpu.VMEM((d - 1, rows, cols), BF),
    ]


def scatter_steps(links, src, out, bufs, ss, rs, offset=0):
    me = links.me
    rows = out.shape[0]
    pitch = src.shape[0] // links.dp

    def part(b, first=0, count=rows):
        return pl.ds(pl.multiple_of(b * pitch + offset + first, math.gcd(math.gcd(pitch, offset + first), count)), count)

    if not links.depth:
        got = bufs[0]
        cps = [links.send(src.at[part(p)], got.at[k], ss.at[k], rs.at[k], p) for k, p in enumerate(links.peers)]

        def begin():
            for c in cps:
                c.start()

        def end():
            for c in cps:
                c.wait()

            def add(k, total):
                return total + got[k].astype(F32)

            out[...] = lax.fori_loop(0, links.dp - 1, add, src[part(me), :].astype(F32))

        return [begin] + [lambda: None] * 8 + [end]
    halves, come, zcome = bufs
    depth = links.depth
    h = rows // 2
    y, x, xn, yn = links.y, links.x, links.xn, links.yn
    ac, bc, cc = [], [], []
    for k in range(depth):
        zz = links.up(k)
        diag = links.at(zz, 1 - y, 1 - x)
        bx = links.at(zz, y, 1 - x)
        by = links.at(zz, 1 - y, x)
        own = links.at(zz, y, x)
        n = 4 * k
        ac.append((
            links.send(src.at[part(diag, 0, h)], halves.at[k, 0], ss.at[n], rs.at[n], xn),
            links.send(src.at[part(diag, h, h)], halves.at[k, 1], ss.at[n + 1], rs.at[n + 1], yn),
        ))
        bc.append((
            links.send(src.at[part(bx)], come.at[k, 0], ss.at[n + 2], rs.at[n + 2], xn),
            links.send(src.at[part(by)], come.at[k, 1], ss.at[n + 3], rs.at[n + 3], yn),
        ))
        if k:
            n = 4 * depth + k - 1
            cc.append(links.send(src.at[part(own)], zcome.at[k - 1], ss.at[n], rs.at[n], links.zs[k - 1]))

    def add(where, more):
        src[where, :] = (src[where, :].astype(F32) + more.astype(F32)).astype(BF)

    def begin():
        for k in (1, 2, 3, 0):
            ac[k][0].start()
            ac[k][1].start()

    def middle(k):
        def run():
            zz = links.up(k)
            ac[k][0].wait_recv()
            add(part(links.at(zz, 1 - y, x), 0, h), halves[k, 0])
            bc[k][1].start()
            ac[k][1].wait_recv()
            add(part(links.at(zz, y, 1 - x), h, h), halves[k, 1])
            bc[k][0].start()
        return run

    def along(k):
        def run():
            bc[k][0].wait_recv()
            bc[k][1].wait_recv()
            own = part(links.at(links.up(k), y, x))
            total = src[own, :].astype(F32) + come[k, 0].astype(F32) + come[k, 1].astype(F32)
            if k:
                src[own, :] = total.astype(BF)
                cc[k - 1].start()
            else:
                out[...] = total
        return run

    def end():
        for k in range(depth - 1):
            cc[k].wait_recv()
            out[...] += zcome[k].astype(F32)
        for k in range(depth):
            for c in ac[k] + bc[k]:
                c.wait_send()
        for c in cc:
            c.wait_send()

    return [begin, middle(1), middle(2), along(1), middle(3), along(2), middle(0), along(3), along(0), end]


def sigmoid(v):
    return 0.5 * jnp.tanh(0.5 * v) + 0.5


def softplus(v):
    u = jnp.exp(-jnp.abs(v))
    return jnp.maximum(v, 0.0) + jnp.where(u < 1e-3, u * (1.0 - 0.5 * u), jnp.log(1.0 + u))


def slope(v, s):
    return s * (1.0 + v * (1.0 - s))


def block_mask(rows=CH):
    r = lax.broadcasted_iota(jnp.int32, (rows, CH * N), 0)
    c = lax.broadcasted_iota(jnp.int32, (rows, CH * N), 1)
    return (c // N) == (r % CH)


def pick(first):
    r = lax.broadcasted_iota(jnp.int32, (128, CH * N), 0)
    c = lax.broadcasted_iota(jnp.int32, (128, CH * N), 1)
    return jnp.where(r - first == c % N, 1.0, 0.0).astype(BF)


def place(first):
    r = lax.broadcasted_iota(jnp.int32, (CH * N, 128), 0)
    c = lax.broadcasted_iota(jnp.int32, (CH * N, 128), 1)
    return jnp.where(c - first == r % N, 1.0, 0.0).astype(BF)


def eighths(v):
    return jnp.sum(v.reshape(v.shape[0] // 8, 8, v.shape[1]), axis=0)


def layer_kernel(*refs, dp, dims, names):
    R = dict(zip(names, refs))
    lens, tok, cot, w_in, w_o = (R[k] for k in ("lens", "tok", "cot", "w_in", "w_o"))
    wi, ww, toks, cots, normed = (R[k] for k in ("wi", "ww", "toks", "cots", "normed"))
    select, delta = R["select"], R["delta"]
    offs, xin, conv, actl, dt, gt, dx, y = (R[k] for k in ("offs", "xin", "conv", "actl", "dt", "gt", "dx", "y"))
    ggr, xo, xr, hs, hbuf = (R[k] for k in ("ggr", "xo", "xr", "hs", "hbuf"))
    par, btc, ctc, cblk, bblk, a2, st, racc = (R[k] for k in ("par", "btc", "ctc", "cblk", "bblk", "a2", "st", "racc"))
    qtmp, sgs, das, wgs, rgs, accs = (R[k] for k in ("qtmp", "sgs", "das", "wgs", "rgs", "accs"))
    d_out, d_gate, msend, mrecv, sw_s, sw_r, hsem, lsem = (
        R[k] for k in ("d_out", "d_gate", "msend", "mrecv", "sw_s", "sw_r", "hsem", "lsem"))
    taps, rank = dims
    links = Links(dp)
    core, me = links.core, links.me
    rows, width = tok.shape
    half = wi.shape[1]
    total = 2 * rows
    own_d = w_in.shape[0]
    inner = 2 * half
    own_e = inner // dp
    lanes = half // 128
    c1 = rank + 2 * N
    r_taps, r_fb, r_db, r_sk, gcol = (c1 + N + k for k in (0, taps, taps + 1, taps + 2, taps + 3))
    gated = toks

    def cut(ref, start):
        return ref[:, pl.ds(pl.multiple_of(start + core * half, 128), half)]

    pitch_i, pitch_w = wi.shape[0] // dp, 2 * own_d

    def cols_of(ref, first, c):
        v = ref[:, c]
        return v.reshape(dp, ref.shape[0] // dp, v.shape[1])[:, first:first + own_d].reshape(width, v.shape[1])

    def rows_of(ref, first, i):
        n = 256 // own_d
        p = ref.shape[0] // dp
        v = ref[pl.ds(pl.multiple_of(i * n * p, n * p), n * p), :]
        return v.reshape(n, p, half)[:, first:first + own_d].reshape(256, half)

    def lane(b, n=128):
        return slice(b * n, (b + 1) * n)

    def tiles(n, body, size, start=0):
        def run(i, _):
            body(pl.multiple_of(i * size, size))
            return 0
        lax.fori_loop(start // size, n // size, run, 0)

    near = bool(links.depth)
    part_i, part_w = R["part_i"], R["part_w"]
    part_i[0:own_d, :] = cut(w_in, 0)
    part_w[0:own_d, :] = cut(w_in, inner)
    part_w[own_d:, :] = cut(w_o, 0)
    if near:
        sm = R["sm"]
        tail = jnp.concatenate(
            [R[k][...].astype(F32) for k in ("s_filter", "s_fb", "s_db", "s_skip")]
            + [jnp.concatenate([R["s_gain"][...].astype(F32), jnp.zeros((1, own_e - own_d), F32)], axis=1),
               jnp.zeros((16 - taps - 4, own_e), F32)], axis=0).astype(BF)
        for q in range(8):
            one = R["s_select"][q * 16:q * 16 + 16, :] if q < c1 // 16 else R["s_decay"][...] if q < 7 else tail
            two = R["s_delta"][q * 16:q * 16 + 16, :] if q < rank // 16 else tail
            part_i[own_d:own_d + 16, lane(q)] = jnp.where(core == 0, one.astype(F32), two.astype(F32)).astype(BF)
    links.barrier()
    mine = pl.ds(pl.multiple_of(core * rows, rows), rows)
    other = pl.ds(pl.multiple_of((1 - core) * rows, rows), rows)
    t_idx = lax.broadcasted_iota(jnp.int32, (rows, 128), 0)
    begin = jnp.zeros((rows, 128), jnp.int32)
    start = lens[0, 0]
    for k in range(1, lens.shape[1]):
        begin = jnp.where(t_idx >= start, start, begin)
        start = start + lens[0, k]
    offs[mine, :] = (t_idx - begin).astype(F32)
    offs[pl.ds(total, 8), :] = jnp.zeros((8, 128), F32)
    t_swap = links.swap(tok, toks.at[mine], sw_s.at[0], sw_r.at[0])
    o_swap = links.swap(offs.at[mine], offs.at[mine], sw_s.at[1], sw_r.at[1])
    c_swap = links.swap(cot, cots.at[mine], sw_s.at[2], sw_r.at[2])
    c_copy = pltpu.make_async_copy(cot, cots.at[mine], lsem.at[0])
    g_i = gather_steps(links, part_i, wi, R["gi_s"], R["gi_r"])
    g_w = gather_steps(links, part_w, ww, R["gw_s"], R["gw_r"])
    g_i[0]()
    g_i[1]()
    t_swap.start()
    o_swap.start()
    toks[mine, :] = tok[...]
    for k in range(2, 8):
        g_i[k]()
    g_w[0]()
    for k in range(8, 15):
        g_i[k]()
    for k in range(1, 8):
        g_w[k]()
    g_i[15]()
    if near:
        for i in range(dp):
            for q in range(8):
                sm[core, i * 128 + q * 16:i * 128 + q * 16 + 16, :] = wi[i * pitch_i + own_d:i * pitch_i + own_d + 16, lane(q)]
        theirs = pl.ds(pl.multiple_of((1 - core) * half, half), half)
        s_swap = links.swap(sm.at[core, theirs], sm.at[core, theirs], sw_s.at[3], sw_r.at[3])
        s_swap.start()
    t_swap.wait()
    o_swap.wait()
    c_swap.start()
    c_copy.start()

    if near:
        gain = jnp.concatenate(
            [sm[core, pl.ds(i * 128 + c1 + N, 16), :].astype(F32)[taps + 3:taps + 4, :own_d] for i in range(dp)], axis=1)
    else:
        gain = R["f_gain"][...].astype(F32)

    def norm(t0):
        r = pl.ds(t0, 64)
        v = toks[r, :].astype(F32)
        inv = lax.rsqrt(jnp.mean(v * v, axis=-1, keepdims=True) + EPS)
        normed[r, :] = (v * inv * gain).astype(BF)

    tiles(total, norm, 64)
    xin[0:8, :] = jnp.zeros((8, half), F32)

    def in_proj(j):
        xin[pl.ds(8, total), pl.ds(j, 256)] = dot(normed[...], cols_of(wi, 0, pl.ds(j, 256)))

    tiles(half, in_proj, 256)
    own = pl.multiple_of(core * half, half)
    row = lax.broadcasted_iota(jnp.int32, (128, 128), 0)
    if near:
        s_swap.wait()
    for b in range(lanes):
        if near:
            one, two = sm[0, pl.ds(own + b * 128, 128), :], sm[1, pl.ds(own + b * 128, 128), :]
        else:
            one, two = R["f_one"][:, lane(b)], R["f_two"][:, lane(b)]
        one, two = one.astype(F32), two.astype(F32)
        par[:, lane(b)] = one
        select[:, lane(b)] = jnp.where(row < c1, one, 0.0).astype(BF)
        delta[:, lane(b)] = jnp.where(row < rank, two, 0.0).astype(BF)
    a2[...] = -jnp.exp(par[c1:c1 + N, :]) * LOG2E

    def conv_tile(t0):
        o = offs[pl.ds(t0, 64), :]
        for b in range(lanes):
            c = lane(b)
            v = xin[pl.ds(t0, 72), c]
            acc = par[r_fb:r_fb + 1, c]
            for j in range(taps):
                s = v[8 - j:72 - j]
                if j:
                    s = jnp.where(o >= float(j), s, 0.0)
                acc = acc + par[r_taps + taps - 1 - j:r_taps + taps - j, c] * s
            conv[pl.ds(t0, 64), c] = acc
            actl[pl.ds(t0, 64), c] = (acc * sigmoid(acc)).astype(BF)

    x_swaps = []
    for p in range(2):
        r = pl.ds(p * rows, rows)
        tiles((p + 1) * rows, conv_tile, 64, p * rows)
        xo[r, :] = dot(actl[r, :], select[...], NT)
        x_swaps.append(links.swap(xo.at[r], xr.at[r], sw_s.at[4 + 9 * p], sw_r.at[4 + 9 * p]))
        x_swaps[p].start()

    def dt_tile(t0):
        low = xo[pl.ds(t0, 64), :].astype(BF)
        for b in range(half // 256):
            pre2 = dot(low, delta[:, lane(b, 256)])
            for q in range(2):
                c = lane(2 * b + q)
                s = softplus(pre2[:, lane(q)] + par[r_db:r_db + 1, c])
                dt[pl.ds(t0, 64), c] = s
                cv = conv[pl.ds(t0, 64), c]
                dx[pl.ds(t0, 64), c] = s * (cv * sigmoid(cv))

    per = 128 // CH

    def cols_tile(i, _):
        t0 = pl.multiple_of(i * 128, 128)
        x = xo[pl.ds(t0, 128), :]
        t = x.T
        for q in range(per):
            btc[i * per + q] = t[rank:rank + N, q * CH:(q + 1) * CH]
            ctc[i * per + q] = t[rank + N:rank + 2 * N, q * CH:(q + 1) * CH]
        m = block_mask(128)
        cblk[pl.ds(t0, 128), :] = jnp.where(m, dot(x.astype(BF), pick(rank + N)), 0.0).astype(BF)
        bblk[pl.ds(t0, 128), :] = jnp.where(m, dot(x.astype(BF), pick(rank)), 0.0).astype(BF)
        return 0

    for p in range(2):
        r = pl.ds(p * rows, rows)
        x_swaps[p].wait()
        xo[r, :] += xr[r, :]
        tiles((p + 1) * rows, dt_tile, 64, p * rows)
        lax.fori_loop(p * rows // 128, (p + 1) * rows // 128, cols_tile, 0)

    steps = g_w[8:15]
    hp = hbuf.shape[1] // N
    hq = hp // CH
    n_blk = total // hp
    st[...] = jnp.zeros_like(st)
    lg = min(512, half)

    def kept(blk):
        return hs.at[pl.ds(pl.multiple_of(blk * hp * N, hp * N), hp * N)]

    def write_out(blk, slot):
        return pltpu.make_async_copy(hbuf.at[slot], kept(blk), hsem.at[slot])

    def f_block(blk, _):
        slot = lax.rem(blk, 2)

        @pl.when(blk >= 2)
        def _():
            write_out(blk - 2, slot).wait()

        def chunk(q):
            c = blk * hq + q
            t0 = pl.multiple_of(c * CH, CH)
            bt = btc[c]
            first = offs[pl.ds(t0, CH), :] == 0.0
            hb = hbuf.at[slot, pl.ds(pl.multiple_of(q * CH * N, CH * N), CH * N), :]
            for g in range(half // lg):
                ls = lane(g, lg)
                a = a2[:, ls]
                h = st[:, ls]
                ds, xs = jnp.where(jnp.concatenate([first] * (lg // 128), axis=1), BIG, dt[pl.ds(t0, CH), ls]), dx[pl.ds(t0, CH), ls]
                for k in range(CH):
                    d = jnp.broadcast_to(ds[k:k + 1], (N, lg))
                    v = jnp.broadcast_to(xs[k:k + 1], (N, lg))
                    w = jnp.broadcast_to(bt[:, k:k + 1], (N, lg))
                    h = jnp.exp2(d * a) * h + w * v
                    hb[k * N:(k + 1) * N, ls] = h.astype(BF)
                st[:, ls] = h
            y[pl.ds(t0, CH), :] = dot(cblk[pl.ds(t0, CH), :], hb[...])

        def several(p, _):
            for k, s in enumerate(steps):
                pl.when(blk * (hq // 2) + p == (6 + 4 * k) // 2)(s)
            for u in range(2):
                chunk(p * 2 + u)
            return 0

        lax.fori_loop(0, hq // 2, several, 0)

        @pl.when(blk < n_blk - 2)
        def _():
            write_out(blk, slot).start()

        return 0

    lax.fori_loop(0, n_blk, f_block, 0)
    c_copy.wait()
    c_swap.wait()

    accs[...] = jnp.zeros_like(accs)

    def gate_cols(j):
        gt[:, pl.ds(j, 256)] = dot(normed[...], cols_of(ww, 0, pl.ds(j, 256)))

        def gate_tile(t0):
            r = pl.ds(t0, 64)
            for q in range(2):
                c = pl.ds(pl.multiple_of(j + q * 128, 128), 128)
                cv = conv[r, c]
                scanned = y[r, c] + par[r_sk:r_sk + 1, c] * (cv * sigmoid(cv))
                y[r, c] = scanned
                g = gt[r, c]
                gated[r, c] = (scanned * (g * sigmoid(g))).astype(BF)

        tiles(total, gate_tile, 64)

    g_w[15]()
    tiles(half, gate_cols, 256)

    def outer(left, right, out):
        def body(i):
            for b in range(half // 512):
                out[pl.ds(i, 256), lane(b, 512)] = dot(left[:, pl.ds(i, 256)], right[:, lane(b, 512)], TN).astype(BF)
        tiles(width, body, 256)

    s_o = scatter_steps(links, d_out, R["red_o"], R["so_b"], R["so_s"], R["so_r"])
    s_g = scatter_steps(links, d_gate, R["red_g"], R["sg_b"], R["sg_s"], R["sg_r"])
    outer(cots, gated, d_out)
    s_o[0]()

    def grad_cols(j):
        qtmp[...] = dot(cots[...], cols_of(ww, own_d, pl.ds(j, 256)))

        def grad_tile(t0):
            r = pl.ds(t0, 64)
            for q in range(2):
                c = pl.ds(pl.multiple_of(j + q * 128, 128), 128)
                cv = conv[r, c]
                g = gt[r, c]
                sg = sigmoid(g)
                gg = qtmp[r, lane(q)]
                ggr[r, c] = (gg * y[r, c] * slope(g, sg)).astype(BF)
                G = gg * (g * sg)
                y[r, c] = G
                accs[0, :, c] += eighths(G * (cv * sigmoid(cv)))

        tiles(total, grad_tile, 64)

    tiles(half, grad_cols, 256)
    outer(normed, ggr, d_gate)
    s_g[0]()

    steps_b = s_o[1:9] + s_g[1:3] + [s_o[9]] + [s_g[3], s_g[4], s_g[5], s_g[6], s_g[7], s_g[8], s_g[9]]
    n_chunks = total // CH
    st[...] = jnp.zeros_like(st)
    racc[...] = jnp.zeros_like(racc)

    def read_back(blk, slot):
        return pltpu.make_async_copy(kept(blk), hbuf.at[slot], hsem.at[slot])

    def b_block(i, _):
        blk = n_blk - 1 - i
        slot = lax.rem(blk, 2)

        def chunk(q):
            c = blk * hq + q
            t0 = pl.multiple_of(c * CH, CH)
            before = jnp.where(q == 0, 1 - slot, slot)
            last = pl.multiple_of(jnp.where(q == 0, hp - 1, q * CH - 1) * N, N)
            ct = ctc[c]
            first = offs[pl.ds(t0, CH), :] == 0.0
            hb = hbuf.at[slot, pl.ds(pl.multiple_of(q * CH * N, CH * N), CH * N), :]
            hl = hbuf.at[before, pl.ds(last, N), :]
            for g in range(half // lg):
                ls = lane(g, lg)
                a = a2[:, ls]
                carry = st[:, ls]
                ra = racc[:, ls]
                ds, gs = jnp.where(jnp.concatenate([first] * (lg // 128), axis=1), BIG, dt[pl.ds(t0, CH), ls]), y[pl.ds(t0, CH), ls]
                for k in range(CH - 1, -1, -1):
                    d = jnp.broadcast_to(ds[k:k + 1], (N, lg))
                    gg = jnp.broadcast_to(gs[k:k + 1], (N, lg))
                    cc = jnp.broadcast_to(ct[:, k:k + 1], (N, lg))
                    h = hb[(k - 1) * N:k * N, ls] if k else hl[:, ls]
                    sg = cc * gg + carry
                    carry = jnp.exp2(d * a) * sg
                    term = carry * h.astype(F32)
                    ra = ra + term * d
                    sgs[k * N:(k + 1) * N, ls] = sg.astype(BF)
                    part = term * a
                    part = part[:N // 2] + part[N // 2:]
                    if k % 2:
                        odd = part
                    else:
                        das[k * N // 2:(k + 2) * N // 2, ls] = jnp.concatenate([part, odd], axis=0).astype(BF)
                st[:, ls] = carry
                racc[:, ls] = ra
            m = block_mask()
            m8 = jnp.where(lax.broadcasted_iota(jnp.int32, (CH, CH * N // 2), 1) // (N // 2)
                           == lax.broadcasted_iota(jnp.int32, (CH, CH * N // 2), 0), 1.0, 0.0).astype(BF)
            r = pl.ds(t0, CH)
            sgc = sgs[...]
            wout = dot(dx[r, :].astype(BF), sgc, NT)
            wgs[pl.ds(c, 1), :] = jnp.sum(jnp.where(m, wout, 0.0), axis=0, keepdims=True)
            rout = dot(y[r, :].astype(BF), hb[...], NT)
            rgs[pl.ds(c, 1), :] = jnp.sum(jnp.where(m, rout, 0.0), axis=0, keepdims=True)
            dx[r, :] = dot(bblk[r, :], sgc)
            gt[r, :] = dot(m8, das[...])

        def several(p, _):
            done = i * (hq ) + p
            for k, s in enumerate(steps_b):
                pl.when(done == 6 + (9 * k) // 4)(s)

            @pl.when((p == hq  - 1) & (blk >= 1) & (blk <= n_blk - 2))
            def _():
                read_back(blk - 1, 1 - slot).wait()

            for u in range(1):
                chunk(hq - 1 - (p  + u))
            return 0

        lax.fori_loop(0, hq , several, 0)

        @pl.when(blk >= 2)
        def _():
            read_back(blk - 2, slot).start()

        return 0

    lax.fori_loop(0, n_blk, b_block, 0)
    dg, low_b = dx, d_gate

    fins = [links.swap(R[k], R[k + "2"], sw_s.at[10 + n], sw_r.at[10 + n])
            for n, k in enumerate(("red_i", "red_g", "red_o"))]
    fins[1].start()
    fins[2].start()

    ln2 = math.log(2.0)

    def pre_tile(t0):
        r = pl.ds(t0, 64)
        for b in range(lanes):
            c = lane(b)
            cv = conv[r, c]
            act = cv * sigmoid(cv)
            v = (dg[r, c] * act + gt[r, c] * ln2) * (1.0 - jnp.exp(-dt[r, c]))
            low_b[r, c] = v.astype(BF)
            accs[1, :, c] += eighths(v)

    xg = qtmp.at[:, 0:128]

    def xg_tile(i, _):
        t0 = pl.multiple_of(i * 128, 128)
        r = pl.ds(t0, 128)
        m = block_mask(128)
        sums = dot(low_b[r, :], delta[...], NT)
        for ref, first in ((wgs, rank), (rgs, rank + N)):
            v = ref[pl.ds(pl.multiple_of(i * per, per), per), :]
            v = jnp.broadcast_to(v[:, None, :], (per, CH, CH * N)).reshape(128, CH * N)
            v = jnp.where(m, v, 0.0)
            hi = v.astype(BF)
            lo = (v - hi.astype(F32)).astype(BF)
            p = place(first)
            sums = sums + dot(hi, p) + dot(lo, p)
        xg[r, :] = sums
        return 0

    g_swaps = []
    for p in range(2):
        r = pl.ds(p * rows, rows)
        tiles((p + 1) * rows, pre_tile, 64, p * rows)
        lax.fori_loop(p * rows // 128, (p + 1) * rows // 128, xg_tile, 0)
        g_swaps.append(links.swap(xg.at[r], R["xr2"].at[r], sw_s.at[6 + 8 * p], sw_r.at[6 + 8 * p]))
        g_swaps[p].start()
    sgrad = R["sgrad"]
    xob = xo[...].astype(BF)
    for b in range(half // 256):
        sgrad[1, :, lane(b, 256)] = dot(xob, low_b[0:total, lane(b, 256)], TN)
    def project(which, out):
        def body(i, _):
            out(pl.multiple_of(i * 256, 256), dot(gated[which, :], rows_of(ww, own_d, i), NT))
            return 0
        lax.fori_loop(0, width // 256, body, 0)

    msent, mcame = hbuf.at[0, pl.ds(0, rows), :], hbuf.at[1, pl.ds(0, rows), :]

    def put_mixed(j, v):
        msent[:, pl.ds(j, 256)] = v.astype(BF)

    project(other, put_mixed)
    for p in range(2):
        g_swaps[p].wait()
    xg[...] = xg[...] + R["xr2"][...]
    m_swap = links.swap(msent, mcame, sw_s.at[5], sw_r.at[5])
    m_swap.start()
    xgb = xg[...].astype(BF)
    for b in range(half // 256):
        sgrad[0, :, lane(b, 256)] = dot(xgb, actl[:, lane(b, 256)], TN)

    quarter = half // 2
    ig = d_gate
    d_in = d_out
    y[pl.ds(total, 8), :] = jnp.zeros((8, half), F32)

    def conv_back(h):
        def cg_tile(t0):
            r = pl.ds(t0, 64)
            low = xg[r, :].astype(BF)
            for b in range(h * quarter // 256, (h + 1) * quarter // 256):
                back = dot(low, select[:, lane(b, 256)])
                for q in range(2):
                    c = lane(2 * b + q)
                    ag = y[r, c] * par[r_sk:r_sk + 1, c] + dg[r, c] * dt[r, c] + back[:, lane(q)]
                    cv = conv[r, c]
                    v = ag * slope(cv, sigmoid(cv))
                    y[r, c] = v
                    accs[2, :, c] += eighths(v)

        tiles(total, cg_tile, 64)

        def ig_tile(t0):
            o = offs[pl.ds(t0, 72), :]
            for b in range(h * quarter // 128, (h + 1) * quarter // 128):
                c = lane(b)
                v = y[pl.ds(t0, 72), c]
                x = xin[pl.ds(t0, 72), c]
                acc = jnp.zeros((64, 128), F32)
                for j in range(taps):
                    mv = jnp.where(o >= float(j), v, 0.0) if j else v
                    accs[3 + taps - 1 - j, :, c] += eighths(mv[0:64] * x[8 - j:72 - j])
                    acc = acc + mv[j:64 + j] * par[r_taps + taps - 1 - j:r_taps + taps - j, c]
                ig[pl.ds(t0, 64), c] = acc.astype(BF)

        tiles(total, ig_tile, 64)

        def outer_tile(i, _):
            v = dot(normed[:, pl.ds(pl.multiple_of(i * 256, 256), 256)], ig[0:total, lane(h, quarter)], TN).astype(BF)
            d_in[pl.ds(pl.multiple_of(i * 256, 256), 256), lane(h, quarter)] = v
            return 0

        lax.fori_loop(0, width // 256, outer_tile, 0)

    def half_scatter(h):
        def part(ref):
            return ref.at[(slice(None),) * (len(ref.shape) - 1) + (lane(h, quarter),)]
        bufs = [part(b) for b in R["so_b"]] if near else [R[("so_b", "sg_b")[h]][0].at[:, :, lane(h, quarter)], None, None]
        return scatter_steps(links, part(d_in), part(R["red_i"]), bufs, R["si_s" if h == 0 else "sj_s"], R["si_r" if h == 0 else "sj_r"])

    s_i, s_j = half_scatter(0), half_scatter(1)
    conv_back(0)
    s_i[0]()
    conv_back(1)
    s_j[0]()
    s_i[1]()
    s_i[2]()
    s_i[3]()
    s_i[4]()

    def back_project(which, out):
        def body(i, _):
            out(pl.multiple_of(i * 256, 256),
                dot(ig[which, :], rows_of(wi, 0, i), NT) + dot(ggr[which, :], rows_of(ww, 0, i), NT))
            return 0
        lax.fori_loop(0, width // 256, body, 0)

    def put_send(j, v):
        msend[:, pl.ds(j, 256)] = v.astype(BF)

    back_project(other, put_send)
    n_swap = links.swap(msend, mrecv, sw_s.at[7], sw_r.at[7])
    n_swap.start()
    s_i[5]()
    s_i[6]()
    s_j[1]()
    s_j[2]()
    ng = R["mixed_f"]

    def put_ng(j, v):
        ng[:, pl.ds(j, 256)] = v

    back_project(mine, put_ng)

    vecs = jnp.concatenate(
        [racc[...] * a2[...] * ln2]
        + [jnp.sum(accs[3 + k], axis=0, keepdims=True) for k in range(taps)]
        + [jnp.sum(accs[2], axis=0, keepdims=True), jnp.sum(accs[1], axis=0, keepdims=True),
           jnp.sum(accs[0], axis=0, keepdims=True), jnp.zeros((16 - taps - 3, half), F32)], axis=0)
    sgrad[0, c1:128, :] = vecs
    sgrad[1, rank:128, :] = jnp.zeros((128 - rank, half), F32)
    if near:
        small, away = R["small"], R["away"]
        for b in range(lanes):
            small[pl.ds(own + b * 128, 128), :] = sgrad[core, :, lane(b)].astype(BF)
            away[lane(b), :] = sgrad[1 - core, :, lane(b)].astype(BF)
        a_swap = links.swap(away, small.at[pl.ds(own, half), :], sw_s.at[8], sw_r.at[8])
        a_swap.start()
        red_s = R["o_small"]
        s_s = scatter_steps(links, small, red_s.at[core], R["ss_b"], R["ss_s"], R["ss_r"])
    else:
        s_s = [lambda: None] * 10
    s_i[7]()
    s_i[8]()
    s_j[3]()
    s_j[4]()
    if near:
        a_swap.wait()
    s_s[0]()
    n_swap.wait()
    def tok_tile(t0):
        r = pl.ds(t0, 32)
        v = tok[r, :].astype(F32)
        inv = lax.rsqrt(jnp.mean(v * v, axis=-1, keepdims=True) + EPS)
        sc = v * inv
        n = ng[r, :] + mrecv[r, :].astype(F32)
        sg = n * gain
        ng[r, :] = cots[pl.ds(pl.multiple_of(core * rows + t0, 32), 32), :].astype(F32) + inv * (
            sg - sc * jnp.mean(sg * sc, axis=-1, keepdims=True))

    tiles(rows, tok_tile, 32)
    t_copy = pltpu.make_async_copy(ng, R["tgrad"], lsem.at[1])
    t_copy.start()
    s_j[5]()
    s_i[9]()
    m_swap.wait()
    def put_own(j, v):
        R["mixed"][:, pl.ds(j, 256)] = (
            tok[:, pl.ds(j, 256)].astype(F32) + v + mcame[:, pl.ds(j, 256)].astype(F32)).astype(BF)

    project(mine, put_own)
    s_s[1]()
    s_s[2]()
    s_j[6]()
    if not near:
        R["f_grad"][...] = sgrad[...]
    s_j[7]()
    for k in range(3, 7):
        s_s[k]()
    s_j[8]()
    for k in range(7, 10):
        s_s[k]()
    if near:
        fs = links.swap(red_s.at[core], red_s.at[core], sw_s.at[9], sw_r.at[9])
        fs.start()
    s_j[9]()
    t_copy.wait()

    fins[0].start()

    def share(first, k, out):
        R[out][:, pl.ds(pl.multiple_of(first + core * half, 128), half)] = R[k][...]
        R[out][:, pl.ds(pl.multiple_of(first + (1 - core) * half, 128), half)] = R[k + "2"][...]

    fins[1].wait()
    share(inner, "red_g", "o_in")
    fins[2].wait()
    share(0, "red_o", "o_out")
    if near:
        fs.wait()
    fins[0].wait()
    share(0, "red_i", "o_in")


def layer(inputs, dp, dims):
    rows, width = inputs["tok"].shape
    half = inputs["w_o"].shape[1] // 2
    inner = 2 * half
    total = 2 * rows
    taps, rank = dims
    own_d, own_e = width // dp, inner // dp
    n = copies_of(dp)
    near = bool(plane(dp))
    extra = 16 if near else 0
    sd = jax.ShapeDtypeStruct
    vm = pl.BlockSpec(memory_space=pltpu.VMEM)
    hbm = pl.BlockSpec(memory_space=pl.ANY)
    dma = pltpu.SemaphoreType.DMA
    V = pltpu.VMEM
    outs = {
        "mixed": sd((rows, width), BF), "tgrad": sd((rows, width), F32),
        "o_in": sd((own_d, 2 * inner), F32), "o_out": sd((own_d, inner), F32), "hs": sd((total * N, half), BF),
    }
    if near:
        outs["o_small"] = sd((2, 128, own_e), F32)
    else:
        outs["f_grad"] = sd((2, 128, half), F32)
    f2 = V((total, half), F32)
    scratch = {
        "part_i": V((own_d + extra, half), BF), "part_w": V((2 * own_d, half), BF),
        "wi": V((dp * (own_d + extra), half), BF), "ww": V((2 * width, half), BF), "select": V((128, half), BF), "delta": V((128, half), BF),
        "toks": V((total, width), BF), "cots": V((total, width), BF), "normed": V((total, width), BF),
        "offs": V((total + 8, 128), F32), "xin": V((total + 8, half), F32), "conv": f2, "actl": V((total, half), BF),
        "dt": f2, "gt": f2, "dx": f2, "y": V((total + 8, half), F32), "ggr": V((total, half), BF),
        "xo": V((total, 128), F32), "xr": V((total, 128), F32), "xr2": V((total, 128), F32),
        "hbuf": V((2, 64 * N, half), BF), "par": V((128, half), F32),
        "btc": V((total // CH, N, CH), F32), "ctc": V((total // CH, N, CH), F32),
        "cblk": V((total, CH * N), BF), "bblk": V((total, CH * N), BF),
        "a2": V((N, half), F32), "st": V((N, half), F32), "racc": V((N, half), F32),
        "qtmp": V((total, 256), F32),
        "sgs": V((CH * N, half), BF), "das": V((CH * N // 2, half), BF),
        "wgs": V((total // CH, CH * N), F32), "rgs": V((total // CH, CH * N), F32),
        "accs": V((3 + taps, 8, half), F32), "d_out": V((width, half), BF), "d_gate": V((width, half), BF),
        "msend": V((rows, width), BF), "mrecv": V((rows, width), BF), "mixed_f": V((rows, width), F32),
        "sgrad": V((2, 128, half), F32),
        "so_b": scatter_scratch(dp, own_d, half), "sg_b": scatter_scratch(dp, own_d, half),
        "sw_s": dma((15,)), "sw_r": dma((15,)), "hsem": dma((2,)), "lsem": dma((2,)),
    }
    for k in ("i", "g", "o"):
        scratch["red_" + k] = V((own_d, half), F32)
        scratch["red_" + k + "2"] = V((own_d, half), F32)
    if near:
        scratch["sm"] = V((2, inner, own_e), BF)
        scratch["small"], scratch["away"] = V((inner, own_e), BF), V((half, own_e), BF)
        scratch["ss_b"] = scatter_scratch(dp, 128, own_e)
    for k in ("gi", "gw", "si", "sj", "sg", "so", "ss"):
        scratch[k + "_s"] = dma((n,))
        scratch[k + "_r"] = dma((n,))
    names = list(inputs) + list(outs) + list(scratch)
    res = pl.pallas_call(
        functools.partial(layer_kernel, dp=dp, dims=dims, names=names),
        out_shape=list(outs.values()),
        in_specs=[pl.BlockSpec(memory_space=pltpu.SMEM) if k == "lens" else hbm if k == "cot" else vm for k in inputs],
        out_specs=[hbm if k in ("tgrad", "hs") else vm for k in outs],
        scratch_shapes=list(scratch.values()),
        compiler_params=pltpu.CompilerParams(collective_id=0, has_side_effects=True, vmem_limit_bytes=127 << 19),
        name="layer",
    )(*inputs.values())
    return dict(zip(outs, res))


def local(
    tokens,
    doc_lengths,
    cotangent,
    norm_gain,
    input_weight,
    filter_weight,
    filter_bias,
    select_weight,
    delta_weight,
    delta_bias,
    decay_log,
    skip_gain,
    output_weight,
    *,
    dp,
):
    rows, length, width = tokens.shape
    rank = delta_weight.shape[1]
    taps = filter_weight.shape[1]
    own_e = filter_weight.shape[0]
    own_d = norm_gain.shape[0]
    inner = own_e * dp
    c1 = rank + 2 * N
    inputs = {
        "lens": doc_lengths, "tok": tokens.reshape(rows * length, width), "cot": cotangent.reshape(rows * length, width),
        "w_in": input_weight, "w_o": output_weight,
    }
    if plane(dp):
        inputs.update(
            s_select=select_weight.T, s_decay=decay_log.T, s_delta=delta_weight.T, s_filter=filter_weight.T,
            s_fb=filter_bias[None], s_db=delta_bias[None], s_skip=skip_gain[None], s_gain=norm_gain[None],
        )
    else:
        core = lax.axis_index("rep")
        vectors = jnp.stack([filter_bias, delta_bias, skip_gain])
        tail = jnp.concatenate([filter_weight.T, vectors, jnp.zeros((16 - taps - 3, own_e), BF)], axis=0)
        one = jnp.concatenate([select_weight.T, decay_log.T, tail], axis=0)
        two = jnp.concatenate([delta_weight.T, jnp.zeros((128 - rank, own_e), BF)], axis=0)
        both = lax.all_gather(jnp.stack([one, two]), "dp", axis=2, tiled=True)
        both = lax.dynamic_slice(both, (0, 0, core * (inner // 2)), (2, 128, inner // 2))
        inputs.update(f_one=both[0], f_two=both[1], f_gain=lax.all_gather(norm_gain, "dp", axis=0, tiled=True)[None])
    r = layer(inputs, dp, (taps, rank))
    if plane(dp):
        small = r["o_small"]
    else:
        small = lax.all_gather(r["f_grad"], "rep", axis=2, tiled=True)
        small = lax.psum_scatter(small, "dp", scatter_dimension=2, tiled=True)
    o = finish(r["mixed"], r["tgrad"], r["o_in"], r["o_out"], small, input_weight, norm_gain[None], (taps, rank))
    return (
        o[0].reshape(rows, length, width),
        o[1].reshape(rows, length, width),
        o[4].reshape(own_d),
        o[2],
        o[5].T,
        o[6].reshape(own_e),
        o[7].T,
        o[8].T,
        o[9].reshape(own_e),
        o[10].T,
        o[11].reshape(own_e),
        o[3],
    )


def finish(mixed, tgrad, o_in, o_out, small, w_in, gain, dims):
    taps, rank = dims
    c1 = rank + 2 * N
    own_e, own_d = small.shape[2], w_in.shape[0]
    sd = jax.ShapeDtypeStruct
    big = [mixed, tgrad, o_in, o_out]
    parts = 2

    def kernel(*refs):
        ins, small_ref, w_ref, gain_ref, outs, acc = refs[:4], refs[4], refs[5], refs[6], refs[7:19], refs[19]
        for i, o in zip(ins, outs[:4]):
            o[...] = i[...]
        p = w_ref[...].astype(F32) * ins[2][...]
        total = p[:, 0:128]
        for b in range(1, p.shape[1] // 128):
            total = total + p[:, b * 128:(b + 1) * 128]
        g = c1 + N + taps + 3

        @pl.when(pl.program_id(0) == 0)
        def _():
            acc[...] = jnp.zeros_like(acc)
            outs[5][...] = small_ref[0, c1 + N:c1 + N + taps, :]
            outs[6][...] = small_ref[0, g - 3:g - 2, :]
            outs[7][...] = small_ref[0, 0:c1, :]
            outs[8][...] = small_ref[1, 0:rank, :]
            outs[9][...] = small_ref[0, g - 2:g - 1, :]
            outs[10][...] = small_ref[0, c1:c1 + N, :]
            outs[11][...] = small_ref[0, g - 1:g, :]

        acc[0:own_d, :] += total

        @pl.when(pl.program_id(0) == parts - 1)
        def _():
            row = jnp.sum(acc[...].T, axis=0, keepdims=True)[:, :own_d]
            outs[4][...] = row / gain_ref[...].astype(F32)

    shapes = [sd(b.shape, b.dtype) for b in big] + [
        sd(s, F32) for s in ((1, own_d), (taps, own_e), (1, own_e), (c1, own_e), (rank, own_e), (1, own_e), (N, own_e), (1, own_e))]
    specs = [pl.BlockSpec((b.shape[0], b.shape[1] // parts), lambda i: (0, i)) for b in big]

    def whole(s):
        return pl.BlockSpec(s.shape, lambda i, n=len(s.shape): (0,) * n)

    wide = pl.BlockSpec((own_d, w_in.shape[1] // parts), lambda i: (0, i))
    return pl.pallas_call(
        kernel, grid=(parts,), out_shape=shapes, in_specs=specs + [whole(small), wide, whole(gain)],
        out_specs=specs + [whole(s) for s in shapes[4:]], scratch_shapes=[pltpu.VMEM((128, 128), F32)], name="finish",
    )(*big, small, w_in, gain)


def solution(mesh):
    dp_rep = ("dp", "rep")
    one = P("dp")
    two = P("dp", None)
    three = P(dp_rep, None, None)
    return jax.shard_map(
        functools.partial(local, dp=mesh.shape["dp"]),
        mesh=mesh,
        in_specs=(three, P(dp_rep, None), three, one, two, two, one, two, two, one, two, one, two),
        out_specs=(three, three, one, two, two, one, two, two, one, two, one, two),
        check_vma=False,
    )
```

```python
import functools
import math

import jax
import jax.numpy as jnp
from jax import lax
from jax.experimental import pallas as pl
from jax.experimental.pallas import tpu as pltpu
from jax.sharding import PartitionSpec as P

EPS = 1e-05
CH = 16
N = 16
F32 = jnp.float32
BF = jnp.bfloat16
NT = (((1,), (1,)), ((), ()))
TN = (((0,), (0,)), ((), ()))
BIG = 1e30
LOG2E = math.log2(math.e)


def dot(a, b, dims=(((1,), (0,)), ((), ()))):
    return lax.dot_general(a, b, dims, preferred_element_type=F32)


MESH = pl.DeviceIdType.MESH


def plane(dp):
    return 4 if dp == 16 else 0


class Links:
    def __init__(self, dp):
        self.dp = dp
        self.depth = plane(dp)
        self.me = lax.axis_index("dp")
        self.core = lax.axis_index("rep")
        if self.depth:
            self.z, self.y, self.x = self.me // 4, (self.me // 2) % 2, self.me % 2
            self.xn = self.at(self.z, self.y, 1 - self.x)
            self.yn = self.at(self.z, 1 - self.y, self.x)
            self.zs = [self.at(self.up(k), self.y, self.x) for k in range(1, self.depth)]
            self.peers = self.zs + [self.xn, self.yn]
        else:
            self.peers = [lax.rem(self.me + k, dp) for k in range(1, dp)]

    def up(self, k):
        return lax.rem(self.z + k, self.depth)

    def down(self, k):
        return lax.rem(self.z + self.depth - k, self.depth)

    def at(self, z, y, x):
        return (z * 2 + y) * 2 + x

    def barrier(self, sibling=True):
        sem = pltpu.get_barrier_semaphore()
        for peer in self.peers:
            pl.semaphore_signal(sem, inc=1, device_id=(peer, self.core), device_id_type=MESH)
        if sibling:
            pl.semaphore_signal(sem, inc=1, device_id=(self.me, 1 - self.core), device_id_type=MESH)
        pl.semaphore_wait(sem, len(self.peers) + int(sibling))

    def send(self, src, dst, send_sem, recv_sem, chip):
        return pltpu.make_async_remote_copy(
            src_ref=src, dst_ref=dst, send_sem=send_sem, recv_sem=recv_sem,
            device_id=(chip, self.core), device_id_type=MESH,
        )

    def swap(self, src, dst, send_sem, recv_sem):
        return pltpu.make_async_remote_copy(
            src_ref=src, dst_ref=dst, send_sem=send_sem, recv_sem=recv_sem,
            device_id=(self.me, 1 - self.core), device_id_type=MESH,
        )


def copies_of(dp):
    return 34 if plane(dp) else dp - 1


def gather_steps(links, src, dst, ss, rs):
    me = links.me
    rows = src.shape[0]

    def part(b, first=0, count=rows):
        return pl.ds(pl.multiple_of(b * rows + first, math.gcd(rows, count)), count)

    if not links.depth:
        cps = [links.send(src, dst.at[part(me)], ss.at[k], rs.at[k], p) for k, p in enumerate(links.peers)]

        def begin():
            for c in cps:
                c.start()
            dst[part(me), :] = src[...]

        def end():
            for c in cps:
                c.wait()

        return [begin] + [lambda: None] * 14 + [end]
    depth, half = links.depth, rows // 2
    cuts = [half if half % 16 == 0 else half + (8 if i % 2 else -8) for i in range(2 * depth - 1)]
    z, y, x, xn, yn = links.z, links.y, links.x, links.xn, links.yn
    origin = [z] + [jnp.maximum(z - d, 0) for d in range(1, depth)] + [jnp.minimum(z + d, depth - 1) for d in range(1, depth)]
    there = [z >= 0] + [z >= d for d in range(1, depth)] + [z + d < depth for d in range(1, depth)]
    up, down, up_on, down_on = {}, {}, {}, {}
    above, below = links.at(jnp.minimum(z + 1, depth - 1), y, x), links.at(jnp.maximum(z - 1, 0), y, x)
    for d in range(1, depth):
        b = links.at(origin[d - 1], y, x)
        s = src if d == 1 else dst.at[part(b)]
        up[d] = links.send(s, dst.at[part(b)], ss.at[d - 1], rs.at[d - 1], above)
        up_on[d] = (z < depth - 1) & (z >= d - 1)
        b = links.at(origin[0 if d == 1 else d + 2], y, x)
        s = src if d == 1 else dst.at[part(b)]
        down[d] = links.send(s, dst.at[part(b)], ss.at[d + 2], rs.at[d + 2], below)
        down_on[d] = (z > 0) & (z + d - 1 < depth)
    xc, yc, xf, yf = [], [], [], []
    for i in range(2 * depth - 1):
        b = links.at(origin[i], y, x)
        s = src if i == 0 else dst.at[part(b)]
        n = 6 + 4 * i
        xc.append(links.send(s, dst.at[part(b)], ss.at[n], rs.at[n], xn))
        yc.append(links.send(s, dst.at[part(b)], ss.at[n + 1], rs.at[n + 1], yn))
        lo = dst.at[part(links.at(origin[i], y, 1 - x), 0, cuts[i])]
        hi = dst.at[part(links.at(origin[i], 1 - y, x), cuts[i], rows - cuts[i])]
        yf.append(links.send(lo, lo, ss.at[n + 2], rs.at[n + 2], yn))
        xf.append(links.send(hi, hi, ss.at[n + 3], rs.at[n + 3], xn))

    def begin():
        pl.when(up_on[1])(up[1].start)
        pl.when(down_on[1])(down[1].start)

    def beside():
        xc[0].start()
        yc[0].start()
        dst[part(me), :] = src[...]

    def spread(i):
        chain, on, d = (up, up_on, i) if i < depth else (down, down_on, i - depth + 1)

        def run():
            @pl.when(there[i])
            def _():
                chain[d].wait_recv()
                if d + 1 < depth:
                    pl.when(on[d + 1])(chain[d + 1].start)
                xc[i].start()
                yc[i].start()
        return run

    def forward(i):
        def run():
            @pl.when(there[i])
            def _():
                xc[i].wait_recv()
                yf[i].start()
                yc[i].wait_recv()
                xf[i].start()
        return run

    def end():
        for i in range(2 * depth - 1):
            @pl.when(there[i])
            def _(i=i):
                yf[i].wait_recv()
                xf[i].wait_recv()
                for c in (xc[i], yc[i], xf[i], yf[i]):
                    c.wait_send()
        for d in range(1, depth):
            pl.when(up_on[d])(up[d].wait_send)
            pl.when(down_on[d])(down[d].wait_send)

    f = forward
    return [begin, beside] + [spread(i) for i in (1, 4, 2, 5, 3, 6)] + [f(i) for i in (0, 1, 4, 2, 5, 3, 6)] + [end]


def scatter_scratch(dp, rows, cols):
    if not plane(dp):
        return [pltpu.VMEM((dp - 1, rows, cols), BF)] + [pltpu.VMEM((8, 128), BF)] * 2
    d, h = plane(dp), rows // 2
    return [
        pltpu.VMEM((d, 2, h, cols), BF),
        pltpu.VMEM((d, 2, rows, cols), BF),
        pltpu.VMEM((d - 1, rows, cols), BF),
    ]


def scatter_steps(links, src, out, bufs, ss, rs, offset=0):
    me = links.me
    rows = out.shape[0]
    pitch = src.shape[0] // links.dp

    def part(b, first=0, count=rows):
        return pl.ds(pl.multiple_of(b * pitch + offset + first, math.gcd(math.gcd(pitch, offset + first), count)), count)

    if not links.depth:
        got = bufs[0]
        cps = [links.send(src.at[part(p)], got.at[k], ss.at[k], rs.at[k], p) for k, p in enumerate(links.peers)]

        def begin():
            for c in cps:
                c.start()

        def end():
            for c in cps:
                c.wait()

            def add(k, total):
                return total + got[k].astype(F32)

            out[...] = lax.fori_loop(0, links.dp - 1, add, src[part(me), :].astype(F32))

        return [begin] + [lambda: None] * 8 + [end]
    halves, come, zcome = bufs
    depth = links.depth
    h = rows // 2
    y, x, xn, yn = links.y, links.x, links.xn, links.yn
    ac, bc, cc = [], [], []
    for k in range(depth):
        zz = links.up(k)
        diag = links.at(zz, 1 - y, 1 - x)
        bx = links.at(zz, y, 1 - x)
        by = links.at(zz, 1 - y, x)
        own = links.at(zz, y, x)
        n = 4 * k
        ac.append((
            links.send(src.at[part(diag, 0, h)], halves.at[k, 0], ss.at[n], rs.at[n], xn),
            links.send(src.at[part(diag, h, h)], halves.at[k, 1], ss.at[n + 1], rs.at[n + 1], yn),
        ))
        bc.append((
            links.send(src.at[part(bx)], come.at[k, 0], ss.at[n + 2], rs.at[n + 2], xn),
            links.send(src.at[part(by)], come.at[k, 1], ss.at[n + 3], rs.at[n + 3], yn),
        ))
        if k:
            n = 4 * depth + k - 1
            cc.append(links.send(src.at[part(own)], zcome.at[k - 1], ss.at[n], rs.at[n], links.zs[k - 1]))

    def add(where, more):
        src[where, :] = (src[where, :].astype(F32) + more.astype(F32)).astype(BF)

    def begin():
        for k in (1, 2, 3, 0):
            ac[k][0].start()
            ac[k][1].start()

    def middle(k):
        def run():
            zz = links.up(k)
            ac[k][0].wait_recv()
            add(part(links.at(zz, 1 - y, x), 0, h), halves[k, 0])
            bc[k][1].start()
            ac[k][1].wait_recv()
            add(part(links.at(zz, y, 1 - x), h, h), halves[k, 1])
            bc[k][0].start()
        return run

    def along(k):
        def run():
            bc[k][0].wait_recv()
            bc[k][1].wait_recv()
            own = part(links.at(links.up(k), y, x))
            total = src[own, :].astype(F32) + come[k, 0].astype(F32) + come[k, 1].astype(F32)
            if k:
                src[own, :] = total.astype(BF)
                cc[k - 1].start()
            else:
                out[...] = total
        return run

    def end():
        for k in range(depth - 1):
            cc[k].wait_recv()
            out[...] += zcome[k].astype(F32)
        for k in range(depth):
            for c in ac[k] + bc[k]:
                c.wait_send()
        for c in cc:
            c.wait_send()

    return [begin, middle(1), middle(2), along(1), middle(3), along(2), middle(0), along(3), along(0), end]


def sigmoid(v):
    return 0.5 * jnp.tanh(0.5 * v) + 0.5


def softplus(v):
    u = jnp.exp(-jnp.abs(v))
    return jnp.maximum(v, 0.0) + jnp.where(u < 1e-3, u * (1.0 - 0.5 * u), jnp.log(1.0 + u))


def slope(v, s):
    return s * (1.0 + v * (1.0 - s))


def block_mask(rows=CH):
    r = lax.broadcasted_iota(jnp.int32, (rows, CH * N), 0)
    c = lax.broadcasted_iota(jnp.int32, (rows, CH * N), 1)
    return (c // N) == (r % CH)


def pick(first):
    r = lax.broadcasted_iota(jnp.int32, (128, CH * N), 0)
    c = lax.broadcasted_iota(jnp.int32, (128, CH * N), 1)
    return jnp.where(r - first == c % N, 1.0, 0.0).astype(BF)


def place(first):
    r = lax.broadcasted_iota(jnp.int32, (CH * N, 128), 0)
    c = lax.broadcasted_iota(jnp.int32, (CH * N, 128), 1)
    return jnp.where(c - first == r % N, 1.0, 0.0).astype(BF)


def eighths(v):
    return jnp.sum(v.reshape(v.shape[0] // 8, 8, v.shape[1]), axis=0)


def layer_kernel(*refs, dp, dims, names):
    R = dict(zip(names, refs))
    lens, tok, cot, w_in, w_o = (R[k] for k in ("lens", "tok", "cot", "w_in", "w_o"))
    wi, ww, toks, cots, normed = (R[k] for k in ("wi", "ww", "toks", "cots", "normed"))
    select, delta = R["select"], R["delta"]
    offs, xin, conv, actl, dt, gt, dx, y = (R[k] for k in ("offs", "xin", "conv", "actl", "dt", "gt", "dx", "y"))
    ggr, xo, xr, hs, hbuf = (R[k] for k in ("ggr", "xo", "xr", "hs", "hbuf"))
    par, btc, ctc, cblk, bblk, a2, st, racc = (R[k] for k in ("par", "btc", "ctc", "cblk", "bblk", "a2", "st", "racc"))
    qtmp, sgs, das, wgs, rgs, accs = (R[k] for k in ("qtmp", "sgs", "das", "wgs", "rgs", "accs"))
    d_out, d_gate, msend, mrecv, sw_s, sw_r, hsem, lsem = (
        R[k] for k in ("d_out", "d_gate", "msend", "mrecv", "sw_s", "sw_r", "hsem", "lsem"))
    taps, rank = dims
    links = Links(dp)
    core, me = links.core, links.me
    rows, width = tok.shape
    half = wi.shape[1]
    total = 2 * rows
    own_d = w_in.shape[0]
    inner = 2 * half
    own_e = inner // dp
    lanes = half // 128
    c1 = rank + 2 * N
    r_taps, r_fb, r_db, r_sk, gcol = (c1 + N + k for k in (0, taps, taps + 1, taps + 2, taps + 3))
    gated = toks

    def cut(ref, start):
        return ref[:, pl.ds(pl.multiple_of(start + core * half, 128), half)]

    pitch_i, pitch_w = wi.shape[0] // dp, 2 * own_d

    def cols_of(ref, first, c):
        v = ref[:, c]
        return v.reshape(dp, ref.shape[0] // dp, v.shape[1])[:, first:first + own_d].reshape(width, v.shape[1])

    def rows_of(ref, first, i):
        n = 256 // own_d
        p = ref.shape[0] // dp
        v = ref[pl.ds(pl.multiple_of(i * n * p, n * p), n * p), :]
        return v.reshape(n, p, half)[:, first:first + own_d].reshape(256, half)

    def lane(b, n=128):
        return slice(b * n, (b + 1) * n)

    def tiles(n, body, size, start=0):
        def run(i, _):
            body(pl.multiple_of(i * size, size))
            return 0
        lax.fori_loop(start // size, n // size, run, 0)

    near = bool(links.depth)
    part_i, part_w = R["part_i"], R["part_w"]
    part_i[0:own_d, :] = cut(w_in, 0)
    part_w[0:own_d, :] = cut(w_in, inner)
    part_w[own_d:, :] = cut(w_o, 0)
    if near:
        sm = R["sm"]
        tail = jnp.concatenate(
            [R[k][...].astype(F32) for k in ("s_filter", "s_fb", "s_db", "s_skip")]
            + [jnp.concatenate([R["s_gain"][...].astype(F32), jnp.zeros((1, own_e - own_d), F32)], axis=1),
               jnp.zeros((16 - taps - 4, own_e), F32)], axis=0).astype(BF)
        for q in range(8):
            one = R["s_select"][q * 16:q * 16 + 16, :] if q < c1 // 16 else R["s_decay"][...] if q < 7 else tail
            two = R["s_delta"][q * 16:q * 16 + 16, :] if q < rank // 16 else tail
            part_i[own_d:own_d + 16, lane(q)] = jnp.where(core == 0, one.astype(F32), two.astype(F32)).astype(BF)
    links.barrier()
    mine = pl.ds(pl.multiple_of(core * rows, rows), rows)
    other = pl.ds(pl.multiple_of((1 - core) * rows, rows), rows)
    t_idx = lax.broadcasted_iota(jnp.int32, (rows, 128), 0)
    begin = jnp.zeros((rows, 128), jnp.int32)
    start = lens[0, 0]
    for k in range(1, lens.shape[1]):
        begin = jnp.where(t_idx >= start, start, begin)
        start = start + lens[0, k]
    offs[mine, :] = (t_idx - begin).astype(F32)
    offs[pl.ds(total, 8), :] = jnp.zeros((8, 128), F32)
    t_swap = links.swap(tok, toks.at[mine], sw_s.at[0], sw_r.at[0])
    o_swap = links.swap(offs.at[mine], offs.at[mine], sw_s.at[1], sw_r.at[1])
    c_swap = links.swap(cot, cots.at[mine], sw_s.at[2], sw_r.at[2])
    c_copy = pltpu.make_async_copy(cot, cots.at[mine], lsem.at[0])
    g_i = gather_steps(links, part_i, wi, R["gi_s"], R["gi_r"])
    g_w = gather_steps(links, part_w, ww, R["gw_s"], R["gw_r"])
    g_i[0]()
    g_i[1]()
    t_swap.start()
    o_swap.start()
    toks[mine, :] = tok[...]
    for k in range(2, 8):
        g_i[k]()
    g_w[0]()
    for k in range(8, 15):
        g_i[k]()
    for k in range(1, 8):
        g_w[k]()
    g_i[15]()
    if near:
        for i in range(dp):
            for q in range(8):
                sm[core, i * 128 + q * 16:i * 128 + q * 16 + 16, :] = wi[i * pitch_i + own_d:i * pitch_i + own_d + 16, lane(q)]
        theirs = pl.ds(pl.multiple_of((1 - core) * half, half), half)
        s_swap = links.swap(sm.at[core, theirs], sm.at[core, theirs], sw_s.at[3], sw_r.at[3])
        s_swap.start()
    t_swap.wait()
    o_swap.wait()
    c_swap.start()
    c_copy.start()

    if near:
        gain = jnp.concatenate(
            [sm[core, pl.ds(i * 128 + c1 + N, 16), :].astype(F32)[taps + 3:taps + 4, :own_d] for i in range(dp)], axis=1)
    else:
        gain = R["f_gain"][...].astype(F32)

    def norm(t0):
        r = pl.ds(t0, 64)
        v = toks[r, :].astype(F32)
        inv = lax.rsqrt(jnp.mean(v * v, axis=-1, keepdims=True) + EPS)
        normed[r, :] = (v * inv * gain).astype(BF)

    tiles(total, norm, 64)
    xin[0:8, :] = jnp.zeros((8, half), F32)

    def in_proj(j):
        xin[pl.ds(8, total), pl.ds(j, 256)] = dot(normed[...], cols_of(wi, 0, pl.ds(j, 256)))

    tiles(half, in_proj, 256)
    own = pl.multiple_of(core * half, half)
    row = lax.broadcasted_iota(jnp.int32, (128, 128), 0)
    if near:
        s_swap.wait()
    for b in range(lanes):
        if near:
            one, two = sm[0, pl.ds(own + b * 128, 128), :], sm[1, pl.ds(own + b * 128, 128), :]
        else:
            one, two = R["f_one"][:, lane(b)], R["f_two"][:, lane(b)]
        one, two = one.astype(F32), two.astype(F32)
        par[:, lane(b)] = one
        select[:, lane(b)] = jnp.where(row < c1, one, 0.0).astype(BF)
        delta[:, lane(b)] = jnp.where(row < rank, two, 0.0).astype(BF)
    a2[...] = -jnp.exp(par[c1:c1 + N, :]) * LOG2E

    def conv_tile(t0):
        o = offs[pl.ds(t0, 64), :]
        for b in range(lanes):
            c = lane(b)
            v = xin[pl.ds(t0, 72), c]
            acc = par[r_fb:r_fb + 1, c]
            for j in range(taps):
                s = v[8 - j:72 - j]
                if j:
                    s = jnp.where(o >= float(j), s, 0.0)
                acc = acc + par[r_taps + taps - 1 - j:r_taps + taps - j, c] * s
            conv[pl.ds(t0, 64), c] = acc
            actl[pl.ds(t0, 64), c] = (acc * sigmoid(acc)).astype(BF)

    x_swaps = []
    for p in range(2):
        r = pl.ds(p * rows, rows)
        tiles((p + 1) * rows, conv_tile, 64, p * rows)
        xo[r, :] = dot(actl[r, :], select[...], NT)
        x_swaps.append(links.swap(xo.at[r], xr.at[r], sw_s.at[4 + 9 * p], sw_r.at[4 + 9 * p]))
        x_swaps[p].start()

    def dt_tile(t0):
        low = xo[pl.ds(t0, 64), :].astype(BF)
        for b in range(half // 256):
            pre2 = dot(low, delta[:, lane(b, 256)])
            for q in range(2):
                c = lane(2 * b + q)
                s = softplus(pre2[:, lane(q)] + par[r_db:r_db + 1, c])
                dt[pl.ds(t0, 64), c] = s
                cv = conv[pl.ds(t0, 64), c]
                dx[pl.ds(t0, 64), c] = s * (cv * sigmoid(cv))

    per = 128 // CH

    def cols_tile(i, _):
        t0 = pl.multiple_of(i * 128, 128)
        x = xo[pl.ds(t0, 128), :]
        t = x.T
        for q in range(per):
            btc[i * per + q] = t[rank:rank + N, q * CH:(q + 1) * CH]
            ctc[i * per + q] = t[rank + N:rank + 2 * N, q * CH:(q + 1) * CH]
        m = block_mask(128)
        cblk[pl.ds(t0, 128), :] = jnp.where(m, dot(x.astype(BF), pick(rank + N)), 0.0).astype(BF)
        bblk[pl.ds(t0, 128), :] = jnp.where(m, dot(x.astype(BF), pick(rank)), 0.0).astype(BF)
        return 0

    for p in range(2):
        r = pl.ds(p * rows, rows)
        x_swaps[p].wait()
        xo[r, :] += xr[r, :]
        tiles((p + 1) * rows, dt_tile, 64, p * rows)
        lax.fori_loop(p * rows // 128, (p + 1) * rows // 128, cols_tile, 0)

    steps = g_w[8:15]
    hp = hbuf.shape[1] // N
    hq = hp // CH
    n_blk = total // hp
    st[...] = jnp.zeros_like(st)
    lg = min(512, half)

    def kept(blk):
        return hs.at[pl.ds(pl.multiple_of(blk * hp * N, hp * N), hp * N)]

    def write_out(blk, slot):
        return pltpu.make_async_copy(hbuf.at[slot], kept(blk), hsem.at[slot])

    def f_block(blk, _):
        slot = lax.rem(blk, 2)

        @pl.when(blk >= 2)
        def _():
            write_out(blk - 2, slot).wait()

        def chunk(q):
            c = blk * hq + q
            t0 = pl.multiple_of(c * CH, CH)
            bt = btc[c]
            first = offs[pl.ds(t0, CH), :] == 0.0
            hb = hbuf.at[slot, pl.ds(pl.multiple_of(q * CH * N, CH * N), CH * N), :]
            for g in range(half // lg):
                ls = lane(g, lg)
                a = a2[:, ls]
                h = st[:, ls]
                ds, xs = jnp.where(jnp.concatenate([first] * (lg // 128), axis=1), BIG, dt[pl.ds(t0, CH), ls]), dx[pl.ds(t0, CH), ls]
                for k in range(CH):
                    d = jnp.broadcast_to(ds[k:k + 1], (N, lg))
                    v = jnp.broadcast_to(xs[k:k + 1], (N, lg))
                    w = jnp.broadcast_to(bt[:, k:k + 1], (N, lg))
                    h = jnp.exp2(d * a) * h + w * v
                    hb[k * N:(k + 1) * N, ls] = h.astype(BF)
                st[:, ls] = h
            y[pl.ds(t0, CH), :] = dot(cblk[pl.ds(t0, CH), :], hb[...])

        def several(p, _):
            for k, s in enumerate(steps):
                pl.when(blk * (hq // 2) + p == (6 + 4 * k) // 2)(s)
            for u in range(2):
                chunk(p * 2 + u)
            return 0

        lax.fori_loop(0, hq // 2, several, 0)

        @pl.when(blk < n_blk - 2)
        def _():
            write_out(blk, slot).start()

        return 0

    lax.fori_loop(0, n_blk, f_block, 0)
    c_copy.wait()
    c_swap.wait()

    accs[...] = jnp.zeros_like(accs)

    def gate_cols(j):
        gt[:, pl.ds(j, 256)] = dot(normed[...], cols_of(ww, 0, pl.ds(j, 256)))

        def gate_tile(t0):
            r = pl.ds(t0, 64)
            for q in range(2):
                c = pl.ds(pl.multiple_of(j + q * 128, 128), 128)
                cv = conv[r, c]
                scanned = y[r, c] + par[r_sk:r_sk + 1, c] * (cv * sigmoid(cv))
                y[r, c] = scanned
                g = gt[r, c]
                gated[r, c] = (scanned * (g * sigmoid(g))).astype(BF)

        tiles(total, gate_tile, 64)

    g_w[15]()
    tiles(half, gate_cols, 256)

    def outer(left, right, out):
        def body(i):
            for b in range(half // 512):
                out[pl.ds(i, 256), lane(b, 512)] = dot(left[:, pl.ds(i, 256)], right[:, lane(b, 512)], TN).astype(BF)
        tiles(width, body, 256)

    s_o = scatter_steps(links, d_out, R["red_o"], R["so_b"], R["so_s"], R["so_r"])
    s_g = scatter_steps(links, d_gate, R["red_g"], R["sg_b"], R["sg_s"], R["sg_r"])
    outer(cots, gated, d_out)
    s_o[0]()

    def grad_cols(j):
        qtmp[...] = dot(cots[...], cols_of(ww, own_d, pl.ds(j, 256)))

        def grad_tile(t0):
            r = pl.ds(t0, 64)
            for q in range(2):
                c = pl.ds(pl.multiple_of(j + q * 128, 128), 128)
                cv = conv[r, c]
                g = gt[r, c]
                sg = sigmoid(g)
                gg = qtmp[r, lane(q)]
                ggr[r, c] = (gg * y[r, c] * slope(g, sg)).astype(BF)
                G = gg * (g * sg)
                y[r, c] = G
                accs[0, :, c] += eighths(G * (cv * sigmoid(cv)))

        tiles(total, grad_tile, 64)

    tiles(half, grad_cols, 256)
    outer(normed, ggr, d_gate)
    s_g[0]()

    steps_b = s_o[1:9] + s_g[1:3] + [s_o[9]] + [s_g[3], s_g[4], s_g[5], s_g[6], s_g[7], s_g[8], s_g[9]]
    n_chunks = total // CH
    st[...] = jnp.zeros_like(st)
    racc[...] = jnp.zeros_like(racc)

    def read_back(blk, slot):
        return pltpu.make_async_copy(kept(blk), hbuf.at[slot], hsem.at[slot])

    def b_block(i, _):
        blk = n_blk - 1 - i
        slot = lax.rem(blk, 2)

        def chunk(q):
            c = blk * hq + q
            t0 = pl.multiple_of(c * CH, CH)
            before = jnp.where(q == 0, 1 - slot, slot)
            last = pl.multiple_of(jnp.where(q == 0, hp - 1, q * CH - 1) * N, N)
            ct = ctc[c]
            first = offs[pl.ds(t0, CH), :] == 0.0
            hb = hbuf.at[slot, pl.ds(pl.multiple_of(q * CH * N, CH * N), CH * N), :]
            hl = hbuf.at[before, pl.ds(last, N), :]
            for g in range(half // lg):
                ls = lane(g, lg)
                a = a2[:, ls]
                carry = st[:, ls]
                ra = racc[:, ls]
                ds, gs = jnp.where(jnp.concatenate([first] * (lg // 128), axis=1), BIG, dt[pl.ds(t0, CH), ls]), y[pl.ds(t0, CH), ls]
                for k in range(CH - 1, -1, -1):
                    d = jnp.broadcast_to(ds[k:k + 1], (N, lg))
                    gg = jnp.broadcast_to(gs[k:k + 1], (N, lg))
                    cc = jnp.broadcast_to(ct[:, k:k + 1], (N, lg))
                    h = hb[(k - 1) * N:k * N, ls] if k else hl[:, ls]
                    sg = cc * gg + carry
                    carry = jnp.exp2(d * a) * sg
                    term = carry * h.astype(F32)
                    ra = ra + term * d
                    sgs[k * N:(k + 1) * N, ls] = sg.astype(BF)
                    part = term * a
                    part = part[:N // 2] + part[N // 2:]
                    if k % 2:
                        odd = part
                    else:
                        das[k * N // 2:(k + 2) * N // 2, ls] = jnp.concatenate([part, odd], axis=0).astype(BF)
                st[:, ls] = carry
                racc[:, ls] = ra
            m = block_mask()
            m8 = jnp.where(lax.broadcasted_iota(jnp.int32, (CH, CH * N // 2), 1) // (N // 2)
                           == lax.broadcasted_iota(jnp.int32, (CH, CH * N // 2), 0), 1.0, 0.0).astype(BF)
            r = pl.ds(t0, CH)
            sgc = sgs[...]
            wout = dot(dx[r, :].astype(BF), sgc, NT)
            wgs[pl.ds(c, 1), :] = jnp.sum(jnp.where(m, wout, 0.0), axis=0, keepdims=True)
            rout = dot(y[r, :].astype(BF), hb[...], NT)
            rgs[pl.ds(c, 1), :] = jnp.sum(jnp.where(m, rout, 0.0), axis=0, keepdims=True)
            dx[r, :] = dot(bblk[r, :], sgc)
            gt[r, :] = dot(m8, das[...])

        def several(p, _):
            done = i * (hq ) + p
            for k, s in enumerate(steps_b):
                pl.when(done == 6 + (9 * k) // 4)(s)

            @pl.when((p == hq  - 1) & (blk >= 1) & (blk <= n_blk - 2))
            def _():
                read_back(blk - 1, 1 - slot).wait()

            for u in range(1):
                chunk(hq - 1 - (p  + u))
            return 0

        lax.fori_loop(0, hq , several, 0)

        @pl.when(blk >= 2)
        def _():
            read_back(blk - 2, slot).start()

        return 0

    lax.fori_loop(0, n_blk, b_block, 0)
    dg, low_b = dx, d_gate

    fins = [links.swap(R[k], R[k + "2"], sw_s.at[10 + n], sw_r.at[10 + n])
            for n, k in enumerate(("red_i", "red_g", "red_o"))]

    ln2 = math.log(2.0)

    def pre_tile(t0):
        r = pl.ds(t0, 64)
        for b in range(lanes):
            c = lane(b)
            cv = conv[r, c]
            act = cv * sigmoid(cv)
            v = (dg[r, c] * act + gt[r, c] * ln2) * (1.0 - jnp.exp(-dt[r, c]))
            low_b[r, c] = v.astype(BF)
            accs[1, :, c] += eighths(v)

    xg = qtmp.at[:, 0:128]

    def xg_tile(i, _):
        t0 = pl.multiple_of(i * 128, 128)
        r = pl.ds(t0, 128)
        m = block_mask(128)
        sums = dot(low_b[r, :], delta[...], NT)
        for ref, first in ((wgs, rank), (rgs, rank + N)):
            v = ref[pl.ds(pl.multiple_of(i * per, per), per), :]
            v = jnp.broadcast_to(v[:, None, :], (per, CH, CH * N)).reshape(128, CH * N)
            v = jnp.where(m, v, 0.0)
            hi = v.astype(BF)
            lo = (v - hi.astype(F32)).astype(BF)
            p = place(first)
            sums = sums + dot(hi, p) + dot(lo, p)
        xg[r, :] = sums
        return 0

    g_swaps = []
    for p in range(2):
        r = pl.ds(p * rows, rows)
        tiles((p + 1) * rows, pre_tile, 64, p * rows)
        lax.fori_loop(p * rows // 128, (p + 1) * rows // 128, xg_tile, 0)
        g_swaps.append(links.swap(xg.at[r], R["xr2"].at[r], sw_s.at[6 + 8 * p], sw_r.at[6 + 8 * p]))
        g_swaps[p].start()
    sgrad = R["sgrad"]
    xob = xo[...].astype(BF)
    for b in range(half // 256):
        sgrad[1, :, lane(b, 256)] = dot(xob, low_b[0:total, lane(b, 256)], TN)
    def project(which, out):
        def body(i, _):
            out(pl.multiple_of(i * 256, 256), dot(gated[which, :], rows_of(ww, own_d, i), NT))
            return 0
        lax.fori_loop(0, width // 256, body, 0)

    msent, mcame = hbuf.at[0, pl.ds(0, rows), :], hbuf.at[1, pl.ds(0, rows), :]

    def put_mixed(j, v):
        msent[:, pl.ds(j, 256)] = v.astype(BF)

    project(other, put_mixed)
    for p in range(2):
        g_swaps[p].wait()
    xg[...] = xg[...] + R["xr2"][...]
    m_swap = links.swap(msent, mcame, sw_s.at[5], sw_r.at[5])
    m_swap.start()
    fins[1].start()
    fins[2].start()
    xgb = xg[...].astype(BF)
    for b in range(half // 256):
        sgrad[0, :, lane(b, 256)] = dot(xgb, actl[:, lane(b, 256)], TN)

    quarter = half // 2
    ig = d_gate
    d_in = d_out
    y[pl.ds(total, 8), :] = jnp.zeros((8, half), F32)

    def conv_back(h):
        def cg_tile(t0):
            r = pl.ds(t0, 64)
            low = xg[r, :].astype(BF)
            for b in range(h * quarter // 256, (h + 1) * quarter // 256):
                back = dot(low, select[:, lane(b, 256)])
                for q in range(2):
                    c = lane(2 * b + q)
                    ag = y[r, c] * par[r_sk:r_sk + 1, c] + dg[r, c] * dt[r, c] + back[:, lane(q)]
                    cv = conv[r, c]
                    v = ag * slope(cv, sigmoid(cv))
                    y[r, c] = v
                    accs[2, :, c] += eighths(v)

        tiles(total, cg_tile, 64)

        def ig_tile(t0):
            o = offs[pl.ds(t0, 72), :]
            for b in range(h * quarter // 128, (h + 1) * quarter // 128):
                c = lane(b)
                v = y[pl.ds(t0, 72), c]
                x = xin[pl.ds(t0, 72), c]
                acc = jnp.zeros((64, 128), F32)
                for j in range(taps):
                    mv = jnp.where(o >= float(j), v, 0.0) if j else v
                    accs[3 + taps - 1 - j, :, c] += eighths(mv[0:64] * x[8 - j:72 - j])
                    acc = acc + mv[j:64 + j] * par[r_taps + taps - 1 - j:r_taps + taps - j, c]
                ig[pl.ds(t0, 64), c] = acc.astype(BF)

        tiles(total, ig_tile, 64)

        def outer_tile(i, _):
            v = dot(normed[:, pl.ds(pl.multiple_of(i * 256, 256), 256)], ig[0:total, lane(h, quarter)], TN).astype(BF)
            d_in[pl.ds(pl.multiple_of(i * 256, 256), 256), lane(h, quarter)] = v
            return 0

        lax.fori_loop(0, width // 256, outer_tile, 0)

    def half_scatter(h):
        def part(ref):
            return ref.at[(slice(None),) * (len(ref.shape) - 1) + (lane(h, quarter),)]
        bufs = [part(b) for b in R["so_b"]] if near else [R[("so_b", "sg_b")[h]][0].at[:, :, lane(h, quarter)], None, None]
        return scatter_steps(links, part(d_in), part(R["red_i"]), bufs, R["si_s" if h == 0 else "sj_s"], R["si_r" if h == 0 else "sj_r"])

    s_i, s_j = half_scatter(0), half_scatter(1)
    conv_back(0)
    s_i[0]()
    conv_back(1)
    s_j[0]()
    s_i[1]()
    s_i[2]()
    s_i[3]()
    s_i[4]()

    def back_project(which, out):
        def body(i, _):
            out(pl.multiple_of(i * 256, 256),
                dot(ig[which, :], rows_of(wi, 0, i), NT) + dot(ggr[which, :], rows_of(ww, 0, i), NT))
            return 0
        lax.fori_loop(0, width // 256, body, 0)

    def put_send(j, v):
        msend[:, pl.ds(j, 256)] = v.astype(BF)

    back_project(other, put_send)
    n_swap = links.swap(msend, mrecv, sw_s.at[7], sw_r.at[7])
    n_swap.start()
    s_i[5]()
    s_i[6]()
    s_j[1]()
    s_j[2]()
    ng = R["mixed_f"]

    def put_ng(j, v):
        ng[:, pl.ds(j, 256)] = v

    back_project(mine, put_ng)

    vecs = jnp.concatenate(
        [racc[...] * a2[...] * ln2]
        + [jnp.sum(accs[3 + k], axis=0, keepdims=True) for k in range(taps)]
        + [jnp.sum(accs[2], axis=0, keepdims=True), jnp.sum(accs[1], axis=0, keepdims=True),
           jnp.sum(accs[0], axis=0, keepdims=True), jnp.zeros((16 - taps - 3, half), F32)], axis=0)
    sgrad[0, c1:128, :] = vecs
    sgrad[1, rank:128, :] = jnp.zeros((128 - rank, half), F32)
    if near:
        small, away = R["small"], R["away"]
        for b in range(lanes):
            small[pl.ds(own + b * 128, 128), :] = sgrad[core, :, lane(b)].astype(BF)
            away[lane(b), :] = sgrad[1 - core, :, lane(b)].astype(BF)
        a_swap = links.swap(away, small.at[pl.ds(own, half), :], sw_s.at[8], sw_r.at[8])
        a_swap.start()
        red_s = R["o_small"]
        s_s = scatter_steps(links, small, red_s.at[core], R["ss_b"], R["ss_s"], R["ss_r"])
    else:
        s_s = [lambda: None] * 10
    s_i[7]()
    s_i[8]()
    s_j[3]()
    s_j[4]()
    if near:
        a_swap.wait()
    s_s[0]()
    n_swap.wait()
    def tok_tile(t0):
        r = pl.ds(t0, 32)
        v = tok[r, :].astype(F32)
        inv = lax.rsqrt(jnp.mean(v * v, axis=-1, keepdims=True) + EPS)
        sc = v * inv
        n = ng[r, :] + mrecv[r, :].astype(F32)
        sg = n * gain
        ng[r, :] = cots[pl.ds(pl.multiple_of(core * rows + t0, 32), 32), :].astype(F32) + inv * (
            sg - sc * jnp.mean(sg * sc, axis=-1, keepdims=True))

    tiles(rows, tok_tile, 32)
    t_copy = pltpu.make_async_copy(ng, R["tgrad"], lsem.at[1])
    t_copy.start()
    s_j[5]()
    s_i[9]()
    m_swap.wait()
    def put_own(j, v):
        R["mixed"][:, pl.ds(j, 256)] = (
            tok[:, pl.ds(j, 256)].astype(F32) + v + mcame[:, pl.ds(j, 256)].astype(F32)).astype(BF)

    project(mine, put_own)
    s_s[1]()
    s_s[2]()
    s_j[6]()
    if not near:
        R["f_grad"][...] = sgrad[...]
    s_j[7]()
    for k in range(3, 7):
        s_s[k]()
    s_j[8]()
    for k in range(7, 10):
        s_s[k]()
    if near:
        fs = links.swap(red_s.at[core], red_s.at[core], sw_s.at[9], sw_r.at[9])
        fs.start()
    s_j[9]()
    t_copy.wait()

    fins[0].start()

    def share(first, k, out):
        R[out][:, pl.ds(pl.multiple_of(first + core * half, 128), half)] = R[k][...]
        R[out][:, pl.ds(pl.multiple_of(first + (1 - core) * half, 128), half)] = R[k + "2"][...]

    fins[1].wait()
    share(inner, "red_g", "o_in")
    fins[2].wait()
    share(0, "red_o", "o_out")
    if near:
        fs.wait()
    fins[0].wait()
    share(0, "red_i", "o_in")


def layer(inputs, dp, dims):
    rows, width = inputs["tok"].shape
    half = inputs["w_o"].shape[1] // 2
    inner = 2 * half
    total = 2 * rows
    taps, rank = dims
    own_d, own_e = width // dp, inner // dp
    n = copies_of(dp)
    near = bool(plane(dp))
    extra = 16 if near else 0
    sd = jax.ShapeDtypeStruct
    vm = pl.BlockSpec(memory_space=pltpu.VMEM)
    hbm = pl.BlockSpec(memory_space=pl.ANY)
    dma = pltpu.SemaphoreType.DMA
    V = pltpu.VMEM
    outs = {
        "mixed": sd((rows, width), BF), "tgrad": sd((rows, width), F32),
        "o_in": sd((own_d, 2 * inner), F32), "o_out": sd((own_d, inner), F32), "hs": sd((total * N, half), BF),
    }
    if near:
        outs["o_small"] = sd((2, 128, own_e), F32)
    else:
        outs["f_grad"] = sd((2, 128, half), F32)
    f2 = V((total, half), F32)
    scratch = {
        "part_i": V((own_d + extra, half), BF), "part_w": V((2 * own_d, half), BF),
        "wi": V((dp * (own_d + extra), half), BF), "ww": V((2 * width, half), BF), "select": V((128, half), BF), "delta": V((128, half), BF),
        "toks": V((total, width), BF), "cots": V((total, width), BF), "normed": V((total, width), BF),
        "offs": V((total + 8, 128), F32), "xin": V((total + 8, half), F32), "conv": f2, "actl": V((total, half), BF),
        "dt": f2, "gt": f2, "dx": f2, "y": V((total + 8, half), F32), "ggr": V((total, half), BF),
        "xo": V((total, 128), F32), "xr": V((total, 128), F32), "xr2": V((total, 128), F32),
        "hbuf": V((2, 64 * N, half), BF), "par": V((128, half), F32),
        "btc": V((total // CH, N, CH), F32), "ctc": V((total // CH, N, CH), F32),
        "cblk": V((total, CH * N), BF), "bblk": V((total, CH * N), BF),
        "a2": V((N, half), F32), "st": V((N, half), F32), "racc": V((N, half), F32),
        "qtmp": V((total, 256), F32),
        "sgs": V((CH * N, half), BF), "das": V((CH * N // 2, half), BF),
        "wgs": V((total // CH, CH * N), F32), "rgs": V((total // CH, CH * N), F32),
        "accs": V((3 + taps, 8, half), F32), "d_out": V((width, half), BF), "d_gate": V((width, half), BF),
        "msend": V((rows, width), BF), "mrecv": V((rows, width), BF), "mixed_f": V((rows, width), F32),
        "sgrad": V((2, 128, half), F32),
        "so_b": scatter_scratch(dp, own_d, half), "sg_b": scatter_scratch(dp, own_d, half),
        "sw_s": dma((15,)), "sw_r": dma((15,)), "hsem": dma((2,)), "lsem": dma((2,)),
    }
    for k in ("i", "g", "o"):
        scratch["red_" + k] = V((own_d, half), F32)
        scratch["red_" + k + "2"] = V((own_d, half), F32)
    if near:
        scratch["sm"] = V((2, inner, own_e), BF)
        scratch["small"], scratch["away"] = V((inner, own_e), BF), V((half, own_e), BF)
        scratch["ss_b"] = scatter_scratch(dp, 128, own_e)
    for k in ("gi", "gw", "si", "sj", "sg", "so", "ss"):
        scratch[k + "_s"] = dma((n,))
        scratch[k + "_r"] = dma((n,))
    names = list(inputs) + list(outs) + list(scratch)
    res = pl.pallas_call(
        functools.partial(layer_kernel, dp=dp, dims=dims, names=names),
        out_shape=list(outs.values()),
        in_specs=[pl.BlockSpec(memory_space=pltpu.SMEM) if k == "lens" else hbm if k == "cot" else vm for k in inputs],
        out_specs=[hbm if k in ("tgrad", "hs") else vm for k in outs],
        scratch_shapes=list(scratch.values()),
        compiler_params=pltpu.CompilerParams(collective_id=0, has_side_effects=True, vmem_limit_bytes=127 << 19),
        name="layer",
    )(*inputs.values())
    return dict(zip(outs, res))


def local(
    tokens,
    doc_lengths,
    cotangent,
    norm_gain,
    input_weight,
    filter_weight,
    filter_bias,
    select_weight,
    delta_weight,
    delta_bias,
    decay_log,
    skip_gain,
    output_weight,
    *,
    dp,
):
    rows, length, width = tokens.shape
    rank = delta_weight.shape[1]
    taps = filter_weight.shape[1]
    own_e = filter_weight.shape[0]
    own_d = norm_gain.shape[0]
    inner = own_e * dp
    c1 = rank + 2 * N
    inputs = {
        "lens": doc_lengths, "tok": tokens.reshape(rows * length, width), "cot": cotangent.reshape(rows * length, width),
        "w_in": input_weight, "w_o": output_weight,
    }
    if plane(dp):
        inputs.update(
            s_select=select_weight.T, s_decay=decay_log.T, s_delta=delta_weight.T, s_filter=filter_weight.T,
            s_fb=filter_bias[None], s_db=delta_bias[None], s_skip=skip_gain[None], s_gain=norm_gain[None],
        )
    else:
        core = lax.axis_index("rep")
        vectors = jnp.stack([filter_bias, delta_bias, skip_gain])
        tail = jnp.concatenate([filter_weight.T, vectors, jnp.zeros((16 - taps - 3, own_e), BF)], axis=0)
        one = jnp.concatenate([select_weight.T, decay_log.T, tail], axis=0)
        two = jnp.concatenate([delta_weight.T, jnp.zeros((128 - rank, own_e), BF)], axis=0)
        both = lax.all_gather(jnp.stack([one, two]), "dp", axis=2, tiled=True)
        both = lax.dynamic_slice(both, (0, 0, core * (inner // 2)), (2, 128, inner // 2))
        inputs.update(f_one=both[0], f_two=both[1], f_gain=lax.all_gather(norm_gain, "dp", axis=0, tiled=True)[None])
    r = layer(inputs, dp, (taps, rank))
    if plane(dp):
        small = r["o_small"]
    else:
        small = lax.all_gather(r["f_grad"], "rep", axis=2, tiled=True)
        small = lax.psum_scatter(small, "dp", scatter_dimension=2, tiled=True)
    o = finish(r["mixed"], r["tgrad"], r["o_in"], r["o_out"], small, input_weight, norm_gain[None], (taps, rank))
    return (
        o[0].reshape(rows, length, width),
        o[1].reshape(rows, length, width),
        o[4].reshape(own_d),
        o[2],
        o[5].T,
        o[6].reshape(own_e),
        o[7].T,
        o[8].T,
        o[9].reshape(own_e),
        o[10].T,
        o[11].reshape(own_e),
        o[3],
    )


def finish(mixed, tgrad, o_in, o_out, small, w_in, gain, dims):
    taps, rank = dims
    c1 = rank + 2 * N
    own_e, own_d = small.shape[2], w_in.shape[0]
    sd = jax.ShapeDtypeStruct
    big = [mixed, tgrad, o_in, o_out]
    parts = 2

    def kernel(*refs):
        ins, small_ref, w_ref, gain_ref, outs, acc = refs[:4], refs[4], refs[5], refs[6], refs[7:19], refs[19]
        for i, o in zip(ins, outs[:4]):
            o[...] = i[...]
        p = w_ref[...].astype(F32) * ins[2][...]
        total = p[:, 0:128]
        for b in range(1, p.shape[1] // 128):
            total = total + p[:, b * 128:(b + 1) * 128]
        g = c1 + N + taps + 3

        @pl.when(pl.program_id(0) == 0)
        def _():
            acc[...] = jnp.zeros_like(acc)
            outs[5][...] = small_ref[0, c1 + N:c1 + N + taps, :]
            outs[6][...] = small_ref[0, g - 3:g - 2, :]
            outs[7][...] = small_ref[0, 0:c1, :]
            outs[8][...] = small_ref[1, 0:rank, :]
            outs[9][...] = small_ref[0, g - 2:g - 1, :]
            outs[10][...] = small_ref[0, c1:c1 + N, :]
            outs[11][...] = small_ref[0, g - 1:g, :]

        acc[0:own_d, :] += total

        @pl.when(pl.program_id(0) == parts - 1)
        def _():
            row = jnp.sum(acc[...].T, axis=0, keepdims=True)[:, :own_d]
            outs[4][...] = row / gain_ref[...].astype(F32)

    shapes = [sd(b.shape, b.dtype) for b in big] + [
        sd(s, F32) for s in ((1, own_d), (taps, own_e), (1, own_e), (c1, own_e), (rank, own_e), (1, own_e), (N, own_e), (1, own_e))]
    specs = [pl.BlockSpec((b.shape[0], b.shape[1] // parts), lambda i: (0, i)) for b in big]

    def whole(s):
        return pl.BlockSpec(s.shape, lambda i, n=len(s.shape): (0,) * n)

    wide = pl.BlockSpec((own_d, w_in.shape[1] // parts), lambda i: (0, i))
    return pl.pallas_call(
        kernel, grid=(parts,), out_shape=shapes, in_specs=specs + [whole(small), wide, whole(gain)],
        out_specs=specs + [whole(s) for s in shapes[4:]], scratch_shapes=[pltpu.VMEM((128, 128), F32)], name="finish",
    )(*big, small, w_in, gain)


def solution(mesh):
    dp_rep = ("dp", "rep")
    one = P("dp")
    two = P("dp", None)
    three = P(dp_rep, None, None)
    return jax.shard_map(
        functools.partial(local, dp=mesh.shape["dp"]),
        mesh=mesh,
        in_specs=(three, P(dp_rep, None), three, one, two, two, one, two, two, one, two, one, two),
        out_specs=(three, three, one, two, two, one, two, two, one, two, one, two),
        check_vma=False,
    )
```
